256 devices in a mesh: ab: 16 (over z_lo, y, core), cd: 16 (over z_hi, x).
Axes of the slice: x: 4, y: 4, z: 8 (z_hi: 4, z_lo: 2; z = z_hi * 2 + z_lo), core: 2. Of those that a mesh axis runs over, the one named last changes fastest.
Arguments:
- pair_values: bfloat16 [32768, 32768], P('ab', 'cd'), may hold values from -0.046875 to 0.046875
- amplitudes: bfloat16 [64, 800, 800], P('ab', 'cd'), may hold values from -6 to 6
- cd_first: int32 [32768], P('cd'), may hold values from 0 to 799, as said below
- cd_second: int32 [32768], P('cd'), may hold values from 0 to 799, as said below
- live_cols: int32 [16], P('cd'), may hold values from 512 to 2048, as said below
Outputs:
- ladder: bfloat16 [64, 32768], P(None, ('ab', 'cd'))
The draws below stay inside these ranges and needn't reach their ends.
Inputs may be any that keep to these rules, and one draw needn't show every extreme that they name: `cd_first`: slot n lies in slab s = n // 2048 and its c lies in orbitals s * 50 to (s + 1) * 50 - 1. cd_second[n] >= cd_first[n] for every slot. `live_cols`: slots 0 and 1 of every slab are live.
All inputs are finite; a program needn't handle non-finite values.
Results may differ from the reference program's by a relative error of at most 0.0051.
Values may be sent and summed in bfloat16 or wider, within the bound.
A program may use at most 64 MiB of HBM per device.

```python
import jax
import jax.numpy as jnp
from jax import lax

NV = 800
PAIRS = 64
AB_DEV = 2048
COLS = 2048
CB = 50
NAB = 32768
NCOL = 32768
SLABS = 16


def pair_lists(key):
    base = jax.random.fold_in(key, 11)
    key_one, key_two, key_three = jax.random.split(base, 3)
    index = jnp.arange(NCOL, dtype=jnp.int32)
    slot = index % COLS
    owner = index // COLS
    local = jax.random.randint(key_one, (NCOL,), 0, CB, dtype=jnp.int32)
    local = jnp.where(slot == 0, 0, jnp.where(slot == 1, CB - 1, local))
    first = owner * CB + local
    offset = jax.random.randint(key_two, (NCOL,), 0, NV - first, dtype=jnp.int32)
    diagonal = jax.random.randint(key_three, (NCOL,), 0, 8, dtype=jnp.int32) == 0
    second = jnp.where(diagonal, first, first + offset)
    second = jnp.where(slot == 0, first, jnp.where(slot == 1, NV - 1, second))
    return (first.astype(jnp.int32), second.astype(jnp.int32))


def draw_cd_first(key, part):
    return pair_lists(key)[0]


def draw_cd_second(key, part):
    return pair_lists(key)[1]


def draw_live_cols(key, part):
    base = jax.random.fold_in(key, 23)
    key_one, key_two, key_three = jax.random.split(base, 3)
    counts = jax.random.randint(key_one, (SLABS,), COLS // 4, COLS + 1, dtype=jnp.int32)
    fullest = jax.random.randint(key_two, (), 0, SLABS, dtype=jnp.int32)
    lightest = (fullest + 1 + jax.random.randint(key_three, (), 0, SLABS - 1, dtype=jnp.int32)) % SLABS
    index = jnp.arange(SLABS, dtype=jnp.int32)
    counts = jnp.where(index == fullest, COLS, counts)
    counts = jnp.where(index == lightest, COLS // 4, counts)
    return counts.astype(jnp.int32)


def raised(values, rng, source, target, blocks, factor):
    def block_of(axis_at):
        return (jnp.arange(values.shape[axis_at]) // (values.shape[axis_at] // blocks)).reshape((-1,) + (1,) * (values.ndim - 1 - axis_at))

    near = jax.random.permutation(rng, blocks)[block_of(target)]
    second = (block_of(target) + blocks // 2) % blocks
    return jnp.where((block_of(source) == near) | (block_of(source) == second), factor * values, values)


def block_scale(stream_key, shape, pieces, low, top_value):
    def one(axis_at, parts):
        heights = jax.random.uniform(jax.random.fold_in(jax.random.fold_in(stream_key, 6), axis_at), (parts,), jnp.float32, low / len(pieces), top_value / len(pieces))
        return jnp.repeat(jnp.exp(heights), shape[axis_at] // parts).reshape((-1,) + (1,) * (len(shape) - axis_at - 1))

    level = one(*pieces[0])
    for cut in pieces[1:]:
        level = level * one(*cut)
    return level


def normal_values(rng, extent, deviation, bound, pieces=(), held_as=jnp.bfloat16):
    values = jax.random.normal(rng, extent, jnp.float32) * deviation
    if len(pieces) > 0:
        values = block_scale(rng, extent, pieces, -0.22, 0.18) * values
    return jnp.clip(values, min=-bound, max=bound).astype(held_as)


def noise_with(stream_key, shape, scale, bound, shards, heavy, kind=jnp.bfloat16):
    drawn = scale * jax.random.normal(stream_key, shape, jnp.float32)
    if shards:
        drawn = drawn * block_scale(stream_key, shape, shards, -0.22, 0.18)
    return jnp.clip(raised(drawn, jax.random.fold_in(stream_key, 3), *heavy), -bound, bound).astype(kind)


def setup_inputs(seed: int = 0) -> dict:
    key_of = jax.random.split(jax.random.key(seed), 6)
    return {
        "pair_values": noise_with(key_of[0], (NAB, NCOL), NCOL ** -0.5, 0.046875, ((0, 16), (1, 16)), (1, 0, 16, 2.0)),
        "amplitudes": normal_values(key_of[1], (PAIRS, NV, NV), 1.0, 6.0, ((0, 16), (1, 16))),
        "cd_first": draw_cd_first(jax.random.fold_in(key_of[5], 71), 0),
        "cd_second": draw_cd_second(jax.random.fold_in(key_of[5], 71), 0),
        "live_cols": draw_live_cols(jax.random.fold_in(key_of[5], 71), 0),
    }


def reference(pair_values, amplitudes, cd_first, cd_second, live_cols):
    ncol = cd_first.shape[0]
    direct = amplitudes[:, cd_first, cd_second].astype(jnp.float32)
    crossed = amplitudes[:, cd_second, cd_first].astype(jnp.float32)
    slot = jnp.arange(ncol, dtype=jnp.int32) % COLS
    owner = jnp.arange(ncol, dtype=jnp.int32) // COLS
    live = (slot < live_cols[owner]).astype(jnp.float32)
    half = jnp.where(cd_first == cd_second, jnp.float32(0.5), jnp.float32(1.0)).astype(jnp.float32)
    weight = half * live
    packed = ((direct + crossed) * weight[None, :]).astype(jnp.bfloat16)
    blocks = pair_values.reshape(NAB // AB_DEV, AB_DEV, ncol)

    def one_block(values_block):
        return lax.dot_general(packed, values_block, (((1,), (1,)), ((), ())), preferred_element_type=jnp.float32)

    result = lax.map(one_block, blocks)
    return jnp.transpose(result, (1, 0, 2)).reshape(PAIRS, NAB).astype(jnp.bfloat16)
```

```python
import jax
import jax.numpy as jnp
from jax import lax
from jax.sharding import PartitionSpec as P


def on_device(pair_values, amplitudes, cd_first, cd_second, live_cols):
    slab = lax.axis_index("cd")
    pair_block = amplitudes.shape[0]
    orbit_block = amplitudes.shape[1]
    orbitals = amplitudes.shape[2]
    columns = cd_first.shape[0]
    local_first = cd_first - slab * orbit_block
    mirrored = lax.all_to_all(amplitudes, "cd", 2, 1, tiled=True)
    pick_d = (lax.broadcasted_iota(jnp.int32, (orbitals, columns), 0) == cd_second[None, :]).astype(
        amplitudes.dtype
    )
    direct_rows = lax.dot_general(
        amplitudes, pick_d, (((2,), (0,)), ((), ())), preferred_element_type=jnp.float32
    )
    crossed_rows = lax.dot_general(
        mirrored, pick_d, (((1,), (0,)), ((), ())), preferred_element_type=jnp.float32
    )
    pick_c = lax.broadcasted_iota(jnp.int32, (orbit_block, columns), 0) == local_first[None, :]
    both = jnp.sum(jnp.where(pick_c[None], direct_rows + crossed_rows, 0.0), axis=1)
    live_count = live_cols[0]
    slots = jnp.arange(columns, dtype=jnp.int32)
    live = (slots < live_count).astype(jnp.float32)
    half = jnp.where(cd_first == cd_second, jnp.float32(0.5), jnp.float32(1.0))
    weight = half * live
    packed = (both * weight[None, :]).astype(jnp.bfloat16)
    contract = (((1,), (1,)), ((), ()))
    partial_sums = lax.dot_general(
        lax.all_gather(packed, "ab", axis=0, tiled=True),
        pair_values,
        contract,
        preferred_element_type=jnp.float32,
    )
    return lax.psum_scatter(partial_sums, "cd", scatter_dimension=1, tiled=True).astype(
        jnp.bfloat16
    )


def solution(mesh):
    placed = (P("ab", "cd"), P("ab", "cd", None), P("cd"), P("cd"), P("cd"))
    return jax.shard_map(
        on_device, mesh=mesh, in_specs=placed, out_specs=P(None, ("ab", "cd")), check_vma=False
    )
```

```python
import functools

import jax
import jax.numpy as jnp
from jax import lax
from jax.experimental import pallas as pl
from jax.experimental.pallas import tpu as pltpu
from jax.sharding import PartitionSpec as P

MESH = pl.DeviceIdType.MESH


def ladder_kernel(
    n_ab, n_cd, packed_ref, values_hbm, out_ref,
    slots, gathered, values_buf, sums_out, sums_in,
    values_sem, pk_send, pk_recv, sum_send, sum_recv, own_sem,
):
    me_ab = lax.axis_index("ab")
    me_cd = lax.axis_index("cd")
    rows = packed_ref.shape[0]
    block = values_buf.shape[1]

    for step in range(n_cd):
        dest = lax.rem(me_cd + 1 + step, n_cd)
        pltpu.make_async_copy(
            values_hbm.at[pl.ds(pl.multiple_of(dest * block, block), block), :],
            values_buf.at[step],
            values_sem.at[step],
        ).start()

    barrier = pltpu.get_barrier_semaphore()
    for k in range(1, n_ab):
        peer = lax.rem(me_ab + k, n_ab)
        pl.semaphore_signal(barrier, inc=1, device_id=(peer, me_cd), device_id_type=MESH)
    for k in range(1, n_cd):
        peer = lax.rem(me_cd + k, n_cd)
        pl.semaphore_signal(barrier, inc=1, device_id=(me_ab, peer), device_id_type=MESH)
    pl.semaphore_wait(barrier, (n_ab - 1) + (n_cd - 1))

    own = pltpu.make_async_copy(packed_ref, slots.at[me_ab], own_sem.at[0])
    own.start()
    for k in range(1, n_ab):
        peer = lax.rem(me_ab + k, n_ab)
        pltpu.make_async_remote_copy(
            src_ref=packed_ref,
            dst_ref=slots.at[me_ab],
            send_sem=pk_send.at[k],
            recv_sem=pk_recv.at[me_ab],
            device_id=(peer, me_cd),
            device_id_type=MESH,
        ).start()
    own.wait()
    for k in range(1, n_ab):
        src = lax.rem(me_ab + n_ab - k, n_ab)
        pltpu.make_async_remote_copy(
            src_ref=packed_ref,
            dst_ref=slots.at[src],
            send_sem=pk_send.at[k],
            recv_sem=pk_recv.at[src],
            device_id=(src, me_cd),
            device_id_type=MESH,
        ).wait_recv()
    for k in range(n_ab):
        gathered[k * rows:(k + 1) * rows, :] = slots[k].astype(jnp.float32)
    lhs = gathered[...].astype(jnp.bfloat16)

    def one_block(step):
        pltpu.make_async_copy(
            values_hbm.at[pl.ds(0, block), :], values_buf.at[step], values_sem.at[step]
        ).wait()
        return lax.dot_general(
            lhs, values_buf[step], (((1,), (1,)), ((), ())), preferred_element_type=jnp.float32
        )

    for step in range(n_cd - 1):
        dest = lax.rem(me_cd + 1 + step, n_cd)
        sums_out[step] = one_block(step)
        pltpu.make_async_remote_copy(
            src_ref=sums_out.at[step],
            dst_ref=sums_in.at[me_cd],
            send_sem=sum_send.at[step],
            recv_sem=sum_recv.at[me_cd],
            device_id=(me_ab, dest),
            device_id_type=MESH,
        ).start()
    total = one_block(n_cd - 1)
    for step in range(n_cd - 1):
        src = lax.rem(me_cd + n_cd - 1 - step, n_cd)
        pltpu.make_async_remote_copy(
            src_ref=sums_out.at[step],
            dst_ref=sums_in.at[src],
            send_sem=sum_send.at[step],
            recv_sem=sum_recv.at[src],
            device_id=(me_ab, src),
            device_id_type=MESH,
        ).wait_recv()
        total = total + sums_in[src]
    out_ref[...] = total.astype(out_ref.dtype)

    for k in range(1, n_ab):
        pltpu.make_async_remote_copy(
            src_ref=packed_ref,
            dst_ref=slots.at[me_ab],
            send_sem=pk_send.at[k],
            recv_sem=pk_recv.at[me_ab],
            device_id=(me_ab, me_cd),
            device_id_type=MESH,
        ).wait_send()
    for step in range(n_cd - 1):
        pltpu.make_async_remote_copy(
            src_ref=sums_out.at[step],
            dst_ref=sums_in.at[me_cd],
            send_sem=sum_send.at[step],
            recv_sem=sum_recv.at[me_cd],
            device_id=(me_ab, me_cd),
            device_id_type=MESH,
        ).wait_send()


def ladder(packed, pair_values, n_ab, n_cd):
    rows, columns = packed.shape
    ab_dev = pair_values.shape[0]
    block = ab_dev // n_cd
    return pl.pallas_call(
        functools.partial(ladder_kernel, n_ab, n_cd),
        out_shape=jax.ShapeDtypeStruct((rows * n_ab, block), jnp.bfloat16),
        in_specs=[pl.BlockSpec(memory_space=pltpu.VMEM), pl.BlockSpec(memory_space=pl.ANY)],
        out_specs=pl.BlockSpec(memory_space=pltpu.VMEM),
        scratch_shapes=[
            pltpu.VMEM((n_ab, rows, columns), packed.dtype),
            pltpu.VMEM((rows * n_ab, columns), jnp.float32),
            pltpu.VMEM((n_cd, block, columns), pair_values.dtype),
            pltpu.VMEM((n_cd - 1, rows * n_ab, block), jnp.float32),
            pltpu.VMEM((n_cd, rows * n_ab, block), jnp.float32),
            pltpu.SemaphoreType.DMA((n_cd,)),
            pltpu.SemaphoreType.DMA((n_ab,)),
            pltpu.SemaphoreType.DMA((n_ab,)),
            pltpu.SemaphoreType.DMA((n_cd,)),
            pltpu.SemaphoreType.DMA((n_cd,)),
            pltpu.SemaphoreType.DMA((1,)),
        ],
        compiler_params=pltpu.CompilerParams(
            collective_id=0, has_side_effects=True, vmem_limit_bytes=48 * 1024 * 1024
        ),
    )(packed, pair_values)


def on_device(n_ab, n_cd, pair_values, amplitudes, cd_first, cd_second, live_cols):
    slab = lax.axis_index("cd")
    orbit_block = amplitudes.shape[1]
    orbitals = amplitudes.shape[2]
    columns = cd_first.shape[0]
    local_first = cd_first - slab * orbit_block
    mirrored = lax.all_to_all(amplitudes, "cd", 2, 1, tiled=True)
    pick_d = (lax.broadcasted_iota(jnp.int32, (orbitals, columns), 0) == cd_second[None, :]).astype(
        amplitudes.dtype
    )
    direct_rows = lax.dot_general(
        amplitudes, pick_d, (((2,), (0,)), ((), ())), preferred_element_type=jnp.float32
    )
    crossed_rows = lax.dot_general(
        mirrored, pick_d, (((1,), (0,)), ((), ())), preferred_element_type=jnp.float32
    )
    pick_c = lax.broadcasted_iota(jnp.int32, (orbit_block, columns), 0) == local_first[None, :]
    both = jnp.sum(jnp.where(pick_c[None], direct_rows + crossed_rows, 0.0), axis=1)
    live_count = live_cols[0]
    slots = jnp.arange(columns, dtype=jnp.int32)
    live = (slots < live_count).astype(jnp.float32)
    half = jnp.where(cd_first == cd_second, jnp.float32(0.5), jnp.float32(1.0))
    weight = half * live
    packed = (both * weight[None, :]).astype(jnp.bfloat16)
    return ladder(packed, pair_values, n_ab, n_cd)


def solution(mesh):
    placed = (P("ab", "cd"), P("ab", "cd", None), P("cd"), P("cd"), P("cd"))
    return jax.shard_map(
        functools.partial(on_device, mesh.shape["ab"], mesh.shape["cd"]),
        mesh=mesh, in_specs=placed, out_specs=P(None, ("ab", "cd")), check_vma=False,
    )
```

```python
import functools

import jax
import jax.numpy as jnp
from jax import lax
from jax.experimental import pallas as pl
from jax.experimental.pallas import tpu as pltpu
from jax.sharding import PartitionSpec as P

MESH = pl.DeviceIdType.MESH


def exchange_kernel(n_cd, chunks_ref, out_ref, landed, send_sem, recv_sem, own_sem):
    me_ab = lax.axis_index("ab")
    me_cd = lax.axis_index("cd")
    barrier = pltpu.get_barrier_semaphore()
    for k in range(1, n_cd):
        peer = lax.rem(me_cd + k, n_cd)
        pl.semaphore_signal(barrier, inc=1, device_id=(me_ab, peer), device_id_type=MESH)
    pl.semaphore_wait(barrier, n_cd - 1)
    own = pltpu.make_async_copy(chunks_ref.at[me_cd], landed.at[me_cd], own_sem.at[0])
    own.start()
    for k in range(1, n_cd):
        peer = lax.rem(me_cd + k, n_cd)
        pltpu.make_async_remote_copy(
            src_ref=chunks_ref.at[peer],
            dst_ref=landed.at[me_cd],
            send_sem=send_sem.at[k],
            recv_sem=recv_sem.at[me_cd],
            device_id=(me_ab, peer),
            device_id_type=MESH,
        ).start()
    own.wait()
    for k in range(1, n_cd):
        src = lax.rem(me_cd + n_cd - k, n_cd)
        pltpu.make_async_remote_copy(
            src_ref=chunks_ref.at[src],
            dst_ref=landed.at[src],
            send_sem=send_sem.at[k],
            recv_sem=recv_sem.at[src],
            device_id=(me_ab, src),
            device_id_type=MESH,
        ).wait_recv()
    out_ref[...] = landed[...]
    for k in range(1, n_cd):
        pltpu.make_async_remote_copy(
            src_ref=chunks_ref.at[me_cd],
            dst_ref=landed.at[me_cd],
            send_sem=send_sem.at[k],
            recv_sem=recv_sem.at[me_cd],
            device_id=(me_ab, me_cd),
            device_id_type=MESH,
        ).wait_send()


def exchange(chunks, n_cd):
    return pl.pallas_call(
        functools.partial(exchange_kernel, n_cd),
        out_shape=jax.ShapeDtypeStruct(chunks.shape, chunks.dtype),
        in_specs=[pl.BlockSpec(memory_space=pltpu.VMEM)],
        out_specs=pl.BlockSpec(memory_space=pltpu.VMEM),
        scratch_shapes=[
            pltpu.VMEM(chunks.shape, chunks.dtype),
            pltpu.SemaphoreType.DMA((n_cd,)),
            pltpu.SemaphoreType.DMA((n_cd,)),
            pltpu.SemaphoreType.DMA((1,)),
        ],
        compiler_params=pltpu.CompilerParams(collective_id=1, has_side_effects=True),
    )(chunks)


def ladder_kernel(
    n_ab, n_cd, packed_ref, values_hbm, out_ref,
    slots, gathered, values_buf, sums_out, sums_in,
    values_sem, pk_send, pk_recv, sum_send, sum_recv, own_sem,
):
    me_ab = lax.axis_index("ab")
    me_cd = lax.axis_index("cd")
    rows = packed_ref.shape[0]
    block = values_buf.shape[1]

    for step in range(n_cd):
        dest = lax.rem(me_cd + 1 + step, n_cd)
        pltpu.make_async_copy(
            values_hbm.at[pl.ds(pl.multiple_of(dest * block, block), block), :],
            values_buf.at[step],
            values_sem.at[step],
        ).start()

    barrier = pltpu.get_barrier_semaphore()
    for k in range(1, n_ab):
        peer = lax.rem(me_ab + k, n_ab)
        pl.semaphore_signal(barrier, inc=1, device_id=(peer, me_cd), device_id_type=MESH)
    for k in range(1, n_cd):
        peer = lax.rem(me_cd + k, n_cd)
        pl.semaphore_signal(barrier, inc=1, device_id=(me_ab, peer), device_id_type=MESH)
    pl.semaphore_wait(barrier, (n_ab - 1) + (n_cd - 1))

    own = pltpu.make_async_copy(packed_ref, slots.at[me_ab], own_sem.at[0])
    own.start()
    for k in range(1, n_ab):
        peer = lax.rem(me_ab + k, n_ab)
        pltpu.make_async_remote_copy(
            src_ref=packed_ref,
            dst_ref=slots.at[me_ab],
            send_sem=pk_send.at[k],
            recv_sem=pk_recv.at[me_ab],
            device_id=(peer, me_cd),
            device_id_type=MESH,
        ).start()
    own.wait()
    for k in range(1, n_ab):
        src = lax.rem(me_ab + n_ab - k, n_ab)
        pltpu.make_async_remote_copy(
            src_ref=packed_ref,
            dst_ref=slots.at[src],
            send_sem=pk_send.at[k],
            recv_sem=pk_recv.at[src],
            device_id=(src, me_cd),
            device_id_type=MESH,
        ).wait_recv()
    for k in range(n_ab):
        gathered[k * rows:(k + 1) * rows, :] = slots[k].astype(jnp.float32)
    lhs = gathered[...].astype(jnp.bfloat16)

    def one_block(step):
        pltpu.make_async_copy(
            values_hbm.at[pl.ds(0, block), :], values_buf.at[step], values_sem.at[step]
        ).wait()
        return lax.dot_general(
            lhs, values_buf[step], (((1,), (1,)), ((), ())), preferred_element_type=jnp.float32
        )

    for step in range(n_cd - 1):
        dest = lax.rem(me_cd + 1 + step, n_cd)
        sums_out[step] = one_block(step)
        pltpu.make_async_remote_copy(
            src_ref=sums_out.at[step],
            dst_ref=sums_in.at[me_cd],
            send_sem=sum_send.at[step],
            recv_sem=sum_recv.at[me_cd],
            device_id=(me_ab, dest),
            device_id_type=MESH,
        ).start()
    total = one_block(n_cd - 1)
    for step in range(n_cd - 1):
        src = lax.rem(me_cd + n_cd - 1 - step, n_cd)
        pltpu.make_async_remote_copy(
            src_ref=sums_out.at[step],
            dst_ref=sums_in.at[src],
            send_sem=sum_send.at[step],
            recv_sem=sum_recv.at[src],
            device_id=(me_ab, src),
            device_id_type=MESH,
        ).wait_recv()
        total = total + sums_in[src]
    out_ref[...] = total.astype(out_ref.dtype)

    for k in range(1, n_ab):
        pltpu.make_async_remote_copy(
            src_ref=packed_ref,
            dst_ref=slots.at[me_ab],
            send_sem=pk_send.at[k],
            recv_sem=pk_recv.at[me_ab],
            device_id=(me_ab, me_cd),
            device_id_type=MESH,
        ).wait_send()
    for step in range(n_cd - 1):
        pltpu.make_async_remote_copy(
            src_ref=sums_out.at[step],
            dst_ref=sums_in.at[me_cd],
            send_sem=sum_send.at[step],
            recv_sem=sum_recv.at[me_cd],
            device_id=(me_ab, me_cd),
            device_id_type=MESH,
        ).wait_send()


def ladder(packed, pair_values, n_ab, n_cd):
    rows, columns = packed.shape
    ab_dev = pair_values.shape[0]
    block = ab_dev // n_cd
    return pl.pallas_call(
        functools.partial(ladder_kernel, n_ab, n_cd),
        out_shape=jax.ShapeDtypeStruct((rows * n_ab, block), jnp.bfloat16),
        in_specs=[pl.BlockSpec(memory_space=pltpu.VMEM), pl.BlockSpec(memory_space=pl.ANY)],
        out_specs=pl.BlockSpec(memory_space=pltpu.VMEM),
        scratch_shapes=[
            pltpu.VMEM((n_ab, rows, columns), packed.dtype),
            pltpu.VMEM((rows * n_ab, columns), jnp.float32),
            pltpu.VMEM((n_cd, block, columns), pair_values.dtype),
            pltpu.VMEM((n_cd - 1, rows * n_ab, block), jnp.float32),
            pltpu.VMEM((n_cd, rows * n_ab, block), jnp.float32),
            pltpu.SemaphoreType.DMA((n_cd,)),
            pltpu.SemaphoreType.DMA((n_ab,)),
            pltpu.SemaphoreType.DMA((n_ab,)),
            pltpu.SemaphoreType.DMA((n_cd,)),
            pltpu.SemaphoreType.DMA((n_cd,)),
            pltpu.SemaphoreType.DMA((1,)),
        ],
        compiler_params=pltpu.CompilerParams(
            collective_id=0, has_side_effects=True, vmem_limit_bytes=48 * 1024 * 1024
        ),
    )(packed, pair_values)


def on_device(n_ab, n_cd, pair_values, amplitudes, cd_first, cd_second, live_cols):
    slab = lax.axis_index("cd")
    orbit_block = amplitudes.shape[1]
    orbitals = amplitudes.shape[2]
    columns = cd_first.shape[0]
    local_first = cd_first - slab * orbit_block
    pair_block = amplitudes.shape[0]
    piece = pair_block * orbit_block * orbit_block
    padded = -(-piece // 1024) * 1024
    chunks = jnp.transpose(amplitudes.reshape(pair_block, orbit_block, n_cd, orbit_block), (2, 0, 1, 3))
    chunks = jnp.pad(chunks.reshape(n_cd, piece), ((0, 0), (0, padded - piece)))
    landed = exchange(chunks.reshape(n_cd, padded // 128, 128), n_cd)
    mirrored = landed.reshape(n_cd, padded)[:, :piece].reshape(n_cd, pair_block, orbit_block, orbit_block)
    pick_d = (lax.broadcasted_iota(jnp.int32, (orbitals, columns), 0) == cd_second[None, :]).astype(
        amplitudes.dtype
    )
    direct_rows = lax.dot_general(
        amplitudes, pick_d, (((2,), (0,)), ((), ())), preferred_element_type=jnp.float32
    )
    crossed_rows = lax.dot_general(
        mirrored,
        pick_d.reshape(n_cd, orbit_block, columns),
        (((0, 2), (0, 1)), ((), ())),
        preferred_element_type=jnp.float32,
    )
    pick_c = lax.broadcasted_iota(jnp.int32, (orbit_block, columns), 0) == local_first[None, :]
    both = jnp.sum(jnp.where(pick_c[None], direct_rows + crossed_rows, 0.0), axis=1)
    live_count = live_cols[0]
    slots = jnp.arange(columns, dtype=jnp.int32)
    live = (slots < live_count).astype(jnp.float32)
    half = jnp.where(cd_first == cd_second, jnp.float32(0.5), jnp.float32(1.0))
    weight = half * live
    packed = (both * weight[None, :]).astype(jnp.bfloat16)
    return ladder(packed, pair_values, n_ab, n_cd)


def solution(mesh):
    placed = (P("ab", "cd"), P("ab", "cd", None), P("cd"), P("cd"), P("cd"))
    return jax.shard_map(
        functools.partial(on_device, mesh.shape["ab"], mesh.shape["cd"]),
        mesh=mesh, in_specs=placed, out_specs=P(None, ("ab", "cd")), check_vma=False,
    )
```

```python
import functools

import jax
import jax.numpy as jnp
from jax import lax
from jax.experimental import pallas as pl
from jax.experimental.pallas import tpu as pltpu
from jax.sharding import PartitionSpec as P

MESH = pl.DeviceIdType.MESH


def exchange_kernel(n_cd, chunks_ref, out_ref, landed, send_sem, recv_sem, own_sem):
    me_ab = lax.axis_index("ab")
    me_cd = lax.axis_index("cd")
    barrier = pltpu.get_barrier_semaphore()
    for k in range(1, n_cd):
        peer = lax.rem(me_cd + k, n_cd)
        pl.semaphore_signal(barrier, inc=1, device_id=(me_ab, peer), device_id_type=MESH)
    pl.semaphore_wait(barrier, n_cd - 1)
    own = pltpu.make_async_copy(chunks_ref.at[me_cd], landed.at[me_cd], own_sem.at[0])
    own.start()
    for k in range(1, n_cd):
        peer = lax.rem(me_cd + k, n_cd)

        @pl.when(peer < me_cd)
        def _():
            pltpu.make_async_remote_copy(
                src_ref=chunks_ref.at[peer],
                dst_ref=landed.at[me_cd],
                send_sem=send_sem.at[k],
                recv_sem=recv_sem.at[me_cd],
                device_id=(me_ab, peer),
                device_id_type=MESH,
            ).start()

    for k in range(1, n_cd):
        src = lax.rem(me_cd + k, n_cd)

        @pl.when(src < me_cd)
        def _():
            landed[src] = jnp.zeros(landed.shape[1:], landed.dtype)

    own.wait()
    for k in range(1, n_cd):
        src = lax.rem(me_cd + n_cd - k, n_cd)

        @pl.when(src > me_cd)
        def _():
            pltpu.make_async_remote_copy(
                src_ref=chunks_ref.at[src],
                dst_ref=landed.at[src],
                send_sem=send_sem.at[k],
                recv_sem=recv_sem.at[src],
                device_id=(me_ab, src),
                device_id_type=MESH,
            ).wait_recv()

    out_ref[...] = landed[...]
    for k in range(1, n_cd):
        peer = lax.rem(me_cd + k, n_cd)

        @pl.when(peer < me_cd)
        def _():
            pltpu.make_async_remote_copy(
                src_ref=chunks_ref.at[me_cd],
                dst_ref=landed.at[me_cd],
                send_sem=send_sem.at[k],
                recv_sem=recv_sem.at[me_cd],
                device_id=(me_ab, me_cd),
                device_id_type=MESH,
            ).wait_send()


def exchange(chunks, n_cd):
    return pl.pallas_call(
        functools.partial(exchange_kernel, n_cd),
        out_shape=jax.ShapeDtypeStruct(chunks.shape, chunks.dtype),
        in_specs=[pl.BlockSpec(memory_space=pltpu.VMEM)],
        out_specs=pl.BlockSpec(memory_space=pltpu.VMEM),
        scratch_shapes=[
            pltpu.VMEM(chunks.shape, chunks.dtype),
            pltpu.SemaphoreType.DMA((n_cd,)),
            pltpu.SemaphoreType.DMA((n_cd,)),
            pltpu.SemaphoreType.DMA((1,)),
        ],
        compiler_params=pltpu.CompilerParams(collective_id=1, has_side_effects=True),
    )(chunks)


def ladder_kernel(
    n_ab, n_cd, packed_ref, values_hbm, out_ref,
    slots, gathered, values_buf, sums_out, sums_in,
    values_sem, pk_send, pk_recv, sum_send, sum_recv, own_sem,
):
    me_ab = lax.axis_index("ab")
    me_cd = lax.axis_index("cd")
    rows = packed_ref.shape[0]
    block = values_buf.shape[1]

    for step in range(n_cd):
        dest = lax.rem(me_cd + 1 + step, n_cd)
        pltpu.make_async_copy(
            values_hbm.at[pl.ds(pl.multiple_of(dest * block, block), block), :],
            values_buf.at[step],
            values_sem.at[step],
        ).start()

    barrier = pltpu.get_barrier_semaphore()
    for k in range(1, n_ab):
        peer = lax.rem(me_ab + k, n_ab)
        pl.semaphore_signal(barrier, inc=1, device_id=(peer, me_cd), device_id_type=MESH)
    for k in range(1, n_cd):
        peer = lax.rem(me_cd + k, n_cd)
        pl.semaphore_signal(barrier, inc=1, device_id=(me_ab, peer), device_id_type=MESH)
    pl.semaphore_wait(barrier, (n_ab - 1) + (n_cd - 1))

    own = pltpu.make_async_copy(packed_ref, slots.at[me_ab], own_sem.at[0])
    own.start()
    for k in range(1, n_ab):
        peer = lax.rem(me_ab + k, n_ab)
        pltpu.make_async_remote_copy(
            src_ref=packed_ref,
            dst_ref=slots.at[me_ab],
            send_sem=pk_send.at[k],
            recv_sem=pk_recv.at[me_ab],
            device_id=(peer, me_cd),
            device_id_type=MESH,
        ).start()
    own.wait()
    for k in range(1, n_ab):
        src = lax.rem(me_ab + n_ab - k, n_ab)
        pltpu.make_async_remote_copy(
            src_ref=packed_ref,
            dst_ref=slots.at[src],
            send_sem=pk_send.at[k],
            recv_sem=pk_recv.at[src],
            device_id=(src, me_cd),
            device_id_type=MESH,
        ).wait_recv()
    for k in range(n_ab):
        gathered[k * rows:(k + 1) * rows, :] = slots[k].astype(jnp.float32)
    lhs = gathered[...].astype(jnp.bfloat16)

    def one_block(step):
        pltpu.make_async_copy(
            values_hbm.at[pl.ds(0, block), :], values_buf.at[step], values_sem.at[step]
        ).wait()
        return lax.dot_general(
            lhs, values_buf[step], (((1,), (1,)), ((), ())), preferred_element_type=jnp.float32
        )

    for step in range(n_cd - 1):
        dest = lax.rem(me_cd + 1 + step, n_cd)
        sums_out[step] = one_block(step).astype(sums_out.dtype)
        pltpu.make_async_remote_copy(
            src_ref=sums_out.at[step],
            dst_ref=sums_in.at[me_cd],
            send_sem=sum_send.at[step],
            recv_sem=sum_recv.at[me_cd],
            device_id=(me_ab, dest),
            device_id_type=MESH,
        ).start()
    total = one_block(n_cd - 1)
    for step in range(n_cd - 1):
        src = lax.rem(me_cd + n_cd - 1 - step, n_cd)
        pltpu.make_async_remote_copy(
            src_ref=sums_out.at[step],
            dst_ref=sums_in.at[src],
            send_sem=sum_send.at[step],
            recv_sem=sum_recv.at[src],
            device_id=(me_ab, src),
            device_id_type=MESH,
        ).wait_recv()
        total = total + sums_in[src].astype(jnp.float32)
    out_ref[...] = total.astype(out_ref.dtype)

    for k in range(1, n_ab):
        pltpu.make_async_remote_copy(
            src_ref=packed_ref,
            dst_ref=slots.at[me_ab],
            send_sem=pk_send.at[k],
            recv_sem=pk_recv.at[me_ab],
            device_id=(me_ab, me_cd),
            device_id_type=MESH,
        ).wait_send()
    for step in range(n_cd - 1):
        pltpu.make_async_remote_copy(
            src_ref=sums_out.at[step],
            dst_ref=sums_in.at[me_cd],
            send_sem=sum_send.at[step],
            recv_sem=sum_recv.at[me_cd],
            device_id=(me_ab, me_cd),
            device_id_type=MESH,
        ).wait_send()


def ladder(packed, pair_values, n_ab, n_cd):
    rows, columns = packed.shape
    ab_dev = pair_values.shape[0]
    block = ab_dev // n_cd
    return pl.pallas_call(
        functools.partial(ladder_kernel, n_ab, n_cd),
        out_shape=jax.ShapeDtypeStruct((rows * n_ab, block), jnp.bfloat16),
        in_specs=[pl.BlockSpec(memory_space=pltpu.VMEM), pl.BlockSpec(memory_space=pl.ANY)],
        out_specs=pl.BlockSpec(memory_space=pltpu.VMEM),
        scratch_shapes=[
            pltpu.VMEM((n_ab, rows, columns), packed.dtype),
            pltpu.VMEM((rows * n_ab, columns), jnp.float32),
            pltpu.VMEM((n_cd, block, columns), pair_values.dtype),
            pltpu.VMEM((n_cd - 1, rows * n_ab, block), jnp.bfloat16),
            pltpu.VMEM((n_cd, rows * n_ab, block), jnp.bfloat16),
            pltpu.SemaphoreType.DMA((n_cd,)),
            pltpu.SemaphoreType.DMA((n_ab,)),
            pltpu.SemaphoreType.DMA((n_ab,)),
            pltpu.SemaphoreType.DMA((n_cd,)),
            pltpu.SemaphoreType.DMA((n_cd,)),
            pltpu.SemaphoreType.DMA((1,)),
        ],
        compiler_params=pltpu.CompilerParams(
            collective_id=0, has_side_effects=True, vmem_limit_bytes=48 * 1024 * 1024
        ),
    )(packed, pair_values)


def on_device(n_ab, n_cd, pair_values, amplitudes, cd_first, cd_second, live_cols):
    slab = lax.axis_index("cd")
    orbit_block = amplitudes.shape[1]
    orbitals = amplitudes.shape[2]
    columns = cd_first.shape[0]
    local_first = cd_first - slab * orbit_block
    pair_block = amplitudes.shape[0]
    piece = pair_block * orbit_block * orbit_block
    padded = -(-piece // 1024) * 1024
    chunks = jnp.transpose(amplitudes.reshape(pair_block, orbit_block, n_cd, orbit_block), (2, 0, 1, 3))
    chunks = jnp.pad(chunks.reshape(n_cd, piece), ((0, 0), (0, padded - piece)))
    landed = exchange(chunks.reshape(n_cd, padded // 128, 128), n_cd)
    mirrored = landed.reshape(n_cd, padded)[:, :piece].reshape(n_cd, pair_block, orbit_block, orbit_block)
    pick_d = (lax.broadcasted_iota(jnp.int32, (orbitals, columns), 0) == cd_second[None, :]).astype(
        amplitudes.dtype
    )
    direct_rows = lax.dot_general(
        amplitudes, pick_d, (((2,), (0,)), ((), ())), preferred_element_type=jnp.float32
    )
    crossed_rows = lax.dot_general(
        mirrored,
        pick_d.reshape(n_cd, orbit_block, columns),
        (((0, 2), (0, 1)), ((), ())),
        preferred_element_type=jnp.float32,
    )
    pick_c = lax.broadcasted_iota(jnp.int32, (orbit_block, columns), 0) == local_first[None, :]
    both = jnp.sum(jnp.where(pick_c[None], direct_rows + crossed_rows, 0.0), axis=1)
    live_count = live_cols[0]
    slots = jnp.arange(columns, dtype=jnp.int32)
    live = (slots < live_count).astype(jnp.float32)
    half = jnp.where(cd_first == cd_second, jnp.float32(0.5), jnp.float32(1.0))
    weight = half * live
    packed = (both * weight[None, :]).astype(jnp.bfloat16)
    return ladder(packed, pair_values, n_ab, n_cd)


def solution(mesh):
    placed = (P("ab", "cd"), P("ab", "cd", None), P("cd"), P("cd"), P("cd"))
    return jax.shard_map(
        functools.partial(on_device, mesh.shape["ab"], mesh.shape["cd"]),
        mesh=mesh, in_specs=placed, out_specs=P(None, ("ab", "cd")), check_vma=False,
    )
```

```python
import functools

import jax
import jax.numpy as jnp
from jax import lax
from jax.experimental import pallas as pl
from jax.experimental.pallas import tpu as pltpu
from jax.sharding import PartitionSpec as P

MESH = pl.DeviceIdType.MESH
X_CHIPS = 4


def exchange_kernel(n_cd, chunks_ref, out_ref, landed, send_sem, recv_sem, own_sem):
    me_ab = lax.axis_index("ab")
    me_cd = lax.axis_index("cd")
    barrier = pltpu.get_barrier_semaphore()
    for k in range(1, n_cd):
        peer = lax.rem(me_cd + k, n_cd)
        pl.semaphore_signal(barrier, inc=1, device_id=(me_ab, peer), device_id_type=MESH)
    pl.semaphore_wait(barrier, n_cd - 1)
    own = pltpu.make_async_copy(chunks_ref.at[me_cd], landed.at[me_cd], own_sem.at[0])
    own.start()
    for k in range(1, n_cd):
        peer = lax.rem(me_cd + k, n_cd)

        @pl.when(peer < me_cd)
        def _():
            pltpu.make_async_remote_copy(
                src_ref=chunks_ref.at[peer],
                dst_ref=landed.at[me_cd],
                send_sem=send_sem.at[k],
                recv_sem=recv_sem.at[me_cd],
                device_id=(me_ab, peer),
                device_id_type=MESH,
            ).start()

    for k in range(1, n_cd):
        src = lax.rem(me_cd + k, n_cd)

        @pl.when(src < me_cd)
        def _():
            landed[src] = jnp.zeros(landed.shape[1:], landed.dtype)

    own.wait()
    for k in range(1, n_cd):
        src = lax.rem(me_cd + n_cd - k, n_cd)

        @pl.when(src > me_cd)
        def _():
            pltpu.make_async_remote_copy(
                src_ref=chunks_ref.at[src],
                dst_ref=landed.at[src],
                send_sem=send_sem.at[k],
                recv_sem=recv_sem.at[src],
                device_id=(me_ab, src),
                device_id_type=MESH,
            ).wait_recv()

    out_ref[...] = landed[...]
    for k in range(1, n_cd):
        peer = lax.rem(me_cd + k, n_cd)

        @pl.when(peer < me_cd)
        def _():
            pltpu.make_async_remote_copy(
                src_ref=chunks_ref.at[me_cd],
                dst_ref=landed.at[me_cd],
                send_sem=send_sem.at[k],
                recv_sem=recv_sem.at[me_cd],
                device_id=(me_ab, me_cd),
                device_id_type=MESH,
            ).wait_send()


def exchange(chunks, n_cd):
    return pl.pallas_call(
        functools.partial(exchange_kernel, n_cd),
        out_shape=jax.ShapeDtypeStruct(chunks.shape, chunks.dtype),
        in_specs=[pl.BlockSpec(memory_space=pltpu.VMEM)],
        out_specs=pl.BlockSpec(memory_space=pltpu.VMEM),
        scratch_shapes=[
            pltpu.VMEM(chunks.shape, chunks.dtype),
            pltpu.SemaphoreType.DMA((n_cd,)),
            pltpu.SemaphoreType.DMA((n_cd,)),
            pltpu.SemaphoreType.DMA((1,)),
        ],
        compiler_params=pltpu.CompilerParams(collective_id=1, has_side_effects=True),
    )(chunks)


def ladder_kernel(
    n_ab, n_x, n_z, packed_ref, values_hbm, out_ref,
    slots, gathered, values_buf, first_out, first_in, second_out, second_in,
    values_sem, pk_send, pk_recv, first_send, first_recv, second_send, second_recv, own_sem,
):
    me_ab = lax.axis_index("ab")
    me_cd = lax.axis_index("cd")
    me_z = me_cd // n_x
    me_x = lax.rem(me_cd, n_x)
    rows = packed_ref.shape[0]
    block = values_buf.shape[1]

    order = []
    for k in list(range(1, n_x)) + [0]:
        for z in range(n_z):
            order.append(z * n_x + lax.rem(me_x + k, n_x))
    for step, owner in enumerate(order):
        pltpu.make_async_copy(
            values_hbm.at[pl.ds(pl.multiple_of(owner * block, block), block), :],
            values_buf.at[step],
            values_sem.at[step],
        ).start()

    barrier = pltpu.get_barrier_semaphore()
    for k in range(1, n_ab):
        peer = lax.rem(me_ab + k, n_ab)
        pl.semaphore_signal(barrier, inc=1, device_id=(peer, me_cd), device_id_type=MESH)
    for k in range(1, n_x):
        peer = me_z * n_x + lax.rem(me_x + k, n_x)
        pl.semaphore_signal(barrier, inc=1, device_id=(me_ab, peer), device_id_type=MESH)
    for j in range(1, n_z):
        peer = lax.rem(me_z + j, n_z) * n_x + me_x
        pl.semaphore_signal(barrier, inc=1, device_id=(me_ab, peer), device_id_type=MESH)
    pl.semaphore_wait(barrier, (n_ab - 1) + (n_x - 1) + (n_z - 1))

    own = pltpu.make_async_copy(packed_ref, slots.at[me_ab], own_sem.at[0])
    own.start()
    for k in range(1, n_ab):
        peer = lax.rem(me_ab + k, n_ab)
        pltpu.make_async_remote_copy(
            src_ref=packed_ref,
            dst_ref=slots.at[me_ab],
            send_sem=pk_send.at[k],
            recv_sem=pk_recv.at[me_ab],
            device_id=(peer, me_cd),
            device_id_type=MESH,
        ).start()
    own.wait()
    for k in range(1, n_ab):
        src = lax.rem(me_ab + n_ab - k, n_ab)
        pltpu.make_async_remote_copy(
            src_ref=packed_ref,
            dst_ref=slots.at[src],
            send_sem=pk_send.at[k],
            recv_sem=pk_recv.at[src],
            device_id=(src, me_cd),
            device_id_type=MESH,
        ).wait_recv()
    for k in range(n_ab):
        gathered[k * rows:(k + 1) * rows, :] = slots[k].astype(jnp.float32)
    lhs = gathered[...].astype(jnp.bfloat16)

    def one_block(step):
        pltpu.make_async_copy(
            values_hbm.at[pl.ds(0, block), :], values_buf.at[step], values_sem.at[step]
        ).wait()
        return lax.dot_general(
            lhs, values_buf[step], (((1,), (1,)), ((), ())), preferred_element_type=jnp.float32
        )

    for k in range(1, n_x):
        peer = me_z * n_x + lax.rem(me_x + k, n_x)
        for z in range(n_z):
            first_out[k - 1, z] = one_block((k - 1) * n_z + z)
        pltpu.make_async_remote_copy(
            src_ref=first_out.at[k - 1],
            dst_ref=first_in.at[k - 1],
            send_sem=first_send.at[k - 1],
            recv_sem=first_recv.at[k - 1],
            device_id=(me_ab, peer),
            device_id_type=MESH,
        ).start()
    stage = [one_block((n_x - 1) * n_z + z) for z in range(n_z)]
    for k in range(1, n_x):
        src = me_z * n_x + lax.rem(me_x + n_x - k, n_x)
        pltpu.make_async_remote_copy(
            src_ref=first_out.at[k - 1],
            dst_ref=first_in.at[k - 1],
            send_sem=first_send.at[k - 1],
            recv_sem=first_recv.at[k - 1],
            device_id=(me_ab, src),
            device_id_type=MESH,
        ).wait_recv()
        stage = [stage[z] + first_in[k - 1, z] for z in range(n_z)]

    for j in range(1, n_z):
        dest_z = lax.rem(me_z + j, n_z)
        peer = dest_z * n_x + me_x
        picked = stage[0]
        for z in range(1, n_z):
            picked = jnp.where(dest_z == z, stage[z], picked)
        second_out[j - 1] = picked
        pltpu.make_async_remote_copy(
            src_ref=second_out.at[j - 1],
            dst_ref=second_in.at[j - 1],
            send_sem=second_send.at[j - 1],
            recv_sem=second_recv.at[j - 1],
            device_id=(me_ab, peer),
            device_id_type=MESH,
        ).start()
    total = stage[0]
    for z in range(1, n_z):
        total = jnp.where(me_z == z, stage[z], total)
    for j in range(1, n_z):
        src = lax.rem(me_z + n_z - j, n_z) * n_x + me_x
        pltpu.make_async_remote_copy(
            src_ref=second_out.at[j - 1],
            dst_ref=second_in.at[j - 1],
            send_sem=second_send.at[j - 1],
            recv_sem=second_recv.at[j - 1],
            device_id=(me_ab, src),
            device_id_type=MESH,
        ).wait_recv()
        total = total + second_in[j - 1]
    out_ref[...] = total.astype(out_ref.dtype)

    for k in range(1, n_ab):
        pltpu.make_async_remote_copy(
            src_ref=packed_ref,
            dst_ref=slots.at[me_ab],
            send_sem=pk_send.at[k],
            recv_sem=pk_recv.at[me_ab],
            device_id=(me_ab, me_cd),
            device_id_type=MESH,
        ).wait_send()
    for k in range(1, n_x):
        pltpu.make_async_remote_copy(
            src_ref=first_out.at[k - 1],
            dst_ref=first_in.at[k - 1],
            send_sem=first_send.at[k - 1],
            recv_sem=first_recv.at[k - 1],
            device_id=(me_ab, me_cd),
            device_id_type=MESH,
        ).wait_send()
    for j in range(1, n_z):
        pltpu.make_async_remote_copy(
            src_ref=second_out.at[j - 1],
            dst_ref=second_in.at[j - 1],
            send_sem=second_send.at[j - 1],
            recv_sem=second_recv.at[j - 1],
            device_id=(me_ab, me_cd),
            device_id_type=MESH,
        ).wait_send()


def ladder(packed, pair_values, n_ab, n_cd):
    rows, columns = packed.shape
    ab_dev = pair_values.shape[0]
    block = ab_dev // n_cd
    n_x = X_CHIPS
    n_z = n_cd // n_x
    width = rows * n_ab
    return pl.pallas_call(
        functools.partial(ladder_kernel, n_ab, n_x, n_z),
        out_shape=jax.ShapeDtypeStruct((width, block), jnp.bfloat16),
        in_specs=[pl.BlockSpec(memory_space=pltpu.VMEM), pl.BlockSpec(memory_space=pl.ANY)],
        out_specs=pl.BlockSpec(memory_space=pltpu.VMEM),
        scratch_shapes=[
            pltpu.VMEM((n_ab, rows, columns), packed.dtype),
            pltpu.VMEM((width, columns), jnp.float32),
            pltpu.VMEM((n_cd, block, columns), pair_values.dtype),
            pltpu.VMEM((n_x - 1, n_z, width, block), jnp.float32),
            pltpu.VMEM((n_x - 1, n_z, width, block), jnp.float32),
            pltpu.VMEM((n_z - 1, width, block), jnp.float32),
            pltpu.VMEM((n_z - 1, width, block), jnp.float32),
            pltpu.SemaphoreType.DMA((n_cd,)),
            pltpu.SemaphoreType.DMA((n_ab,)),
            pltpu.SemaphoreType.DMA((n_ab,)),
            pltpu.SemaphoreType.DMA((n_x - 1,)),
            pltpu.SemaphoreType.DMA((n_x - 1,)),
            pltpu.SemaphoreType.DMA((n_z - 1,)),
            pltpu.SemaphoreType.DMA((n_z - 1,)),
            pltpu.SemaphoreType.DMA((1,)),
        ],
        compiler_params=pltpu.CompilerParams(
            collective_id=0, has_side_effects=True, vmem_limit_bytes=48 * 1024 * 1024
        ),
    )(packed, pair_values)


def on_device(n_ab, n_cd, pair_values, amplitudes, cd_first, cd_second, live_cols):
    slab = lax.axis_index("cd")
    orbit_block = amplitudes.shape[1]
    orbitals = amplitudes.shape[2]
    columns = cd_first.shape[0]
    local_first = cd_first - slab * orbit_block
    pair_block = amplitudes.shape[0]
    piece = pair_block * orbit_block * orbit_block
    padded = -(-piece // 1024) * 1024
    chunks = jnp.transpose(amplitudes.reshape(pair_block, orbit_block, n_cd, orbit_block), (2, 0, 1, 3))
    chunks = jnp.pad(chunks.reshape(n_cd, piece), ((0, 0), (0, padded - piece)))
    landed = exchange(chunks.reshape(n_cd, padded // 128, 128), n_cd)
    mirrored = landed.reshape(n_cd, padded)[:, :piece].reshape(n_cd, pair_block, orbit_block, orbit_block)
    pick_d = (lax.broadcasted_iota(jnp.int32, (orbitals, columns), 0) == cd_second[None, :]).astype(
        amplitudes.dtype
    )
    direct_rows = lax.dot_general(
        amplitudes, pick_d, (((2,), (0,)), ((), ())), preferred_element_type=jnp.float32
    )
    crossed_rows = lax.dot_general(
        mirrored,
        pick_d.reshape(n_cd, orbit_block, columns),
        (((0, 2), (0, 1)), ((), ())),
        preferred_element_type=jnp.float32,
    )
    pick_c = lax.broadcasted_iota(jnp.int32, (orbit_block, columns), 0) == local_first[None, :]
    both = jnp.sum(jnp.where(pick_c[None], direct_rows + crossed_rows, 0.0), axis=1)
    live_count = live_cols[0]
    slots = jnp.arange(columns, dtype=jnp.int32)
    live = (slots < live_count).astype(jnp.float32)
    half = jnp.where(cd_first == cd_second, jnp.float32(0.5), jnp.float32(1.0))
    weight = half * live
    packed = (both * weight[None, :]).astype(jnp.bfloat16)
    return ladder(packed, pair_values, n_ab, n_cd)


def solution(mesh):
    placed = (P("ab", "cd"), P("ab", "cd", None), P("cd"), P("cd"), P("cd"))
    return jax.shard_map(
        functools.partial(on_device, mesh.shape["ab"], mesh.shape["cd"]),
        mesh=mesh, in_specs=placed, out_specs=P(None, ("ab", "cd")), check_vma=False,
    )
```

```python
import functools

import jax
import jax.numpy as jnp
from jax import lax
from jax.experimental import pallas as pl
from jax.experimental.pallas import tpu as pltpu
from jax.sharding import PartitionSpec as P

MESH = pl.DeviceIdType.MESH
X_CHIPS = 4


def exchange_kernel(n_cd, chunks_ref, out_ref, landed, send_sem, recv_sem, own_sem):
    me_ab = lax.axis_index("ab")
    me_cd = lax.axis_index("cd")
    barrier = pltpu.get_barrier_semaphore()
    for k in range(1, n_cd):
        peer = lax.rem(me_cd + k, n_cd)
        pl.semaphore_signal(barrier, inc=1, device_id=(me_ab, peer), device_id_type=MESH)
    pl.semaphore_wait(barrier, n_cd - 1)
    own = pltpu.make_async_copy(chunks_ref.at[me_cd], landed.at[me_cd], own_sem.at[0])
    own.start()
    for k in range(1, n_cd):
        peer = lax.rem(me_cd + k, n_cd)

        @pl.when(peer < me_cd)
        def _():
            pltpu.make_async_remote_copy(
                src_ref=chunks_ref.at[peer],
                dst_ref=landed.at[me_cd],
                send_sem=send_sem.at[k],
                recv_sem=recv_sem.at[me_cd],
                device_id=(me_ab, peer),
                device_id_type=MESH,
            ).start()

    for k in range(1, n_cd):
        src = lax.rem(me_cd + k, n_cd)

        @pl.when(src < me_cd)
        def _():
            landed[src] = jnp.zeros(landed.shape[1:], landed.dtype)

    own.wait()
    for k in range(1, n_cd):
        src = lax.rem(me_cd + n_cd - k, n_cd)

        @pl.when(src > me_cd)
        def _():
            pltpu.make_async_remote_copy(
                src_ref=chunks_ref.at[src],
                dst_ref=landed.at[src],
                send_sem=send_sem.at[k],
                recv_sem=recv_sem.at[src],
                device_id=(me_ab, src),
                device_id_type=MESH,
            ).wait_recv()

    out_ref[...] = landed[...]
    for k in range(1, n_cd):
        peer = lax.rem(me_cd + k, n_cd)

        @pl.when(peer < me_cd)
        def _():
            pltpu.make_async_remote_copy(
                src_ref=chunks_ref.at[me_cd],
                dst_ref=landed.at[me_cd],
                send_sem=send_sem.at[k],
                recv_sem=recv_sem.at[me_cd],
                device_id=(me_ab, me_cd),
                device_id_type=MESH,
            ).wait_send()


def exchange(chunks, n_cd):
    return pl.pallas_call(
        functools.partial(exchange_kernel, n_cd),
        out_shape=jax.ShapeDtypeStruct(chunks.shape, chunks.dtype),
        in_specs=[pl.BlockSpec(memory_space=pltpu.VMEM)],
        out_specs=pl.BlockSpec(memory_space=pltpu.VMEM),
        scratch_shapes=[
            pltpu.VMEM(chunks.shape, chunks.dtype),
            pltpu.SemaphoreType.DMA((n_cd,)),
            pltpu.SemaphoreType.DMA((n_cd,)),
            pltpu.SemaphoreType.DMA((1,)),
        ],
        compiler_params=pltpu.CompilerParams(collective_id=1, has_side_effects=True),
    )(chunks)


def ladder_kernel(
    n_ab, n_x, n_z, packed_ref, values_hbm, out_ref,
    slots, gathered, values_buf, first_out, first_in, second_out, second_in,
    values_sem, pk_send, pk_recv, first_send, first_recv, second_send, second_recv, own_sem,
):
    me_ab = lax.axis_index("ab")
    me_cd = lax.axis_index("cd")
    me_z = me_cd // n_x
    me_x = lax.rem(me_cd, n_x)
    rows = packed_ref.shape[0]
    block = values_buf.shape[1]

    order = []
    for k in list(range(1, n_x)) + [0]:
        for z in range(n_z):
            order.append(z * n_x + lax.rem(me_x + k, n_x))
    for step, owner in enumerate(order):
        pltpu.make_async_copy(
            values_hbm.at[pl.ds(pl.multiple_of(owner * block, block), block), :],
            values_buf.at[step],
            values_sem.at[step],
        ).start()

    barrier = pltpu.get_barrier_semaphore()
    for k in range(1, n_ab):
        peer = lax.rem(me_ab + k, n_ab)
        pl.semaphore_signal(barrier, inc=1, device_id=(peer, me_cd), device_id_type=MESH)
    for k in range(1, n_x):
        peer = me_z * n_x + lax.rem(me_x + k, n_x)
        pl.semaphore_signal(barrier, inc=1, device_id=(me_ab, peer), device_id_type=MESH)
    for j in range(1, n_z):
        peer = lax.rem(me_z + j, n_z) * n_x + me_x
        pl.semaphore_signal(barrier, inc=1, device_id=(me_ab, peer), device_id_type=MESH)
    pl.semaphore_wait(barrier, (n_ab - 1) + (n_x - 1) + (n_z - 1))

    own = pltpu.make_async_copy(packed_ref, slots.at[me_ab], own_sem.at[0])
    own.start()
    for k in range(1, n_ab):
        peer = lax.rem(me_ab + k, n_ab)
        pltpu.make_async_remote_copy(
            src_ref=packed_ref,
            dst_ref=slots.at[me_ab],
            send_sem=pk_send.at[k],
            recv_sem=pk_recv.at[me_ab],
            device_id=(peer, me_cd),
            device_id_type=MESH,
        ).start()
    own.wait()
    for k in range(1, n_ab):
        src = lax.rem(me_ab + n_ab - k, n_ab)
        pltpu.make_async_remote_copy(
            src_ref=packed_ref,
            dst_ref=slots.at[src],
            send_sem=pk_send.at[k],
            recv_sem=pk_recv.at[src],
            device_id=(src, me_cd),
            device_id_type=MESH,
        ).wait_recv()
    for k in range(n_ab):
        gathered[k * rows:(k + 1) * rows, :] = slots[k].astype(jnp.float32)
    lhs = gathered[...].astype(jnp.bfloat16)

    def one_block(step):
        pltpu.make_async_copy(
            values_hbm.at[pl.ds(0, block), :], values_buf.at[step], values_sem.at[step]
        ).wait()
        return lax.dot_general(
            lhs, values_buf[step], (((1,), (1,)), ((), ())), preferred_element_type=jnp.float32
        )

    for k in range(1, n_x):
        peer = me_z * n_x + lax.rem(me_x + k, n_x)
        for z in range(n_z):
            first_out[k - 1, z] = one_block((k - 1) * n_z + z).astype(first_out.dtype)
        pltpu.make_async_remote_copy(
            src_ref=first_out.at[k - 1],
            dst_ref=first_in.at[k - 1],
            send_sem=first_send.at[k - 1],
            recv_sem=first_recv.at[k - 1],
            device_id=(me_ab, peer),
            device_id_type=MESH,
        ).start()
    stage = [one_block((n_x - 1) * n_z + z) for z in range(n_z)]
    for k in range(1, n_x):
        src = me_z * n_x + lax.rem(me_x + n_x - k, n_x)
        pltpu.make_async_remote_copy(
            src_ref=first_out.at[k - 1],
            dst_ref=first_in.at[k - 1],
            send_sem=first_send.at[k - 1],
            recv_sem=first_recv.at[k - 1],
            device_id=(me_ab, src),
            device_id_type=MESH,
        ).wait_recv()
        stage = [stage[z] + first_in[k - 1, z].astype(jnp.float32) for z in range(n_z)]

    for j in range(1, n_z):
        dest_z = lax.rem(me_z + j, n_z)
        peer = dest_z * n_x + me_x
        picked = stage[0]
        for z in range(1, n_z):
            picked = jnp.where(dest_z == z, stage[z], picked)
        second_out[j - 1] = picked.astype(second_out.dtype)
        pltpu.make_async_remote_copy(
            src_ref=second_out.at[j - 1],
            dst_ref=second_in.at[j - 1],
            send_sem=second_send.at[j - 1],
            recv_sem=second_recv.at[j - 1],
            device_id=(me_ab, peer),
            device_id_type=MESH,
        ).start()
    total = stage[0]
    for z in range(1, n_z):
        total = jnp.where(me_z == z, stage[z], total)
    for j in range(1, n_z):
        src = lax.rem(me_z + n_z - j, n_z) * n_x + me_x
        pltpu.make_async_remote_copy(
            src_ref=second_out.at[j - 1],
            dst_ref=second_in.at[j - 1],
            send_sem=second_send.at[j - 1],
            recv_sem=second_recv.at[j - 1],
            device_id=(me_ab, src),
            device_id_type=MESH,
        ).wait_recv()
        total = total + second_in[j - 1].astype(jnp.float32)
    out_ref[...] = total.astype(out_ref.dtype)

    for k in range(1, n_ab):
        pltpu.make_async_remote_copy(
            src_ref=packed_ref,
            dst_ref=slots.at[me_ab],
            send_sem=pk_send.at[k],
            recv_sem=pk_recv.at[me_ab],
            device_id=(me_ab, me_cd),
            device_id_type=MESH,
        ).wait_send()
    for k in range(1, n_x):
        pltpu.make_async_remote_copy(
            src_ref=first_out.at[k - 1],
            dst_ref=first_in.at[k - 1],
            send_sem=first_send.at[k - 1],
            recv_sem=first_recv.at[k - 1],
            device_id=(me_ab, me_cd),
            device_id_type=MESH,
        ).wait_send()
    for j in range(1, n_z):
        pltpu.make_async_remote_copy(
            src_ref=second_out.at[j - 1],
            dst_ref=second_in.at[j - 1],
            send_sem=second_send.at[j - 1],
            recv_sem=second_recv.at[j - 1],
            device_id=(me_ab, me_cd),
            device_id_type=MESH,
        ).wait_send()


def ladder(packed, pair_values, n_ab, n_cd):
    rows, columns = packed.shape
    ab_dev = pair_values.shape[0]
    block = ab_dev // n_cd
    n_x = X_CHIPS
    n_z = n_cd // n_x
    width = rows * n_ab
    return pl.pallas_call(
        functools.partial(ladder_kernel, n_ab, n_x, n_z),
        out_shape=jax.ShapeDtypeStruct((width, block), jnp.bfloat16),
        in_specs=[pl.BlockSpec(memory_space=pltpu.VMEM), pl.BlockSpec(memory_space=pl.ANY)],
        out_specs=pl.BlockSpec(memory_space=pltpu.VMEM),
        scratch_shapes=[
            pltpu.VMEM((n_ab, rows, columns), packed.dtype),
            pltpu.VMEM((width, columns), jnp.float32),
            pltpu.VMEM((n_cd, block, columns), pair_values.dtype),
            pltpu.VMEM((n_x - 1, n_z, width, block), jnp.bfloat16),
            pltpu.VMEM((n_x - 1, n_z, width, block), jnp.bfloat16),
            pltpu.VMEM((n_z - 1, width, block), jnp.bfloat16),
            pltpu.VMEM((n_z - 1, width, block), jnp.bfloat16),
            pltpu.SemaphoreType.DMA((n_cd,)),
            pltpu.SemaphoreType.DMA((n_ab,)),
            pltpu.SemaphoreType.DMA((n_ab,)),
            pltpu.SemaphoreType.DMA((n_x - 1,)),
            pltpu.SemaphoreType.DMA((n_x - 1,)),
            pltpu.SemaphoreType.DMA((n_z - 1,)),
            pltpu.SemaphoreType.DMA((n_z - 1,)),
            pltpu.SemaphoreType.DMA((1,)),
        ],
        compiler_params=pltpu.CompilerParams(
            collective_id=0, has_side_effects=True, vmem_limit_bytes=48 * 1024 * 1024
        ),
    )(packed, pair_values)


def on_device(n_ab, n_cd, pair_values, amplitudes, cd_first, cd_second, live_cols):
    slab = lax.axis_index("cd")
    orbit_block = amplitudes.shape[1]
    orbitals = amplitudes.shape[2]
    columns = cd_first.shape[0]
    local_first = cd_first - slab * orbit_block
    pair_block = amplitudes.shape[0]
    piece = pair_block * orbit_block * orbit_block
    padded = -(-piece // 1024) * 1024
    chunks = jnp.transpose(amplitudes.reshape(pair_block, orbit_block, n_cd, orbit_block), (2, 0, 1, 3))
    chunks = jnp.pad(chunks.reshape(n_cd, piece), ((0, 0), (0, padded - piece)))
    landed = exchange(chunks.reshape(n_cd, padded // 128, 128), n_cd)
    mirrored = landed.reshape(n_cd, padded)[:, :piece].reshape(n_cd, pair_block, orbit_block, orbit_block)
    pick_d = (lax.broadcasted_iota(jnp.int32, (orbitals, columns), 0) == cd_second[None, :]).astype(
        amplitudes.dtype
    )
    direct_rows = lax.dot_general(
        amplitudes, pick_d, (((2,), (0,)), ((), ())), preferred_element_type=jnp.float32
    )
    crossed_rows = lax.dot_general(
        mirrored,
        pick_d.reshape(n_cd, orbit_block, columns),
        (((0, 2), (0, 1)), ((), ())),
        preferred_element_type=jnp.float32,
    )
    pick_c = lax.broadcasted_iota(jnp.int32, (orbit_block, columns), 0) == local_first[None, :]
    both = jnp.sum(jnp.where(pick_c[None], direct_rows + crossed_rows, 0.0), axis=1)
    live_count = live_cols[0]
    slots = jnp.arange(columns, dtype=jnp.int32)
    live = (slots < live_count).astype(jnp.float32)
    half = jnp.where(cd_first == cd_second, jnp.float32(0.5), jnp.float32(1.0))
    weight = half * live
    packed = (both * weight[None, :]).astype(jnp.bfloat16)
    return ladder(packed, pair_values, n_ab, n_cd)


def solution(mesh):
    placed = (P("ab", "cd"), P("ab", "cd", None), P("cd"), P("cd"), P("cd"))
    return jax.shard_map(
        functools.partial(on_device, mesh.shape["ab"], mesh.shape["cd"]),
        mesh=mesh, in_specs=placed, out_specs=P(None, ("ab", "cd")), check_vma=False,
    )
```

```python
import functools

import jax
import jax.numpy as jnp
from jax import lax
from jax.experimental import pallas as pl
from jax.experimental.pallas import tpu as pltpu
from jax.sharding import PartitionSpec as P

MESH = pl.DeviceIdType.MESH
X_CHIPS = 4


def exchange_kernel(n_cd, chunks_ref, out_ref, landed, send_sem, recv_sem, own_sem):
    me_ab = lax.axis_index("ab")
    me_cd = lax.axis_index("cd")
    barrier = pltpu.get_barrier_semaphore()
    for k in range(1, n_cd):
        peer = lax.rem(me_cd + k, n_cd)
        pl.semaphore_signal(barrier, inc=1, device_id=(me_ab, peer), device_id_type=MESH)
    pl.semaphore_wait(barrier, n_cd - 1)
    own = pltpu.make_async_copy(chunks_ref.at[me_cd], landed.at[me_cd], own_sem.at[0])
    own.start()
    for k in range(1, n_cd):
        peer = lax.rem(me_cd + k, n_cd)

        @pl.when(peer < me_cd)
        def _():
            pltpu.make_async_remote_copy(
                src_ref=chunks_ref.at[peer],
                dst_ref=landed.at[me_cd],
                send_sem=send_sem.at[k],
                recv_sem=recv_sem.at[me_cd],
                device_id=(me_ab, peer),
                device_id_type=MESH,
            ).start()

    for k in range(1, n_cd):
        src = lax.rem(me_cd + k, n_cd)

        @pl.when(src < me_cd)
        def _():
            landed[src] = jnp.zeros(landed.shape[1:], landed.dtype)

    own.wait()
    for k in range(1, n_cd):
        src = lax.rem(me_cd + n_cd - k, n_cd)

        @pl.when(src > me_cd)
        def _():
            pltpu.make_async_remote_copy(
                src_ref=chunks_ref.at[src],
                dst_ref=landed.at[src],
                send_sem=send_sem.at[k],
                recv_sem=recv_sem.at[src],
                device_id=(me_ab, src),
                device_id_type=MESH,
            ).wait_recv()

    out_ref[...] = landed[...]
    for k in range(1, n_cd):
        peer = lax.rem(me_cd + k, n_cd)

        @pl.when(peer < me_cd)
        def _():
            pltpu.make_async_remote_copy(
                src_ref=chunks_ref.at[me_cd],
                dst_ref=landed.at[me_cd],
                send_sem=send_sem.at[k],
                recv_sem=recv_sem.at[me_cd],
                device_id=(me_ab, me_cd),
                device_id_type=MESH,
            ).wait_send()


def exchange(chunks, n_cd):
    return pl.pallas_call(
        functools.partial(exchange_kernel, n_cd),
        out_shape=jax.ShapeDtypeStruct(chunks.shape, chunks.dtype),
        in_specs=[pl.BlockSpec(memory_space=pltpu.VMEM)],
        out_specs=pl.BlockSpec(memory_space=pltpu.VMEM),
        scratch_shapes=[
            pltpu.VMEM(chunks.shape, chunks.dtype),
            pltpu.SemaphoreType.DMA((n_cd,)),
            pltpu.SemaphoreType.DMA((n_cd,)),
            pltpu.SemaphoreType.DMA((1,)),
        ],
        compiler_params=pltpu.CompilerParams(collective_id=1, has_side_effects=True),
    )(chunks)


def ladder_kernel(
    n_ab, n_x, n_z, packed_ref, values_hbm, out_ref,
    slots, gathered, values_buf, first_out, first_in, second_out, second_in,
    values_sem, pk_send, pk_recv, first_send, first_recv, second_send, second_recv, own_sem,
):
    me_ab = lax.axis_index("ab")
    me_cd = lax.axis_index("cd")
    me_z = me_cd // n_x
    me_x = lax.rem(me_cd, n_x)
    rows = packed_ref.shape[0]
    block = values_buf.shape[1]

    order = []
    for k in list(range(1, n_x)) + [0]:
        for z in range(n_z):
            order.append(z * n_x + lax.rem(me_x + k, n_x))
    for step, owner in enumerate(order):
        pltpu.make_async_copy(
            values_hbm.at[pl.ds(pl.multiple_of(owner * block, block), block), :],
            values_buf.at[step],
            values_sem.at[step],
        ).start()

    barrier = pltpu.get_barrier_semaphore()
    for k in range(1, n_ab):
        peer = lax.rem(me_ab + k, n_ab)
        pl.semaphore_signal(barrier, inc=1, device_id=(peer, me_cd), device_id_type=MESH)
    for k in range(1, n_x):
        peer = me_z * n_x + lax.rem(me_x + k, n_x)
        pl.semaphore_signal(barrier, inc=1, device_id=(me_ab, peer), device_id_type=MESH)
    for j in range(1, n_z):
        peer = lax.rem(me_z + j, n_z) * n_x + me_x
        pl.semaphore_signal(barrier, inc=1, device_id=(me_ab, peer), device_id_type=MESH)
    pl.semaphore_wait(barrier, (n_ab - 1) + (n_x - 1) + (n_z - 1))

    own = pltpu.make_async_copy(packed_ref, slots.at[me_ab], own_sem.at[0])
    own.start()
    for k in range(1, n_ab):
        peer = lax.rem(me_ab + k, n_ab)
        pltpu.make_async_remote_copy(
            src_ref=packed_ref,
            dst_ref=slots.at[me_ab],
            send_sem=pk_send.at[k],
            recv_sem=pk_recv.at[me_ab],
            device_id=(peer, me_cd),
            device_id_type=MESH,
        ).start()
    own.wait()
    for k in range(1, n_ab):
        src = lax.rem(me_ab + n_ab - k, n_ab)
        pltpu.make_async_remote_copy(
            src_ref=packed_ref,
            dst_ref=slots.at[src],
            send_sem=pk_send.at[k],
            recv_sem=pk_recv.at[src],
            device_id=(src, me_cd),
            device_id_type=MESH,
        ).wait_recv()
    for k in range(n_ab):
        gathered[k * rows:(k + 1) * rows, :] = slots[k].astype(jnp.float32)
    lhs = gathered[...].astype(jnp.bfloat16)

    def one_block(step):
        pltpu.make_async_copy(
            values_hbm.at[pl.ds(0, block), :], values_buf.at[step], values_sem.at[step]
        ).wait()
        return lax.dot_general(
            lhs, values_buf[step], (((1,), (1,)), ((), ())), preferred_element_type=jnp.float32
        )

    for k in range(1, n_x):
        peer = me_z * n_x + lax.rem(me_x + k, n_x)
        for z in range(n_z):
            first_out[k - 1, z] = one_block((k - 1) * n_z + z)
        pltpu.make_async_remote_copy(
            src_ref=first_out.at[k - 1],
            dst_ref=first_in.at[k - 1],
            send_sem=first_send.at[k - 1],
            recv_sem=first_recv.at[k - 1],
            device_id=(me_ab, peer),
            device_id_type=MESH,
        ).start()
    stage = [one_block((n_x - 1) * n_z + z) for z in range(n_z)]
    for k in range(1, n_x):
        src = me_z * n_x + lax.rem(me_x + n_x - k, n_x)
        pltpu.make_async_remote_copy(
            src_ref=first_out.at[k - 1],
            dst_ref=first_in.at[k - 1],
            send_sem=first_send.at[k - 1],
            recv_sem=first_recv.at[k - 1],
            device_id=(me_ab, src),
            device_id_type=MESH,
        ).wait_recv()
        stage = [stage[z] + first_in[k - 1, z] for z in range(n_z)]

    for j in range(1, n_z):
        dest_z = lax.rem(me_z + j, n_z)
        peer = dest_z * n_x + me_x
        picked = stage[0]
        for z in range(1, n_z):
            picked = jnp.where(dest_z == z, stage[z], picked)
        second_out[j - 1] = picked
        pltpu.make_async_remote_copy(
            src_ref=second_out.at[j - 1],
            dst_ref=second_in.at[j - 1],
            send_sem=second_send.at[j - 1],
            recv_sem=second_recv.at[j - 1],
            device_id=(me_ab, peer),
            device_id_type=MESH,
        ).start()
    total = stage[0]
    for z in range(1, n_z):
        total = jnp.where(me_z == z, stage[z], total)
    for j in range(1, n_z):
        src = lax.rem(me_z + n_z - j, n_z) * n_x + me_x
        pltpu.make_async_remote_copy(
            src_ref=second_out.at[j - 1],
            dst_ref=second_in.at[j - 1],
            send_sem=second_send.at[j - 1],
            recv_sem=second_recv.at[j - 1],
            device_id=(me_ab, src),
            device_id_type=MESH,
        ).wait_recv()
        total = total + second_in[j - 1]
    out_ref[...] = total.astype(out_ref.dtype)

    for k in range(1, n_ab):
        pltpu.make_async_remote_copy(
            src_ref=packed_ref,
            dst_ref=slots.at[me_ab],
            send_sem=pk_send.at[k],
            recv_sem=pk_recv.at[me_ab],
            device_id=(me_ab, me_cd),
            device_id_type=MESH,
        ).wait_send()
    for k in range(1, n_x):
        pltpu.make_async_remote_copy(
            src_ref=first_out.at[k - 1],
            dst_ref=first_in.at[k - 1],
            send_sem=first_send.at[k - 1],
            recv_sem=first_recv.at[k - 1],
            device_id=(me_ab, me_cd),
            device_id_type=MESH,
        ).wait_send()
    for j in range(1, n_z):
        pltpu.make_async_remote_copy(
            src_ref=second_out.at[j - 1],
            dst_ref=second_in.at[j - 1],
            send_sem=second_send.at[j - 1],
            recv_sem=second_recv.at[j - 1],
            device_id=(me_ab, me_cd),
            device_id_type=MESH,
        ).wait_send()


def ladder(packed, pair_values, n_ab, n_cd):
    rows, columns = packed.shape
    ab_dev = pair_values.shape[0]
    block = ab_dev // n_cd
    n_x = X_CHIPS
    n_z = n_cd // n_x
    width = rows * n_ab
    return pl.pallas_call(
        functools.partial(ladder_kernel, n_ab, n_x, n_z),
        out_shape=jax.ShapeDtypeStruct((width, block), jnp.bfloat16),
        in_specs=[pl.BlockSpec(memory_space=pltpu.VMEM), pl.BlockSpec(memory_space=pl.ANY)],
        out_specs=pl.BlockSpec(memory_space=pltpu.VMEM),
        scratch_shapes=[
            pltpu.VMEM((n_ab, rows, columns), packed.dtype),
            pltpu.VMEM((width, columns), jnp.float32),
            pltpu.VMEM((n_cd, block, columns), pair_values.dtype),
            pltpu.VMEM((n_x - 1, n_z, width, block), jnp.float32),
            pltpu.VMEM((n_x - 1, n_z, width, block), jnp.float32),
            pltpu.VMEM((n_z - 1, width, block), jnp.float32),
            pltpu.VMEM((n_z - 1, width, block), jnp.float32),
            pltpu.SemaphoreType.DMA((n_cd,)),
            pltpu.SemaphoreType.DMA((n_ab,)),
            pltpu.SemaphoreType.DMA((n_ab,)),
            pltpu.SemaphoreType.DMA((n_x - 1,)),
            pltpu.SemaphoreType.DMA((n_x - 1,)),
            pltpu.SemaphoreType.DMA((n_z - 1,)),
            pltpu.SemaphoreType.DMA((n_z - 1,)),
            pltpu.SemaphoreType.DMA((1,)),
        ],
        compiler_params=pltpu.CompilerParams(
            collective_id=0, has_side_effects=True, vmem_limit_bytes=48 * 1024 * 1024
        ),
    )(packed, pair_values)


def on_device(n_ab, n_cd, pair_values, amplitudes, cd_first, cd_second, live_cols):
    slab = lax.axis_index("cd")
    orbit_block = amplitudes.shape[1]
    orbitals = amplitudes.shape[2]
    columns = cd_first.shape[0]
    local_first = cd_first - slab * orbit_block
    pair_block = amplitudes.shape[0]
    piece = pair_block * orbit_block * orbit_block
    padded = -(-piece // 1024) * 1024
    rows_first = jnp.transpose(amplitudes, (1, 0, 2)).reshape(orbit_block, pair_block, n_cd, orbit_block)
    chunks = jnp.transpose(rows_first, (2, 0, 1, 3)).reshape(n_cd, piece)
    chunks = jnp.pad(chunks, ((0, 0), (0, padded - piece)))
    landed = exchange(chunks.reshape(n_cd, padded // 128, 128), n_cd)
    mirrored = landed.reshape(n_cd, padded)[:, :piece].reshape(n_cd, orbit_block, pair_block, orbit_block)
    mirrored = jnp.transpose(mirrored, (2, 3, 0, 1)).reshape(pair_block, orbit_block, orbitals)
    stacked = jnp.concatenate([amplitudes, mirrored], axis=2)
    pick_d = (lax.broadcasted_iota(jnp.int32, (orbitals, columns), 0) == cd_second[None, :]).astype(
        amplitudes.dtype
    )
    pick_twice = jnp.concatenate([pick_d, pick_d], axis=0)
    both_rows = lax.dot_general(
        stacked, pick_twice, (((2,), (0,)), ((), ())), preferred_element_type=jnp.float32
    )
    pick_c = lax.broadcasted_iota(jnp.int32, (orbit_block, columns), 0) == local_first[None, :]
    both = jnp.sum(jnp.where(pick_c[None], both_rows, 0.0), axis=1)
    live_count = live_cols[0]
    slots = jnp.arange(columns, dtype=jnp.int32)
    live = (slots < live_count).astype(jnp.float32)
    half = jnp.where(cd_first == cd_second, jnp.float32(0.5), jnp.float32(1.0))
    weight = half * live
    packed = (both * weight[None, :]).astype(jnp.bfloat16)
    return ladder(packed, pair_values, n_ab, n_cd)


def solution(mesh):
    placed = (P("ab", "cd"), P("ab", "cd", None), P("cd"), P("cd"), P("cd"))
    return jax.shard_map(
        functools.partial(on_device, mesh.shape["ab"], mesh.shape["cd"]),
        mesh=mesh, in_specs=placed, out_specs=P(None, ("ab", "cd")), check_vma=False,
    )
```

```python
import functools

import jax
import jax.numpy as jnp
from jax import lax
from jax.experimental import pallas as pl
from jax.experimental.pallas import tpu as pltpu
from jax.sharding import PartitionSpec as P

MESH = pl.DeviceIdType.MESH
X_CHIPS = 4


def exchange_kernel(n_cd, chunks_ref, out_ref, landed, send_sem, recv_sem, own_sem):
    me_ab = lax.axis_index("ab")
    me_cd = lax.axis_index("cd")
    barrier = pltpu.get_barrier_semaphore()
    for k in range(1, n_cd):
        peer = lax.rem(me_cd + k, n_cd)
        pl.semaphore_signal(barrier, inc=1, device_id=(me_ab, peer), device_id_type=MESH)
    pl.semaphore_wait(barrier, n_cd - 1)
    own = pltpu.make_async_copy(chunks_ref.at[me_cd], landed.at[me_cd], own_sem.at[0])
    own.start()
    for k in range(1, n_cd):
        peer = lax.rem(me_cd + k, n_cd)

        @pl.when(peer < me_cd)
        def _():
            pltpu.make_async_remote_copy(
                src_ref=chunks_ref.at[peer],
                dst_ref=landed.at[me_cd],
                send_sem=send_sem.at[k],
                recv_sem=recv_sem.at[me_cd],
                device_id=(me_ab, peer),
                device_id_type=MESH,
            ).start()

    for k in range(1, n_cd):
        src = lax.rem(me_cd + k, n_cd)

        @pl.when(src < me_cd)
        def _():
            landed[src] = jnp.zeros(landed.shape[1:], landed.dtype)

    own.wait()
    for k in range(1, n_cd):
        src = lax.rem(me_cd + n_cd - k, n_cd)

        @pl.when(src > me_cd)
        def _():
            pltpu.make_async_remote_copy(
                src_ref=chunks_ref.at[src],
                dst_ref=landed.at[src],
                send_sem=send_sem.at[k],
                recv_sem=recv_sem.at[src],
                device_id=(me_ab, src),
                device_id_type=MESH,
            ).wait_recv()

    out_ref[...] = landed[...]
    for k in range(1, n_cd):
        peer = lax.rem(me_cd + k, n_cd)

        @pl.when(peer < me_cd)
        def _():
            pltpu.make_async_remote_copy(
                src_ref=chunks_ref.at[me_cd],
                dst_ref=landed.at[me_cd],
                send_sem=send_sem.at[k],
                recv_sem=recv_sem.at[me_cd],
                device_id=(me_ab, me_cd),
                device_id_type=MESH,
            ).wait_send()


def exchange(chunks, n_cd):
    return pl.pallas_call(
        functools.partial(exchange_kernel, n_cd),
        out_shape=jax.ShapeDtypeStruct(chunks.shape, chunks.dtype),
        in_specs=[pl.BlockSpec(memory_space=pltpu.VMEM)],
        out_specs=pl.BlockSpec(memory_space=pltpu.VMEM),
        scratch_shapes=[
            pltpu.VMEM(chunks.shape, chunks.dtype),
            pltpu.SemaphoreType.DMA((n_cd,)),
            pltpu.SemaphoreType.DMA((n_cd,)),
            pltpu.SemaphoreType.DMA((1,)),
        ],
        compiler_params=pltpu.CompilerParams(collective_id=1, has_side_effects=True),
    )(chunks)


def ladder_kernel(
    n_ab, n_x, n_z, packed_ref, values_hbm, out_ref,
    slots, gathered, values_buf, first_out, first_in, second_out, second_in,
    values_sem, pk_send, pk_recv, first_send, first_recv, second_send, second_recv, own_sem,
):
    me_ab = lax.axis_index("ab")
    me_cd = lax.axis_index("cd")
    me_z = me_cd // n_x
    me_x = lax.rem(me_cd, n_x)
    rows = packed_ref.shape[0]
    block = values_buf.shape[1]

    z_order = [lax.rem(me_z + j, n_z) for j in list(range(1, n_z)) + [0]]
    order = []
    for z in z_order:
        for k in list(range(1, n_x)) + [0]:
            order.append(z * n_x + lax.rem(me_x + k, n_x))
    for step, owner in enumerate(order):
        pltpu.make_async_copy(
            values_hbm.at[pl.ds(pl.multiple_of(owner * block, block), block), :],
            values_buf.at[step],
            values_sem.at[step],
        ).start()

    barrier = pltpu.get_barrier_semaphore()
    for k in range(1, n_ab):
        peer = lax.rem(me_ab + k, n_ab)
        pl.semaphore_signal(barrier, inc=1, device_id=(peer, me_cd), device_id_type=MESH)
    for k in range(1, n_x):
        peer = me_z * n_x + lax.rem(me_x + k, n_x)
        pl.semaphore_signal(barrier, inc=1, device_id=(me_ab, peer), device_id_type=MESH)
    for j in range(1, n_z):
        peer = lax.rem(me_z + j, n_z) * n_x + me_x
        pl.semaphore_signal(barrier, inc=1, device_id=(me_ab, peer), device_id_type=MESH)
    pl.semaphore_wait(barrier, (n_ab - 1) + (n_x - 1) + (n_z - 1))

    own = pltpu.make_async_copy(packed_ref, slots.at[me_ab], own_sem.at[0])
    own.start()
    for k in range(1, n_ab):
        peer = lax.rem(me_ab + k, n_ab)
        pltpu.make_async_remote_copy(
            src_ref=packed_ref,
            dst_ref=slots.at[me_ab],
            send_sem=pk_send.at[k],
            recv_sem=pk_recv.at[me_ab],
            device_id=(peer, me_cd),
            device_id_type=MESH,
        ).start()
    own.wait()
    for k in range(1, n_ab):
        src = lax.rem(me_ab + n_ab - k, n_ab)
        pltpu.make_async_remote_copy(
            src_ref=packed_ref,
            dst_ref=slots.at[src],
            send_sem=pk_send.at[k],
            recv_sem=pk_recv.at[src],
            device_id=(src, me_cd),
            device_id_type=MESH,
        ).wait_recv()
    for k in range(n_ab):
        gathered[k * rows:(k + 1) * rows, :] = slots[k].astype(jnp.float32)
    lhs = gathered[...].astype(jnp.bfloat16)

    def one_block(step):
        pltpu.make_async_copy(
            values_hbm.at[pl.ds(0, block), :], values_buf.at[step], values_sem.at[step]
        ).wait()
        return lax.dot_general(
            lhs, values_buf[step], (((1,), (1,)), ((), ())), preferred_element_type=jnp.float32
        )

    def first_copy(j, k, peer):
        slot = j * (n_x - 1) + (k - 1)
        return pltpu.make_async_remote_copy(
            src_ref=first_out.at[slot],
            dst_ref=first_in.at[slot],
            send_sem=first_send.at[slot],
            recv_sem=first_recv.at[slot],
            device_id=(me_ab, peer),
            device_id_type=MESH,
        )

    def second_copy(j, peer):
        return pltpu.make_async_remote_copy(
            src_ref=second_out.at[j],
            dst_ref=second_in.at[j],
            send_sem=second_send.at[j],
            recv_sem=second_recv.at[j],
            device_id=(me_ab, peer),
            device_id_type=MESH,
        )

    own = []
    for j in range(n_z):
        for k in range(1, n_x):
            first_out[j * (n_x - 1) + (k - 1)] = one_block(j * n_x + (k - 1))
            first_copy(j, k, me_z * n_x + lax.rem(me_x + k, n_x)).start()
        own.append(one_block(j * n_x + (n_x - 1)))

    total = None
    for j in range(n_z):
        summed = own[j]
        for k in range(1, n_x):
            first_copy(j, k, me_z * n_x + lax.rem(me_x + n_x - k, n_x)).wait_recv()
            summed = summed + first_in[j * (n_x - 1) + (k - 1)]
        if j < n_z - 1:
            second_out[j] = summed
            second_copy(j, z_order[j] * n_x + me_x).start()
        else:
            total = summed
    for j in range(n_z - 1):
        second_copy(j, lax.rem(me_z + n_z - 1 - j, n_z) * n_x + me_x).wait_recv()
        total = total + second_in[j]
    out_ref[...] = total.astype(out_ref.dtype)

    for k in range(1, n_ab):
        pltpu.make_async_remote_copy(
            src_ref=packed_ref,
            dst_ref=slots.at[me_ab],
            send_sem=pk_send.at[k],
            recv_sem=pk_recv.at[me_ab],
            device_id=(me_ab, me_cd),
            device_id_type=MESH,
        ).wait_send()
    for j in range(n_z):
        for k in range(1, n_x):
            first_copy(j, k, me_cd).wait_send()
    for j in range(n_z - 1):
        second_copy(j, me_cd).wait_send()


def ladder(packed, pair_values, n_ab, n_cd):
    rows, columns = packed.shape
    ab_dev = pair_values.shape[0]
    block = ab_dev // n_cd
    n_x = X_CHIPS
    n_z = n_cd // n_x
    width = rows * n_ab
    return pl.pallas_call(
        functools.partial(ladder_kernel, n_ab, n_x, n_z),
        out_shape=jax.ShapeDtypeStruct((width, block), jnp.bfloat16),
        in_specs=[pl.BlockSpec(memory_space=pltpu.VMEM), pl.BlockSpec(memory_space=pl.ANY)],
        out_specs=pl.BlockSpec(memory_space=pltpu.VMEM),
        scratch_shapes=[
            pltpu.VMEM((n_ab, rows, columns), packed.dtype),
            pltpu.VMEM((width, columns), jnp.float32),
            pltpu.VMEM((n_cd, block, columns), pair_values.dtype),
            pltpu.VMEM((n_z * (n_x - 1), width, block), jnp.float32),
            pltpu.VMEM((n_z * (n_x - 1), width, block), jnp.float32),
            pltpu.VMEM((n_z - 1, width, block), jnp.float32),
            pltpu.VMEM((n_z - 1, width, block), jnp.float32),
            pltpu.SemaphoreType.DMA((n_cd,)),
            pltpu.SemaphoreType.DMA((n_ab,)),
            pltpu.SemaphoreType.DMA((n_ab,)),
            pltpu.SemaphoreType.DMA((n_z * (n_x - 1),)),
            pltpu.SemaphoreType.DMA((n_z * (n_x - 1),)),
            pltpu.SemaphoreType.DMA((n_z - 1,)),
            pltpu.SemaphoreType.DMA((n_z - 1,)),
            pltpu.SemaphoreType.DMA((1,)),
        ],
        compiler_params=pltpu.CompilerParams(
            collective_id=0, has_side_effects=True, vmem_limit_bytes=48 * 1024 * 1024
        ),
    )(packed, pair_values)


def on_device(n_ab, n_cd, pair_values, amplitudes, cd_first, cd_second, live_cols):
    slab = lax.axis_index("cd")
    orbit_block = amplitudes.shape[1]
    orbitals = amplitudes.shape[2]
    columns = cd_first.shape[0]
    local_first = cd_first - slab * orbit_block
    pair_block = amplitudes.shape[0]
    piece = pair_block * orbit_block * orbit_block
    padded = -(-piece // 1024) * 1024
    chunks = jnp.transpose(amplitudes.reshape(pair_block, orbit_block, n_cd, orbit_block), (2, 0, 1, 3))
    chunks = jnp.pad(chunks.reshape(n_cd, piece), ((0, 0), (0, padded - piece)))
    landed = exchange(chunks.reshape(n_cd, padded // 128, 128), n_cd)
    mirrored = landed.reshape(n_cd, padded)[:, :piece].reshape(n_cd, pair_block, orbit_block, orbit_block)
    pick_d = (lax.broadcasted_iota(jnp.int32, (orbitals, columns), 0) == cd_second[None, :]).astype(
        amplitudes.dtype
    )
    direct_rows = lax.dot_general(
        amplitudes, pick_d, (((2,), (0,)), ((), ())), preferred_element_type=jnp.float32
    )
    crossed_rows = lax.dot_general(
        mirrored,
        pick_d.reshape(n_cd, orbit_block, columns),
        (((0, 2), (0, 1)), ((), ())),
        preferred_element_type=jnp.float32,
    )
    pick_c = lax.broadcasted_iota(jnp.int32, (orbit_block, columns), 0) == local_first[None, :]
    both = jnp.sum(jnp.where(pick_c[None], direct_rows + crossed_rows, 0.0), axis=1)
    live_count = live_cols[0]
    slots = jnp.arange(columns, dtype=jnp.int32)
    live = (slots < live_count).astype(jnp.float32)
    half = jnp.where(cd_first == cd_second, jnp.float32(0.5), jnp.float32(1.0))
    weight = half * live
    packed = (both * weight[None, :]).astype(jnp.bfloat16)
    return ladder(packed, pair_values, n_ab, n_cd)


def solution(mesh):
    placed = (P("ab", "cd"), P("ab", "cd", None), P("cd"), P("cd"), P("cd"))
    return jax.shard_map(
        functools.partial(on_device, mesh.shape["ab"], mesh.shape["cd"]),
        mesh=mesh, in_specs=placed, out_specs=P(None, ("ab", "cd")), check_vma=False,
    )
```

```python
import functools

import jax
import jax.numpy as jnp
from jax import lax
from jax.experimental import pallas as pl
from jax.experimental.pallas import tpu as pltpu
from jax.sharding import PartitionSpec as P

MESH = pl.DeviceIdType.MESH
X_CHIPS = 4


def exchange_kernel(n_cd, chunks_ref, out_ref, landed, send_sem, recv_sem, own_sem):
    me_ab = lax.axis_index("ab")
    me_cd = lax.axis_index("cd")
    barrier = pltpu.get_barrier_semaphore()
    for k in range(1, n_cd):
        peer = lax.rem(me_cd + k, n_cd)
        pl.semaphore_signal(barrier, inc=1, device_id=(me_ab, peer), device_id_type=MESH)
    pl.semaphore_wait(barrier, n_cd - 1)
    own = pltpu.make_async_copy(chunks_ref.at[me_cd], landed.at[me_cd], own_sem.at[0])
    own.start()
    for k in range(1, n_cd):
        peer = lax.rem(me_cd + k, n_cd)

        @pl.when(peer < me_cd)
        def _():
            pltpu.make_async_remote_copy(
                src_ref=chunks_ref.at[peer],
                dst_ref=landed.at[me_cd],
                send_sem=send_sem.at[k],
                recv_sem=recv_sem.at[me_cd],
                device_id=(me_ab, peer),
                device_id_type=MESH,
            ).start()

    for k in range(1, n_cd):
        src = lax.rem(me_cd + k, n_cd)

        @pl.when(src < me_cd)
        def _():
            landed[src] = jnp.zeros(landed.shape[1:], landed.dtype)

    own.wait()
    for k in range(1, n_cd):
        src = lax.rem(me_cd + n_cd - k, n_cd)

        @pl.when(src > me_cd)
        def _():
            pltpu.make_async_remote_copy(
                src_ref=chunks_ref.at[src],
                dst_ref=landed.at[src],
                send_sem=send_sem.at[k],
                recv_sem=recv_sem.at[src],
                device_id=(me_ab, src),
                device_id_type=MESH,
            ).wait_recv()

    out_ref[...] = landed[...]
    for k in range(1, n_cd):
        peer = lax.rem(me_cd + k, n_cd)

        @pl.when(peer < me_cd)
        def _():
            pltpu.make_async_remote_copy(
                src_ref=chunks_ref.at[me_cd],
                dst_ref=landed.at[me_cd],
                send_sem=send_sem.at[k],
                recv_sem=recv_sem.at[me_cd],
                device_id=(me_ab, me_cd),
                device_id_type=MESH,
            ).wait_send()


def exchange(chunks, n_cd):
    return pl.pallas_call(
        functools.partial(exchange_kernel, n_cd),
        out_shape=jax.ShapeDtypeStruct(chunks.shape, chunks.dtype),
        in_specs=[pl.BlockSpec(memory_space=pltpu.VMEM)],
        out_specs=pl.BlockSpec(memory_space=pltpu.VMEM),
        scratch_shapes=[
            pltpu.VMEM(chunks.shape, chunks.dtype),
            pltpu.SemaphoreType.DMA((n_cd,)),
            pltpu.SemaphoreType.DMA((n_cd,)),
            pltpu.SemaphoreType.DMA((1,)),
        ],
        compiler_params=pltpu.CompilerParams(collective_id=1, has_side_effects=True),
    )(chunks)


def ladder_kernel(
    n_ab, n_x, n_z, packed_ref, values_hbm, out_ref,
    slots, gathered, values_buf, first_out, first_in, second_out, second_in,
    values_sem, pk_send, pk_recv, first_send, first_recv, second_send, second_recv, own_sem,
):
    me_ab = lax.axis_index("ab")
    me_cd = lax.axis_index("cd")
    me_z = me_cd // n_x
    me_x = lax.rem(me_cd, n_x)
    rows = packed_ref.shape[0]
    block = values_buf.shape[1]

    z_order = [lax.rem(me_z + j, n_z) for j in list(range(1, n_z)) + [0]]
    order = []
    for z in z_order:
        for k in list(range(1, n_x)) + [0]:
            order.append(z * n_x + lax.rem(me_x + k, n_x))
    for step, owner in enumerate(order):
        pltpu.make_async_copy(
            values_hbm.at[pl.ds(pl.multiple_of(owner * block, block), block), :],
            values_buf.at[step],
            values_sem.at[step],
        ).start()

    barrier = pltpu.get_barrier_semaphore()
    for k in range(1, n_ab):
        peer = lax.rem(me_ab + k, n_ab)
        pl.semaphore_signal(barrier, inc=1, device_id=(peer, me_cd), device_id_type=MESH)
    for k in range(1, n_x):
        peer = me_z * n_x + lax.rem(me_x + k, n_x)
        pl.semaphore_signal(barrier, inc=1, device_id=(me_ab, peer), device_id_type=MESH)
    for j in range(1, n_z):
        peer = lax.rem(me_z + j, n_z) * n_x + me_x
        pl.semaphore_signal(barrier, inc=1, device_id=(me_ab, peer), device_id_type=MESH)
    pl.semaphore_wait(barrier, (n_ab - 1) + (n_x - 1) + (n_z - 1))

    own = pltpu.make_async_copy(packed_ref, slots.at[me_ab], own_sem.at[0])
    own.start()
    for k in range(1, n_ab):
        peer = lax.rem(me_ab + k, n_ab)
        pltpu.make_async_remote_copy(
            src_ref=packed_ref,
            dst_ref=slots.at[me_ab],
            send_sem=pk_send.at[k],
            recv_sem=pk_recv.at[me_ab],
            device_id=(peer, me_cd),
            device_id_type=MESH,
        ).start()
    own.wait()
    for k in range(1, n_ab):
        src = lax.rem(me_ab + n_ab - k, n_ab)
        pltpu.make_async_remote_copy(
            src_ref=packed_ref,
            dst_ref=slots.at[src],
            send_sem=pk_send.at[k],
            recv_sem=pk_recv.at[src],
            device_id=(src, me_cd),
            device_id_type=MESH,
        ).wait_recv()
    for k in range(n_ab):
        gathered[k * rows:(k + 1) * rows, :] = slots[k].astype(jnp.float32)
    lhs = gathered[...].astype(jnp.bfloat16)

    def one_block(step):
        pltpu.make_async_copy(
            values_hbm.at[pl.ds(0, block), :], values_buf.at[step], values_sem.at[step]
        ).wait()
        return lax.dot_general(
            lhs, values_buf[step], (((1,), (1,)), ((), ())), preferred_element_type=jnp.float32
        )

    def first_copy(j, k, peer):
        slot = j * (n_x - 1) + (k - 1)
        return pltpu.make_async_remote_copy(
            src_ref=first_out.at[slot],
            dst_ref=first_in.at[slot],
            send_sem=first_send.at[slot],
            recv_sem=first_recv.at[slot],
            device_id=(me_ab, peer),
            device_id_type=MESH,
        )

    def second_copy(j, peer):
        return pltpu.make_async_remote_copy(
            src_ref=second_out.at[j],
            dst_ref=second_in.at[j],
            send_sem=second_send.at[j],
            recv_sem=second_recv.at[j],
            device_id=(me_ab, peer),
            device_id_type=MESH,
        )

    own = []
    for j in range(n_z):
        for k in range(1, n_x):
            first_out[j * (n_x - 1) + (k - 1)] = one_block(j * n_x + (k - 1))
            first_copy(j, k, me_z * n_x + lax.rem(me_x + k, n_x)).start()
        own.append(one_block(j * n_x + (n_x - 1)))

    total = None
    for j in range(n_z):
        summed = own[j]
        for k in range(1, n_x):
            first_copy(j, k, me_z * n_x + lax.rem(me_x + n_x - k, n_x)).wait_recv()
            summed = summed + first_in[j * (n_x - 1) + (k - 1)]
        if j < n_z - 1:
            second_out[j] = summed
            second_copy(j, z_order[j] * n_x + me_x).start()
        else:
            total = summed
    for j in range(n_z - 1):
        second_copy(j, lax.rem(me_z + n_z - 1 - j, n_z) * n_x + me_x).wait_recv()
        total = total + second_in[j]
    out_ref[...] = total.astype(out_ref.dtype)

    for k in range(1, n_ab):
        pltpu.make_async_remote_copy(
            src_ref=packed_ref,
            dst_ref=slots.at[me_ab],
            send_sem=pk_send.at[k],
            recv_sem=pk_recv.at[me_ab],
            device_id=(me_ab, me_cd),
            device_id_type=MESH,
        ).wait_send()
    for j in range(n_z):
        for k in range(1, n_x):
            first_copy(j, k, me_cd).wait_send()
    for j in range(n_z - 1):
        second_copy(j, me_cd).wait_send()


def ladder(packed, pair_values, n_ab, n_cd):
    rows, columns = packed.shape
    ab_dev = pair_values.shape[0]
    block = ab_dev // n_cd
    n_x = X_CHIPS
    n_z = n_cd // n_x
    width = rows * n_ab
    return pl.pallas_call(
        functools.partial(ladder_kernel, n_ab, n_x, n_z),
        out_shape=jax.ShapeDtypeStruct((width, block), jnp.bfloat16),
        in_specs=[pl.BlockSpec(memory_space=pltpu.VMEM), pl.BlockSpec(memory_space=pl.ANY)],
        out_specs=pl.BlockSpec(memory_space=pltpu.VMEM),
        scratch_shapes=[
            pltpu.VMEM((n_ab, rows, columns), packed.dtype),
            pltpu.VMEM((width, columns), jnp.float32),
            pltpu.VMEM((n_cd, block, columns), pair_values.dtype),
            pltpu.VMEM((n_z * (n_x - 1), width, block), jnp.float32),
            pltpu.VMEM((n_z * (n_x - 1), width, block), jnp.float32),
            pltpu.VMEM((n_z - 1, width, block), jnp.float32),
            pltpu.VMEM((n_z - 1, width, block), jnp.float32),
            pltpu.SemaphoreType.DMA((n_cd,)),
            pltpu.SemaphoreType.DMA((n_ab,)),
            pltpu.SemaphoreType.DMA((n_ab,)),
            pltpu.SemaphoreType.DMA((n_z * (n_x - 1),)),
            pltpu.SemaphoreType.DMA((n_z * (n_x - 1),)),
            pltpu.SemaphoreType.DMA((n_z - 1,)),
            pltpu.SemaphoreType.DMA((n_z - 1,)),
            pltpu.SemaphoreType.DMA((1,)),
        ],
        compiler_params=pltpu.CompilerParams(
            collective_id=0, has_side_effects=True, vmem_limit_bytes=48 * 1024 * 1024
        ),
    )(packed, pair_values)


def on_device(n_ab, n_cd, pair_values, amplitudes, cd_first, cd_second, live_cols):
    slab = lax.axis_index("cd")
    orbit_block = amplitudes.shape[1]
    orbitals = amplitudes.shape[2]
    columns = cd_first.shape[0]
    local_first = cd_first - slab * orbit_block
    pair_block = amplitudes.shape[0]
    piece = pair_block * orbit_block * orbit_block
    padded = -(-piece // 1024) * 1024
    rows_first = jnp.transpose(amplitudes, (1, 0, 2)).reshape(orbit_block, pair_block, n_cd, orbit_block)
    chunks = jnp.transpose(rows_first, (2, 0, 1, 3)).reshape(n_cd, piece)
    chunks = jnp.pad(chunks, ((0, 0), (0, padded - piece)))
    landed = exchange(chunks.reshape(n_cd, padded // 128, 128), n_cd)
    mirrored = landed.reshape(n_cd, padded)[:, :piece].reshape(n_cd, orbit_block, pair_block, orbit_block)
    pick_d = (lax.broadcasted_iota(jnp.int32, (orbitals, columns), 0) == cd_second[None, :]).astype(
        amplitudes.dtype
    )
    direct_rows = lax.dot_general(
        amplitudes, pick_d, (((2,), (0,)), ((), ())), preferred_element_type=jnp.float32
    )
    crossed_rows = lax.dot_general(
        mirrored,
        pick_d.reshape(n_cd, orbit_block, columns),
        (((0, 1), (0, 1)), ((), ())),
        preferred_element_type=jnp.float32,
    )
    pick_c = lax.broadcasted_iota(jnp.int32, (orbit_block, columns), 0) == local_first[None, :]
    both = jnp.sum(jnp.where(pick_c[None], direct_rows + crossed_rows, 0.0), axis=1)
    live_count = live_cols[0]
    slots = jnp.arange(columns, dtype=jnp.int32)
    live = (slots < live_count).astype(jnp.float32)
    half = jnp.where(cd_first == cd_second, jnp.float32(0.5), jnp.float32(1.0))
    weight = half * live
    packed = (both * weight[None, :]).astype(jnp.bfloat16)
    return ladder(packed, pair_values, n_ab, n_cd)


def solution(mesh):
    placed = (P("ab", "cd"), P("ab", "cd", None), P("cd"), P("cd"), P("cd"))
    return jax.shard_map(
        functools.partial(on_device, mesh.shape["ab"], mesh.shape["cd"]),
        mesh=mesh, in_specs=placed, out_specs=P(None, ("ab", "cd")), check_vma=False,
    )
```

```python
import functools

import jax
import jax.numpy as jnp
from jax import lax
from jax.experimental import pallas as pl
from jax.experimental.pallas import tpu as pltpu
from jax.sharding import PartitionSpec as P

MESH = pl.DeviceIdType.MESH
X_CHIPS = 4


def exchange_kernel(
    n_cd, chunks_ref, amp_ref, second_ref, first_ref, out_ref, direct_ref, landed, send_sem, recv_sem, own_sem
):
    me_ab = lax.axis_index("ab")
    me_cd = lax.axis_index("cd")
    barrier = pltpu.get_barrier_semaphore()
    for k in range(1, n_cd):
        peer = lax.rem(me_cd + k, n_cd)
        pl.semaphore_signal(barrier, inc=1, device_id=(me_ab, peer), device_id_type=MESH)
    pl.semaphore_wait(barrier, n_cd - 1)
    own = pltpu.make_async_copy(chunks_ref.at[me_cd], landed.at[me_cd], own_sem.at[0])
    own.start()
    for k in range(1, n_cd):
        peer = lax.rem(me_cd + k, n_cd)

        @pl.when(peer < me_cd)
        def _():
            pltpu.make_async_remote_copy(
                src_ref=chunks_ref.at[peer],
                dst_ref=landed.at[me_cd],
                send_sem=send_sem.at[k],
                recv_sem=recv_sem.at[me_cd],
                device_id=(me_ab, peer),
                device_id_type=MESH,
            ).start()

    for k in range(1, n_cd):
        src = lax.rem(me_cd + k, n_cd)

        @pl.when(src < me_cd)
        def _():
            landed[src] = jnp.zeros(landed.shape[1:], landed.dtype)

    orbitals, columns = amp_ref.shape[2], second_ref.shape[1]
    pick_d = (lax.broadcasted_iota(jnp.int32, (orbitals, columns), 0) == second_ref[...]).astype(amp_ref.dtype)
    pick_c = lax.broadcasted_iota(jnp.int32, (amp_ref.shape[1], columns), 0) == first_ref[...]
    for ij in range(amp_ref.shape[0]):
        rows = jnp.dot(amp_ref[ij], pick_d, preferred_element_type=jnp.float32)
        direct_ref[ij:ij + 1, :] = jnp.sum(jnp.where(pick_c, rows, 0.0), axis=0, keepdims=True)

    own.wait()
    for k in range(1, n_cd):
        src = lax.rem(me_cd + n_cd - k, n_cd)

        @pl.when(src > me_cd)
        def _():
            pltpu.make_async_remote_copy(
                src_ref=chunks_ref.at[src],
                dst_ref=landed.at[src],
                send_sem=send_sem.at[k],
                recv_sem=recv_sem.at[src],
                device_id=(me_ab, src),
                device_id_type=MESH,
            ).wait_recv()

    out_ref[...] = landed[...]
    for k in range(1, n_cd):
        peer = lax.rem(me_cd + k, n_cd)

        @pl.when(peer < me_cd)
        def _():
            pltpu.make_async_remote_copy(
                src_ref=chunks_ref.at[me_cd],
                dst_ref=landed.at[me_cd],
                send_sem=send_sem.at[k],
                recv_sem=recv_sem.at[me_cd],
                device_id=(me_ab, me_cd),
                device_id_type=MESH,
            ).wait_send()


def exchange(chunks, amplitudes, second, local_first, n_cd):
    pair_block, columns = amplitudes.shape[0], second.shape[0]
    return pl.pallas_call(
        functools.partial(exchange_kernel, n_cd),
        out_shape=(
            jax.ShapeDtypeStruct(chunks.shape, chunks.dtype),
            jax.ShapeDtypeStruct((pair_block, columns), jnp.float32),
        ),
        in_specs=[pl.BlockSpec(memory_space=pltpu.VMEM)] * 4,
        out_specs=(pl.BlockSpec(memory_space=pltpu.VMEM), pl.BlockSpec(memory_space=pltpu.VMEM)),
        scratch_shapes=[
            pltpu.VMEM(chunks.shape, chunks.dtype),
            pltpu.SemaphoreType.DMA((n_cd,)),
            pltpu.SemaphoreType.DMA((n_cd,)),
            pltpu.SemaphoreType.DMA((1,)),
        ],
        compiler_params=pltpu.CompilerParams(collective_id=1, has_side_effects=True),
    )(chunks, amplitudes, second.reshape(1, columns), local_first.reshape(1, columns))


def ladder_kernel(
    n_ab, n_x, n_z, packed_ref, values_hbm, out_ref,
    slots, gathered, values_buf, first_out, first_in, second_out, second_in,
    values_sem, pk_send, pk_recv, first_send, first_recv, second_send, second_recv, own_sem,
):
    me_ab = lax.axis_index("ab")
    me_cd = lax.axis_index("cd")
    me_z = me_cd // n_x
    me_x = lax.rem(me_cd, n_x)
    rows = packed_ref.shape[0]
    block = values_buf.shape[1]

    z_order = [lax.rem(me_z + j, n_z) for j in list(range(1, n_z)) + [0]]
    order = []
    for z in z_order:
        for k in list(range(1, n_x)) + [0]:
            order.append(z * n_x + lax.rem(me_x + k, n_x))
    for step, owner in enumerate(order):
        pltpu.make_async_copy(
            values_hbm.at[pl.ds(pl.multiple_of(owner * block, block), block), :],
            values_buf.at[step],
            values_sem.at[step],
        ).start()

    barrier = pltpu.get_barrier_semaphore()
    for k in range(1, n_ab):
        peer = lax.rem(me_ab + k, n_ab)
        pl.semaphore_signal(barrier, inc=1, device_id=(peer, me_cd), device_id_type=MESH)
    for k in range(1, n_x):
        peer = me_z * n_x + lax.rem(me_x + k, n_x)
        pl.semaphore_signal(barrier, inc=1, device_id=(me_ab, peer), device_id_type=MESH)
    for j in range(1, n_z):
        peer = lax.rem(me_z + j, n_z) * n_x + me_x
        pl.semaphore_signal(barrier, inc=1, device_id=(me_ab, peer), device_id_type=MESH)
    pl.semaphore_wait(barrier, (n_ab - 1) + (n_x - 1) + (n_z - 1))

    own = pltpu.make_async_copy(packed_ref, slots.at[me_ab], own_sem.at[0])
    own.start()
    for k in range(1, n_ab):
        peer = lax.rem(me_ab + k, n_ab)
        pltpu.make_async_remote_copy(
            src_ref=packed_ref,
            dst_ref=slots.at[me_ab],
            send_sem=pk_send.at[k],
            recv_sem=pk_recv.at[me_ab],
            device_id=(peer, me_cd),
            device_id_type=MESH,
        ).start()
    own.wait()
    for k in range(1, n_ab):
        src = lax.rem(me_ab + n_ab - k, n_ab)
        pltpu.make_async_remote_copy(
            src_ref=packed_ref,
            dst_ref=slots.at[src],
            send_sem=pk_send.at[k],
            recv_sem=pk_recv.at[src],
            device_id=(src, me_cd),
            device_id_type=MESH,
        ).wait_recv()
    for k in range(n_ab):
        gathered[k * rows:(k + 1) * rows, :] = slots[k].astype(jnp.float32)
    lhs = gathered[...].astype(jnp.bfloat16)

    def one_block(step):
        pltpu.make_async_copy(
            values_hbm.at[pl.ds(0, block), :], values_buf.at[step], values_sem.at[step]
        ).wait()
        return lax.dot_general(
            lhs, values_buf[step], (((1,), (1,)), ((), ())), preferred_element_type=jnp.float32
        )

    def first_copy(j, k, peer):
        slot = j * (n_x - 1) + (k - 1)
        return pltpu.make_async_remote_copy(
            src_ref=first_out.at[slot],
            dst_ref=first_in.at[slot],
            send_sem=first_send.at[slot],
            recv_sem=first_recv.at[slot],
            device_id=(me_ab, peer),
            device_id_type=MESH,
        )

    def second_copy(j, peer):
        return pltpu.make_async_remote_copy(
            src_ref=second_out.at[j],
            dst_ref=second_in.at[j],
            send_sem=second_send.at[j],
            recv_sem=second_recv.at[j],
            device_id=(me_ab, peer),
            device_id_type=MESH,
        )

    own = []
    for j in range(n_z):
        for k in range(1, n_x):
            first_out[j * (n_x - 1) + (k - 1)] = one_block(j * n_x + (k - 1))
            first_copy(j, k, me_z * n_x + lax.rem(me_x + k, n_x)).start()
        own.append(one_block(j * n_x + (n_x - 1)))

    total = None
    for j in range(n_z):
        summed = own[j]
        for k in range(1, n_x):
            first_copy(j, k, me_z * n_x + lax.rem(me_x + n_x - k, n_x)).wait_recv()
            summed = summed + first_in[j * (n_x - 1) + (k - 1)]
        if j < n_z - 1:
            second_out[j] = summed
            second_copy(j, z_order[j] * n_x + me_x).start()
        else:
            total = summed
    for j in range(n_z - 1):
        second_copy(j, lax.rem(me_z + n_z - 1 - j, n_z) * n_x + me_x).wait_recv()
        total = total + second_in[j]
    out_ref[...] = total.astype(out_ref.dtype)

    for k in range(1, n_ab):
        pltpu.make_async_remote_copy(
            src_ref=packed_ref,
            dst_ref=slots.at[me_ab],
            send_sem=pk_send.at[k],
            recv_sem=pk_recv.at[me_ab],
            device_id=(me_ab, me_cd),
            device_id_type=MESH,
        ).wait_send()
    for j in range(n_z):
        for k in range(1, n_x):
            first_copy(j, k, me_cd).wait_send()
    for j in range(n_z - 1):
        second_copy(j, me_cd).wait_send()


def ladder(packed, pair_values, n_ab, n_cd):
    rows, columns = packed.shape
    ab_dev = pair_values.shape[0]
    block = ab_dev // n_cd
    n_x = X_CHIPS
    n_z = n_cd // n_x
    width = rows * n_ab
    return pl.pallas_call(
        functools.partial(ladder_kernel, n_ab, n_x, n_z),
        out_shape=jax.ShapeDtypeStruct((width, block), jnp.bfloat16),
        in_specs=[pl.BlockSpec(memory_space=pltpu.VMEM), pl.BlockSpec(memory_space=pl.ANY)],
        out_specs=pl.BlockSpec(memory_space=pltpu.VMEM),
        scratch_shapes=[
            pltpu.VMEM((n_ab, rows, columns), packed.dtype),
            pltpu.VMEM((width, columns), jnp.float32),
            pltpu.VMEM((n_cd, block, columns), pair_values.dtype),
            pltpu.VMEM((n_z * (n_x - 1), width, block), jnp.float32),
            pltpu.VMEM((n_z * (n_x - 1), width, block), jnp.float32),
            pltpu.VMEM((n_z - 1, width, block), jnp.float32),
            pltpu.VMEM((n_z - 1, width, block), jnp.float32),
            pltpu.SemaphoreType.DMA((n_cd,)),
            pltpu.SemaphoreType.DMA((n_ab,)),
            pltpu.SemaphoreType.DMA((n_ab,)),
            pltpu.SemaphoreType.DMA((n_z * (n_x - 1),)),
            pltpu.SemaphoreType.DMA((n_z * (n_x - 1),)),
            pltpu.SemaphoreType.DMA((n_z - 1,)),
            pltpu.SemaphoreType.DMA((n_z - 1,)),
            pltpu.SemaphoreType.DMA((1,)),
        ],
        compiler_params=pltpu.CompilerParams(
            collective_id=0, has_side_effects=True, vmem_limit_bytes=48 * 1024 * 1024
        ),
    )(packed, pair_values)


def on_device(n_ab, n_cd, pair_values, amplitudes, cd_first, cd_second, live_cols):
    slab = lax.axis_index("cd")
    orbit_block = amplitudes.shape[1]
    orbitals = amplitudes.shape[2]
    columns = cd_first.shape[0]
    local_first = cd_first - slab * orbit_block
    pair_block = amplitudes.shape[0]
    piece = pair_block * orbit_block * orbit_block
    padded = -(-piece // 1024) * 1024
    rows_first = jnp.transpose(amplitudes, (1, 0, 2)).reshape(orbit_block, pair_block, n_cd, orbit_block)
    chunks = jnp.transpose(rows_first, (2, 0, 1, 3)).reshape(n_cd, piece)
    chunks = jnp.pad(chunks, ((0, 0), (0, padded - piece)))
    landed, direct = exchange(chunks.reshape(n_cd, padded // 128, 128), amplitudes, cd_second, local_first, n_cd)
    mirrored = landed.reshape(n_cd, padded)[:, :piece].reshape(n_cd, orbit_block, pair_block, orbit_block)
    pick_d = (lax.broadcasted_iota(jnp.int32, (orbitals, columns), 0) == cd_second[None, :]).astype(
        amplitudes.dtype
    )
    crossed_rows = lax.dot_general(
        mirrored,
        pick_d.reshape(n_cd, orbit_block, columns),
        (((0, 1), (0, 1)), ((), ())),
        preferred_element_type=jnp.float32,
    )
    pick_c = lax.broadcasted_iota(jnp.int32, (orbit_block, columns), 0) == local_first[None, :]
    both = direct + jnp.sum(jnp.where(pick_c[None], crossed_rows, 0.0), axis=1)
    live_count = live_cols[0]
    slots = jnp.arange(columns, dtype=jnp.int32)
    live = (slots < live_count).astype(jnp.float32)
    half = jnp.where(cd_first == cd_second, jnp.float32(0.5), jnp.float32(1.0))
    weight = half * live
    packed = (both * weight[None, :]).astype(jnp.bfloat16)
    return ladder(packed, pair_values, n_ab, n_cd)


def solution(mesh):
    placed = (P("ab", "cd"), P("ab", "cd", None), P("cd"), P("cd"), P("cd"))
    return jax.shard_map(
        functools.partial(on_device, mesh.shape["ab"], mesh.shape["cd"]),
        mesh=mesh, in_specs=placed, out_specs=P(None, ("ab", "cd")), check_vma=False,
    )
```

```python
import functools

import jax
import jax.numpy as jnp
from jax import lax
from jax.experimental import pallas as pl
from jax.experimental.pallas import tpu as pltpu
from jax.sharding import PartitionSpec as P

MESH = pl.DeviceIdType.MESH
X_CHIPS = 4


def exchange_kernel(
    n_cd, chunks_ref, amp_ref, second_ref, first_ref, out_ref, direct_ref, landed, send_sem, recv_sem, own_sem
):
    me_ab = lax.axis_index("ab")
    me_cd = lax.axis_index("cd")
    barrier = pltpu.get_barrier_semaphore()
    for k in range(1, n_cd):
        peer = lax.rem(me_cd + k, n_cd)
        pl.semaphore_signal(barrier, inc=1, device_id=(me_ab, peer), device_id_type=MESH)
    pl.semaphore_wait(barrier, n_cd - 1)
    own = pltpu.make_async_copy(chunks_ref.at[me_cd], landed.at[me_cd], own_sem.at[0])
    own.start()
    for k in range(1, n_cd):
        peer = lax.rem(me_cd + k, n_cd)

        @pl.when(peer < me_cd)
        def _():
            pltpu.make_async_remote_copy(
                src_ref=chunks_ref.at[peer],
                dst_ref=landed.at[me_cd],
                send_sem=send_sem.at[k],
                recv_sem=recv_sem.at[me_cd],
                device_id=(me_ab, peer),
                device_id_type=MESH,
            ).start()

    for k in range(1, n_cd):
        src = lax.rem(me_cd + k, n_cd)

        @pl.when(src < me_cd)
        def _():
            landed[src] = jnp.zeros(landed.shape[1:], landed.dtype)

    orbitals, columns = amp_ref.shape[2], second_ref.shape[1]
    pick_d = (lax.broadcasted_iota(jnp.int32, (orbitals, columns), 0) == second_ref[...]).astype(amp_ref.dtype)
    local = first_ref[...] - me_cd * amp_ref.shape[1]
    pick_c = lax.broadcasted_iota(jnp.int32, (amp_ref.shape[1], columns), 0) == local
    for ij in range(amp_ref.shape[0]):
        rows = jnp.dot(amp_ref[ij], pick_d, preferred_element_type=jnp.float32)
        direct_ref[ij:ij + 1, :] = jnp.sum(jnp.where(pick_c, rows, 0.0), axis=0, keepdims=True)

    own.wait()
    for k in range(1, n_cd):
        src = lax.rem(me_cd + n_cd - k, n_cd)

        @pl.when(src > me_cd)
        def _():
            pltpu.make_async_remote_copy(
                src_ref=chunks_ref.at[src],
                dst_ref=landed.at[src],
                send_sem=send_sem.at[k],
                recv_sem=recv_sem.at[src],
                device_id=(me_ab, src),
                device_id_type=MESH,
            ).wait_recv()

    out_ref[...] = landed[...]
    for k in range(1, n_cd):
        peer = lax.rem(me_cd + k, n_cd)

        @pl.when(peer < me_cd)
        def _():
            pltpu.make_async_remote_copy(
                src_ref=chunks_ref.at[me_cd],
                dst_ref=landed.at[me_cd],
                send_sem=send_sem.at[k],
                recv_sem=recv_sem.at[me_cd],
                device_id=(me_ab, me_cd),
                device_id_type=MESH,
            ).wait_send()


def exchange(chunks, amplitudes, second, first, n_cd):
    pair_block, columns = amplitudes.shape[0], second.shape[0]
    return pl.pallas_call(
        functools.partial(exchange_kernel, n_cd),
        out_shape=(
            jax.ShapeDtypeStruct(chunks.shape, chunks.dtype),
            jax.ShapeDtypeStruct((pair_block, columns), jnp.float32),
        ),
        in_specs=[pl.BlockSpec(memory_space=pltpu.VMEM)] * 4,
        out_specs=(pl.BlockSpec(memory_space=pltpu.VMEM), pl.BlockSpec(memory_space=pltpu.VMEM)),
        scratch_shapes=[
            pltpu.VMEM(chunks.shape, chunks.dtype),
            pltpu.SemaphoreType.DMA((n_cd,)),
            pltpu.SemaphoreType.DMA((n_cd,)),
            pltpu.SemaphoreType.DMA((1,)),
        ],
        compiler_params=pltpu.CompilerParams(collective_id=1, has_side_effects=True),
    )(chunks, amplitudes, second.reshape(1, columns), first.reshape(1, columns))


def ladder_kernel(
    n_ab, n_x, n_z, packed_ref, values_hbm, out_ref,
    slots, gathered, values_buf, first_out, first_in, second_out, second_in,
    values_sem, pk_send, pk_recv, first_send, first_recv, second_send, second_recv, own_sem,
):
    me_ab = lax.axis_index("ab")
    me_cd = lax.axis_index("cd")
    me_z = me_cd // n_x
    me_x = lax.rem(me_cd, n_x)
    rows = packed_ref.shape[0]
    block = values_buf.shape[1]

    z_order = [lax.rem(me_z + j, n_z) for j in list(range(1, n_z)) + [0]]
    order = []
    for z in z_order:
        for k in list(range(1, n_x)) + [0]:
            order.append(z * n_x + lax.rem(me_x + k, n_x))
    for step, owner in enumerate(order):
        pltpu.make_async_copy(
            values_hbm.at[pl.ds(pl.multiple_of(owner * block, block), block), :],
            values_buf.at[step],
            values_sem.at[step],
        ).start()

    barrier = pltpu.get_barrier_semaphore()
    for k in range(1, n_ab):
        peer = lax.rem(me_ab + k, n_ab)
        pl.semaphore_signal(barrier, inc=1, device_id=(peer, me_cd), device_id_type=MESH)
    for k in range(1, n_x):
        peer = me_z * n_x + lax.rem(me_x + k, n_x)
        pl.semaphore_signal(barrier, inc=1, device_id=(me_ab, peer), device_id_type=MESH)
    for j in range(1, n_z):
        peer = lax.rem(me_z + j, n_z) * n_x + me_x
        pl.semaphore_signal(barrier, inc=1, device_id=(me_ab, peer), device_id_type=MESH)
    pl.semaphore_wait(barrier, (n_ab - 1) + (n_x - 1) + (n_z - 1))

    own = pltpu.make_async_copy(packed_ref, slots.at[me_ab], own_sem.at[0])
    own.start()
    for k in range(1, n_ab):
        peer = lax.rem(me_ab + k, n_ab)
        pltpu.make_async_remote_copy(
            src_ref=packed_ref,
            dst_ref=slots.at[me_ab],
            send_sem=pk_send.at[k],
            recv_sem=pk_recv.at[me_ab],
            device_id=(peer, me_cd),
            device_id_type=MESH,
        ).start()
    own.wait()
    for k in range(1, n_ab):
        src = lax.rem(me_ab + n_ab - k, n_ab)
        pltpu.make_async_remote_copy(
            src_ref=packed_ref,
            dst_ref=slots.at[src],
            send_sem=pk_send.at[k],
            recv_sem=pk_recv.at[src],
            device_id=(src, me_cd),
            device_id_type=MESH,
        ).wait_recv()
    for k in range(n_ab):
        gathered[k * rows:(k + 1) * rows, :] = slots[k].astype(jnp.float32)
    lhs = gathered[...].astype(jnp.bfloat16)

    def one_block(step):
        pltpu.make_async_copy(
            values_hbm.at[pl.ds(0, block), :], values_buf.at[step], values_sem.at[step]
        ).wait()
        return lax.dot_general(
            lhs, values_buf[step], (((1,), (1,)), ((), ())), preferred_element_type=jnp.float32
        )

    def first_copy(j, k, peer):
        slot = j * (n_x - 1) + (k - 1)
        return pltpu.make_async_remote_copy(
            src_ref=first_out.at[slot],
            dst_ref=first_in.at[slot],
            send_sem=first_send.at[slot],
            recv_sem=first_recv.at[slot],
            device_id=(me_ab, peer),
            device_id_type=MESH,
        )

    def second_copy(j, peer):
        return pltpu.make_async_remote_copy(
            src_ref=second_out.at[j],
            dst_ref=second_in.at[j],
            send_sem=second_send.at[j],
            recv_sem=second_recv.at[j],
            device_id=(me_ab, peer),
            device_id_type=MESH,
        )

    own = []
    for j in range(n_z):
        for k in range(1, n_x):
            first_out[j * (n_x - 1) + (k - 1)] = one_block(j * n_x + (k - 1))
            first_copy(j, k, me_z * n_x + lax.rem(me_x + k, n_x)).start()
        own.append(one_block(j * n_x + (n_x - 1)))

    total = None
    for j in range(n_z):
        summed = own[j]
        for k in range(1, n_x):
            first_copy(j, k, me_z * n_x + lax.rem(me_x + n_x - k, n_x)).wait_recv()
            summed = summed + first_in[j * (n_x - 1) + (k - 1)]
        if j < n_z - 1:
            second_out[j] = summed
            second_copy(j, z_order[j] * n_x + me_x).start()
        else:
            total = summed
    for j in range(n_z - 1):
        second_copy(j, lax.rem(me_z + n_z - 1 - j, n_z) * n_x + me_x).wait_recv()
        total = total + second_in[j]
    out_ref[...] = total.astype(out_ref.dtype)

    for k in range(1, n_ab):
        pltpu.make_async_remote_copy(
            src_ref=packed_ref,
            dst_ref=slots.at[me_ab],
            send_sem=pk_send.at[k],
            recv_sem=pk_recv.at[me_ab],
            device_id=(me_ab, me_cd),
            device_id_type=MESH,
        ).wait_send()
    for j in range(n_z):
        for k in range(1, n_x):
            first_copy(j, k, me_cd).wait_send()
    for j in range(n_z - 1):
        second_copy(j, me_cd).wait_send()


def ladder(packed, pair_values, n_ab, n_cd):
    rows, columns = packed.shape
    ab_dev = pair_values.shape[0]
    block = ab_dev // n_cd
    n_x = X_CHIPS
    n_z = n_cd // n_x
    width = rows * n_ab
    return pl.pallas_call(
        functools.partial(ladder_kernel, n_ab, n_x, n_z),
        out_shape=jax.ShapeDtypeStruct((width, block), jnp.bfloat16),
        in_specs=[pl.BlockSpec(memory_space=pltpu.VMEM), pl.BlockSpec(memory_space=pl.ANY)],
        out_specs=pl.BlockSpec(memory_space=pltpu.VMEM),
        scratch_shapes=[
            pltpu.VMEM((n_ab, rows, columns), packed.dtype),
            pltpu.VMEM((width, columns), jnp.float32),
            pltpu.VMEM((n_cd, block, columns), pair_values.dtype),
            pltpu.VMEM((n_z * (n_x - 1), width, block), jnp.float32),
            pltpu.VMEM((n_z * (n_x - 1), width, block), jnp.float32),
            pltpu.VMEM((n_z - 1, width, block), jnp.float32),
            pltpu.VMEM((n_z - 1, width, block), jnp.float32),
            pltpu.SemaphoreType.DMA((n_cd,)),
            pltpu.SemaphoreType.DMA((n_ab,)),
            pltpu.SemaphoreType.DMA((n_ab,)),
            pltpu.SemaphoreType.DMA((n_z * (n_x - 1),)),
            pltpu.SemaphoreType.DMA((n_z * (n_x - 1),)),
            pltpu.SemaphoreType.DMA((n_z - 1,)),
            pltpu.SemaphoreType.DMA((n_z - 1,)),
            pltpu.SemaphoreType.DMA((1,)),
        ],
        compiler_params=pltpu.CompilerParams(
            collective_id=0, has_side_effects=True, vmem_limit_bytes=48 * 1024 * 1024
        ),
    )(packed, pair_values)


def on_device(n_ab, n_cd, pair_values, amplitudes, cd_first, cd_second, live_cols):
    slab = lax.axis_index("cd")
    orbit_block = amplitudes.shape[1]
    orbitals = amplitudes.shape[2]
    columns = cd_first.shape[0]
    local_first = cd_first - slab * orbit_block
    pair_block = amplitudes.shape[0]
    piece = pair_block * orbit_block * orbit_block
    padded = -(-piece // 1024) * 1024
    rows_first = jnp.transpose(amplitudes, (1, 0, 2)).reshape(orbit_block, pair_block, n_cd, orbit_block)
    chunks = jnp.transpose(rows_first, (2, 0, 1, 3)).reshape(n_cd, piece)
    chunks = jnp.pad(chunks, ((0, 0), (0, padded - piece)))
    landed, direct = exchange(chunks.reshape(n_cd, padded // 128, 128), amplitudes, cd_second, cd_first, n_cd)
    mirrored = landed.reshape(n_cd, padded)[:, :piece].reshape(n_cd, orbit_block, pair_block, orbit_block)
    pick_d = (lax.broadcasted_iota(jnp.int32, (orbitals, columns), 0) == cd_second[None, :]).astype(
        amplitudes.dtype
    )
    crossed_rows = lax.dot_general(
        mirrored,
        pick_d.reshape(n_cd, orbit_block, columns),
        (((0, 1), (0, 1)), ((), ())),
        preferred_element_type=jnp.float32,
    )
    pick_c = lax.broadcasted_iota(jnp.int32, (orbit_block, columns), 0) == local_first[None, :]
    both = direct + jnp.sum(jnp.where(pick_c[None], crossed_rows, 0.0), axis=1)
    live_count = live_cols[0]
    slots = jnp.arange(columns, dtype=jnp.int32)
    live = (slots < live_count).astype(jnp.float32)
    half = jnp.where(cd_first == cd_second, jnp.float32(0.5), jnp.float32(1.0))
    weight = half * live
    packed = (both * weight[None, :]).astype(jnp.bfloat16)
    return ladder(packed, pair_values, n_ab, n_cd)


def solution(mesh):
    placed = (P("ab", "cd"), P("ab", "cd", None), P("cd"), P("cd"), P("cd"))
    return jax.shard_map(
        functools.partial(on_device, mesh.shape["ab"], mesh.shape["cd"]),
        mesh=mesh, in_specs=placed, out_specs=P(None, ("ab", "cd")), check_vma=False,
    )
```

```python
import functools

import jax
import jax.numpy as jnp
from jax import lax
from jax.experimental import pallas as pl
from jax.experimental.pallas import tpu as pltpu
from jax.sharding import PartitionSpec as P

MESH = pl.DeviceIdType.MESH
X_CHIPS = 4


def exchange_kernel(
    n_cd, chunks_ref, amp_ref, second_ref, first_ref, out_ref, direct_ref, landed, send_sem, recv_sem, own_sem
):
    me_ab = lax.axis_index("ab")
    me_cd = lax.axis_index("cd")
    barrier = pltpu.get_barrier_semaphore()
    for k in range(1, n_cd):
        peer = lax.rem(me_cd + k, n_cd)
        pl.semaphore_signal(barrier, inc=1, device_id=(me_ab, peer), device_id_type=MESH)
    pl.semaphore_wait(barrier, n_cd - 1)
    own = pltpu.make_async_copy(chunks_ref.at[me_cd], landed.at[me_cd], own_sem.at[0])
    own.start()
    for k in range(1, n_cd):
        peer = lax.rem(me_cd + k, n_cd)

        @pl.when(peer < me_cd)
        def _():
            pltpu.make_async_remote_copy(
                src_ref=chunks_ref.at[peer],
                dst_ref=landed.at[me_cd],
                send_sem=send_sem.at[k],
                recv_sem=recv_sem.at[me_cd],
                device_id=(me_ab, peer),
                device_id_type=MESH,
            ).start()

    for k in range(1, n_cd):
        src = lax.rem(me_cd + k, n_cd)

        @pl.when(src < me_cd)
        def _():
            landed[src] = jnp.zeros(landed.shape[1:], landed.dtype)

    orbitals, columns = amp_ref.shape[2], second_ref.shape[1]
    pick_d = (lax.broadcasted_iota(jnp.int32, (orbitals, columns), 0) == second_ref[...]).astype(amp_ref.dtype)
    local = first_ref[...] - me_cd * amp_ref.shape[1]
    pick_c = lax.broadcasted_iota(jnp.int32, (amp_ref.shape[1], columns), 0) == local
    for ij in range(amp_ref.shape[0]):
        rows = jnp.dot(amp_ref[ij], pick_d, preferred_element_type=jnp.float32)
        direct_ref[ij:ij + 1, :] = jnp.sum(jnp.where(pick_c, rows, 0.0), axis=0, keepdims=True)

    own.wait()
    for k in range(1, n_cd):
        src = lax.rem(me_cd + n_cd - k, n_cd)

        @pl.when(src > me_cd)
        def _():
            pltpu.make_async_remote_copy(
                src_ref=chunks_ref.at[src],
                dst_ref=landed.at[src],
                send_sem=send_sem.at[k],
                recv_sem=recv_sem.at[src],
                device_id=(me_ab, src),
                device_id_type=MESH,
            ).wait_recv()

    out_ref[...] = landed[...]
    for k in range(1, n_cd):
        peer = lax.rem(me_cd + k, n_cd)

        @pl.when(peer < me_cd)
        def _():
            pltpu.make_async_remote_copy(
                src_ref=chunks_ref.at[me_cd],
                dst_ref=landed.at[me_cd],
                send_sem=send_sem.at[k],
                recv_sem=recv_sem.at[me_cd],
                device_id=(me_ab, me_cd),
                device_id_type=MESH,
            ).wait_send()


def exchange(chunks, amplitudes, second, first, n_cd):
    pair_block, columns = amplitudes.shape[0], second.shape[0]
    return pl.pallas_call(
        functools.partial(exchange_kernel, n_cd),
        out_shape=(
            jax.ShapeDtypeStruct(chunks.shape, chunks.dtype),
            jax.ShapeDtypeStruct((pair_block, columns), jnp.float32),
        ),
        in_specs=[pl.BlockSpec(memory_space=pltpu.VMEM)] * 4,
        out_specs=(pl.BlockSpec(memory_space=pltpu.VMEM), pl.BlockSpec(memory_space=pltpu.VMEM)),
        scratch_shapes=[
            pltpu.VMEM(chunks.shape, chunks.dtype),
            pltpu.SemaphoreType.DMA((n_cd,)),
            pltpu.SemaphoreType.DMA((n_cd,)),
            pltpu.SemaphoreType.DMA((1,)),
        ],
        compiler_params=pltpu.CompilerParams(collective_id=1, has_side_effects=True),
    )(chunks, amplitudes, second.reshape(1, columns), first.reshape(1, columns))


def far_first(n):
    offsets = list(range(1, n))
    if n % 2 == 0 and n > 2:
        offsets.remove(n // 2)
        offsets.insert(0, n // 2)
    return offsets


def ladder_kernel(
    n_ab, n_x, n_z, packed_ref, values_hbm, out_ref,
    slots, gathered, values_buf, first_out, first_in, second_out, second_in,
    values_sem, pk_send, pk_recv, first_send, first_recv, second_send, second_recv, own_sem,
):
    me_ab = lax.axis_index("ab")
    me_cd = lax.axis_index("cd")
    me_z = me_cd // n_x
    me_x = lax.rem(me_cd, n_x)
    rows = packed_ref.shape[0]
    block = values_buf.shape[1]

    z_offsets = far_first(n_z)
    x_offsets = far_first(n_x)
    z_order = [lax.rem(me_z + o, n_z) for o in z_offsets] + [me_z]
    order = []
    for z in z_order:
        for k in x_offsets + [0]:
            order.append(z * n_x + lax.rem(me_x + k, n_x))
    for step, owner in enumerate(order):
        pltpu.make_async_copy(
            values_hbm.at[pl.ds(pl.multiple_of(owner * block, block), block), :],
            values_buf.at[step],
            values_sem.at[step],
        ).start()

    barrier = pltpu.get_barrier_semaphore()
    for k in range(1, n_ab):
        peer = lax.rem(me_ab + k, n_ab)
        pl.semaphore_signal(barrier, inc=1, device_id=(peer, me_cd), device_id_type=MESH)
    for k in range(1, n_x):
        peer = me_z * n_x + lax.rem(me_x + k, n_x)
        pl.semaphore_signal(barrier, inc=1, device_id=(me_ab, peer), device_id_type=MESH)
    for j in range(1, n_z):
        peer = lax.rem(me_z + j, n_z) * n_x + me_x
        pl.semaphore_signal(barrier, inc=1, device_id=(me_ab, peer), device_id_type=MESH)
    pl.semaphore_wait(barrier, (n_ab - 1) + (n_x - 1) + (n_z - 1))

    own = pltpu.make_async_copy(packed_ref, slots.at[me_ab], own_sem.at[0])
    own.start()
    for k in range(1, n_ab):
        peer = lax.rem(me_ab + k, n_ab)
        pltpu.make_async_remote_copy(
            src_ref=packed_ref,
            dst_ref=slots.at[me_ab],
            send_sem=pk_send.at[k],
            recv_sem=pk_recv.at[me_ab],
            device_id=(peer, me_cd),
            device_id_type=MESH,
        ).start()
    own.wait()
    for k in range(1, n_ab):
        src = lax.rem(me_ab + n_ab - k, n_ab)
        pltpu.make_async_remote_copy(
            src_ref=packed_ref,
            dst_ref=slots.at[src],
            send_sem=pk_send.at[k],
            recv_sem=pk_recv.at[src],
            device_id=(src, me_cd),
            device_id_type=MESH,
        ).wait_recv()
    for k in range(n_ab):
        gathered[k * rows:(k + 1) * rows, :] = slots[k].astype(jnp.float32)
    lhs = gathered[...].astype(jnp.bfloat16)

    def one_block(step):
        pltpu.make_async_copy(
            values_hbm.at[pl.ds(0, block), :], values_buf.at[step], values_sem.at[step]
        ).wait()
        return lax.dot_general(
            lhs, values_buf[step], (((1,), (1,)), ((), ())), preferred_element_type=jnp.float32
        )

    def first_copy(j, k, peer):
        slot = j * (n_x - 1) + (k - 1)
        return pltpu.make_async_remote_copy(
            src_ref=first_out.at[slot],
            dst_ref=first_in.at[slot],
            send_sem=first_send.at[slot],
            recv_sem=first_recv.at[slot],
            device_id=(me_ab, peer),
            device_id_type=MESH,
        )

    def second_copy(j, peer):
        return pltpu.make_async_remote_copy(
            src_ref=second_out.at[j],
            dst_ref=second_in.at[j],
            send_sem=second_send.at[j],
            recv_sem=second_recv.at[j],
            device_id=(me_ab, peer),
            device_id_type=MESH,
        )

    own = []
    for j in range(n_z):
        for position, k in enumerate(x_offsets):
            first_out[j * (n_x - 1) + (k - 1)] = one_block(j * n_x + position)
            first_copy(j, k, me_z * n_x + lax.rem(me_x + k, n_x)).start()
        own.append(one_block(j * n_x + (n_x - 1)))

    total = None
    for j in range(n_z):
        summed = own[j]
        for k in range(1, n_x):
            first_copy(j, k, me_z * n_x + lax.rem(me_x + n_x - k, n_x)).wait_recv()
            summed = summed + first_in[j * (n_x - 1) + (k - 1)]
        if j < n_z - 1:
            second_out[j] = summed
            second_copy(j, z_order[j] * n_x + me_x).start()
        else:
            total = summed
    for j in range(n_z - 1):
        second_copy(j, lax.rem(me_z + n_z - z_offsets[j], n_z) * n_x + me_x).wait_recv()
        total = total + second_in[j]
    out_ref[...] = total.astype(out_ref.dtype)

    for k in range(1, n_ab):
        pltpu.make_async_remote_copy(
            src_ref=packed_ref,
            dst_ref=slots.at[me_ab],
            send_sem=pk_send.at[k],
            recv_sem=pk_recv.at[me_ab],
            device_id=(me_ab, me_cd),
            device_id_type=MESH,
        ).wait_send()
    for j in range(n_z):
        for k in range(1, n_x):
            first_copy(j, k, me_cd).wait_send()
    for j in range(n_z - 1):
        second_copy(j, me_cd).wait_send()


def ladder(packed, pair_values, n_ab, n_cd):
    rows, columns = packed.shape
    ab_dev = pair_values.shape[0]
    block = ab_dev // n_cd
    n_x = X_CHIPS
    n_z = n_cd // n_x
    width = rows * n_ab
    return pl.pallas_call(
        functools.partial(ladder_kernel, n_ab, n_x, n_z),
        out_shape=jax.ShapeDtypeStruct((width, block), jnp.bfloat16),
        in_specs=[pl.BlockSpec(memory_space=pltpu.VMEM), pl.BlockSpec(memory_space=pl.ANY)],
        out_specs=pl.BlockSpec(memory_space=pltpu.VMEM),
        scratch_shapes=[
            pltpu.VMEM((n_ab, rows, columns), packed.dtype),
            pltpu.VMEM((width, columns), jnp.float32),
            pltpu.VMEM((n_cd, block, columns), pair_values.dtype),
            pltpu.VMEM((n_z * (n_x - 1), width, block), jnp.float32),
            pltpu.VMEM((n_z * (n_x - 1), width, block), jnp.float32),
            pltpu.VMEM((n_z - 1, width, block), jnp.float32),
            pltpu.VMEM((n_z - 1, width, block), jnp.float32),
            pltpu.SemaphoreType.DMA((n_cd,)),
            pltpu.SemaphoreType.DMA((n_ab,)),
            pltpu.SemaphoreType.DMA((n_ab,)),
            pltpu.SemaphoreType.DMA((n_z * (n_x - 1),)),
            pltpu.SemaphoreType.DMA((n_z * (n_x - 1),)),
            pltpu.SemaphoreType.DMA((n_z - 1,)),
            pltpu.SemaphoreType.DMA((n_z - 1,)),
            pltpu.SemaphoreType.DMA((1,)),
        ],
        compiler_params=pltpu.CompilerParams(
            collective_id=0, has_side_effects=True, vmem_limit_bytes=48 * 1024 * 1024
        ),
    )(packed, pair_values)


def on_device(n_ab, n_cd, pair_values, amplitudes, cd_first, cd_second, live_cols):
    slab = lax.axis_index("cd")
    orbit_block = amplitudes.shape[1]
    orbitals = amplitudes.shape[2]
    columns = cd_first.shape[0]
    local_first = cd_first - slab * orbit_block
    pair_block = amplitudes.shape[0]
    piece = pair_block * orbit_block * orbit_block
    padded = -(-piece // 1024) * 1024
    rows_first = jnp.transpose(amplitudes, (1, 0, 2)).reshape(orbit_block, pair_block, n_cd, orbit_block)
    chunks = jnp.transpose(rows_first, (2, 0, 1, 3)).reshape(n_cd, piece)
    chunks = jnp.pad(chunks, ((0, 0), (0, padded - piece)))
    landed, direct = exchange(chunks.reshape(n_cd, padded // 128, 128), amplitudes, cd_second, cd_first, n_cd)
    mirrored = landed.reshape(n_cd, padded)[:, :piece].reshape(n_cd, orbit_block, pair_block, orbit_block)
    pick_d = (lax.broadcasted_iota(jnp.int32, (orbitals, columns), 0) == cd_second[None, :]).astype(
        amplitudes.dtype
    )
    crossed_rows = lax.dot_general(
        mirrored,
        pick_d.reshape(n_cd, orbit_block, columns),
        (((0, 1), (0, 1)), ((), ())),
        preferred_element_type=jnp.float32,
    )
    pick_c = lax.broadcasted_iota(jnp.int32, (orbit_block, columns), 0) == local_first[None, :]
    both = direct + jnp.sum(jnp.where(pick_c[None], crossed_rows, 0.0), axis=1)
    live_count = live_cols[0]
    slots = jnp.arange(columns, dtype=jnp.int32)
    live = (slots < live_count).astype(jnp.float32)
    half = jnp.where(cd_first == cd_second, jnp.float32(0.5), jnp.float32(1.0))
    weight = half * live
    packed = (both * weight[None, :]).astype(jnp.bfloat16)
    return ladder(packed, pair_values, n_ab, n_cd)


def solution(mesh):
    placed = (P("ab", "cd"), P("ab", "cd", None), P("cd"), P("cd"), P("cd"))
    return jax.shard_map(
        functools.partial(on_device, mesh.shape["ab"], mesh.shape["cd"]),
        mesh=mesh, in_specs=placed, out_specs=P(None, ("ab", "cd")), check_vma=False,
    )
```

```python
import functools

import jax
import jax.numpy as jnp
from jax import lax
from jax.experimental import pallas as pl
from jax.experimental.pallas import tpu as pltpu
from jax.sharding import PartitionSpec as P

MESH = pl.DeviceIdType.MESH
X_CHIPS = 4


def exchange_kernel(
    n_cd, chunks_ref, amp_ref, second_ref, first_ref, out_ref, direct_ref, landed, send_sem, recv_sem, own_sem
):
    me_ab = lax.axis_index("ab")
    me_cd = lax.axis_index("cd")
    barrier = pltpu.get_barrier_semaphore()
    for k in range(1, n_cd):
        peer = lax.rem(me_cd + k, n_cd)
        pl.semaphore_signal(barrier, inc=1, device_id=(me_ab, peer), device_id_type=MESH)
    pl.semaphore_wait(barrier, n_cd - 1)
    own = pltpu.make_async_copy(chunks_ref.at[me_cd], landed.at[me_cd], own_sem.at[0])
    own.start()
    for k in range(1, n_cd):
        peer = lax.rem(me_cd + k, n_cd)

        @pl.when(peer < me_cd)
        def _():
            pltpu.make_async_remote_copy(
                src_ref=chunks_ref.at[peer],
                dst_ref=landed.at[me_cd],
                send_sem=send_sem.at[k],
                recv_sem=recv_sem.at[me_cd],
                device_id=(me_ab, peer),
                device_id_type=MESH,
            ).start()

    for k in range(1, n_cd):
        src = lax.rem(me_cd + k, n_cd)

        @pl.when(src < me_cd)
        def _():
            landed[src] = jnp.zeros(landed.shape[1:], landed.dtype)

    orbitals, columns = amp_ref.shape[2], second_ref.shape[1]
    pick_d = (lax.broadcasted_iota(jnp.int32, (orbitals, columns), 0) == second_ref[...]).astype(amp_ref.dtype)
    local = first_ref[...] - me_cd * amp_ref.shape[1]
    pick_c = lax.broadcasted_iota(jnp.int32, (amp_ref.shape[1], columns), 0) == local
    for ij in range(amp_ref.shape[0]):
        rows = jnp.dot(amp_ref[ij], pick_d, preferred_element_type=jnp.float32)
        direct_ref[ij:ij + 1, :] = jnp.sum(jnp.where(pick_c, rows, 0.0), axis=0, keepdims=True)

    own.wait()
    for k in range(1, n_cd):
        src = lax.rem(me_cd + n_cd - k, n_cd)

        @pl.when(src > me_cd)
        def _():
            pltpu.make_async_remote_copy(
                src_ref=chunks_ref.at[src],
                dst_ref=landed.at[src],
                send_sem=send_sem.at[k],
                recv_sem=recv_sem.at[src],
                device_id=(me_ab, src),
                device_id_type=MESH,
            ).wait_recv()

    out_ref[...] = landed[...]
    for k in range(1, n_cd):
        peer = lax.rem(me_cd + k, n_cd)

        @pl.when(peer < me_cd)
        def _():
            pltpu.make_async_remote_copy(
                src_ref=chunks_ref.at[me_cd],
                dst_ref=landed.at[me_cd],
                send_sem=send_sem.at[k],
                recv_sem=recv_sem.at[me_cd],
                device_id=(me_ab, me_cd),
                device_id_type=MESH,
            ).wait_send()


def exchange(chunks, amplitudes, second, first, n_cd):
    pair_block, columns = amplitudes.shape[0], second.shape[0]
    return pl.pallas_call(
        functools.partial(exchange_kernel, n_cd),
        out_shape=(
            jax.ShapeDtypeStruct(chunks.shape, chunks.dtype),
            jax.ShapeDtypeStruct((pair_block, columns), jnp.float32),
        ),
        in_specs=[pl.BlockSpec(memory_space=pltpu.VMEM)] * 4,
        out_specs=(pl.BlockSpec(memory_space=pltpu.VMEM), pl.BlockSpec(memory_space=pltpu.VMEM)),
        scratch_shapes=[
            pltpu.VMEM(chunks.shape, chunks.dtype),
            pltpu.SemaphoreType.DMA((n_cd,)),
            pltpu.SemaphoreType.DMA((n_cd,)),
            pltpu.SemaphoreType.DMA((1,)),
        ],
        compiler_params=pltpu.CompilerParams(collective_id=1, has_side_effects=True),
    )(chunks, amplitudes, second.reshape(1, columns), first.reshape(1, columns))


def ladder_kernel(
    n_ab, n_x, n_z, packed_ref, values_hbm, out_ref,
    slots, gathered, values_buf, first_out, first_in, second_out, second_in,
    values_sem, pk_send, pk_recv, first_send, first_recv, second_send, second_recv, own_sem,
):
    me_ab = lax.axis_index("ab")
    me_cd = lax.axis_index("cd")
    me_z = me_cd // n_x
    me_x = lax.rem(me_cd, n_x)
    rows = packed_ref.shape[0]
    block = values_buf.shape[1]

    z_order = [lax.rem(me_z + j, n_z) for j in list(range(1, n_z)) + [0]]
    order = []
    for z in z_order:
        for k in list(range(1, n_x)) + [0]:
            order.append(z * n_x + lax.rem(me_x + k, n_x))
    barrier = pltpu.get_barrier_semaphore()
    for k in range(1, n_ab):
        peer = lax.rem(me_ab + k, n_ab)
        pl.semaphore_signal(barrier, inc=1, device_id=(peer, me_cd), device_id_type=MESH)
    for k in range(1, n_x):
        peer = me_z * n_x + lax.rem(me_x + k, n_x)
        pl.semaphore_signal(barrier, inc=1, device_id=(me_ab, peer), device_id_type=MESH)
    for j in range(1, n_z):
        peer = lax.rem(me_z + j, n_z) * n_x + me_x
        pl.semaphore_signal(barrier, inc=1, device_id=(me_ab, peer), device_id_type=MESH)
    pl.semaphore_wait(barrier, (n_ab - 1) + (n_x - 1) + (n_z - 1))

    own = pltpu.make_async_copy(packed_ref, slots.at[me_ab], own_sem.at[0])
    own.start()
    for k in range(1, n_ab):
        peer = lax.rem(me_ab + k, n_ab)
        pltpu.make_async_remote_copy(
            src_ref=packed_ref,
            dst_ref=slots.at[me_ab],
            send_sem=pk_send.at[k],
            recv_sem=pk_recv.at[me_ab],
            device_id=(peer, me_cd),
            device_id_type=MESH,
        ).start()
    for step, owner in enumerate(order):
        pltpu.make_async_copy(
            values_hbm.at[pl.ds(pl.multiple_of(owner * block, block), block), :],
            values_buf.at[step],
            values_sem.at[step],
        ).start()
    own.wait()
    for k in range(1, n_ab):
        src = lax.rem(me_ab + n_ab - k, n_ab)
        pltpu.make_async_remote_copy(
            src_ref=packed_ref,
            dst_ref=slots.at[src],
            send_sem=pk_send.at[k],
            recv_sem=pk_recv.at[src],
            device_id=(src, me_cd),
            device_id_type=MESH,
        ).wait_recv()
    for k in range(n_ab):
        gathered[k * rows:(k + 1) * rows, :] = slots[k].astype(jnp.float32)
    lhs = gathered[...].astype(jnp.bfloat16)

    def one_block(step):
        pltpu.make_async_copy(
            values_hbm.at[pl.ds(0, block), :], values_buf.at[step], values_sem.at[step]
        ).wait()
        return lax.dot_general(
            lhs, values_buf[step], (((1,), (1,)), ((), ())), preferred_element_type=jnp.float32
        )

    def first_copy(j, k, peer):
        slot = j * (n_x - 1) + (k - 1)
        return pltpu.make_async_remote_copy(
            src_ref=first_out.at[slot],
            dst_ref=first_in.at[slot],
            send_sem=first_send.at[slot],
            recv_sem=first_recv.at[slot],
            device_id=(me_ab, peer),
            device_id_type=MESH,
        )

    def second_copy(j, peer):
        return pltpu.make_async_remote_copy(
            src_ref=second_out.at[j],
            dst_ref=second_in.at[j],
            send_sem=second_send.at[j],
            recv_sem=second_recv.at[j],
            device_id=(me_ab, peer),
            device_id_type=MESH,
        )

    own = []
    for j in range(n_z):
        for k in range(1, n_x):
            first_out[j * (n_x - 1) + (k - 1)] = one_block(j * n_x + (k - 1))
            first_copy(j, k, me_z * n_x + lax.rem(me_x + k, n_x)).start()
        own.append(one_block(j * n_x + (n_x - 1)))

    total = None
    for j in range(n_z):
        summed = own[j]
        for k in range(1, n_x):
            first_copy(j, k, me_z * n_x + lax.rem(me_x + n_x - k, n_x)).wait_recv()
            summed = summed + first_in[j * (n_x - 1) + (k - 1)]
        if j < n_z - 1:
            second_out[j] = summed
            second_copy(j, z_order[j] * n_x + me_x).start()
        else:
            total = summed
    for j in range(n_z - 1):
        second_copy(j, lax.rem(me_z + n_z - 1 - j, n_z) * n_x + me_x).wait_recv()
        total = total + second_in[j]
    out_ref[...] = total.astype(out_ref.dtype)

    for k in range(1, n_ab):
        pltpu.make_async_remote_copy(
            src_ref=packed_ref,
            dst_ref=slots.at[me_ab],
            send_sem=pk_send.at[k],
            recv_sem=pk_recv.at[me_ab],
            device_id=(me_ab, me_cd),
            device_id_type=MESH,
        ).wait_send()
    for j in range(n_z):
        for k in range(1, n_x):
            first_copy(j, k, me_cd).wait_send()
    for j in range(n_z - 1):
        second_copy(j, me_cd).wait_send()


def ladder(packed, pair_values, n_ab, n_cd):
    rows, columns = packed.shape
    ab_dev = pair_values.shape[0]
    block = ab_dev // n_cd
    n_x = X_CHIPS
    n_z = n_cd // n_x
    width = rows * n_ab
    return pl.pallas_call(
        functools.partial(ladder_kernel, n_ab, n_x, n_z),
        out_shape=jax.ShapeDtypeStruct((width, block), jnp.bfloat16),
        in_specs=[pl.BlockSpec(memory_space=pltpu.VMEM), pl.BlockSpec(memory_space=pl.ANY)],
        out_specs=pl.BlockSpec(memory_space=pltpu.VMEM),
        scratch_shapes=[
            pltpu.VMEM((n_ab, rows, columns), packed.dtype),
            pltpu.VMEM((width, columns), jnp.float32),
            pltpu.VMEM((n_cd, block, columns), pair_values.dtype),
            pltpu.VMEM((n_z * (n_x - 1), width, block), jnp.float32),
            pltpu.VMEM((n_z * (n_x - 1), width, block), jnp.float32),
            pltpu.VMEM((n_z - 1, width, block), jnp.float32),
            pltpu.VMEM((n_z - 1, width, block), jnp.float32),
            pltpu.SemaphoreType.DMA((n_cd,)),
            pltpu.SemaphoreType.DMA((n_ab,)),
            pltpu.SemaphoreType.DMA((n_ab,)),
            pltpu.SemaphoreType.DMA((n_z * (n_x - 1),)),
            pltpu.SemaphoreType.DMA((n_z * (n_x - 1),)),
            pltpu.SemaphoreType.DMA((n_z - 1,)),
            pltpu.SemaphoreType.DMA((n_z - 1,)),
            pltpu.SemaphoreType.DMA((1,)),
        ],
        compiler_params=pltpu.CompilerParams(
            collective_id=0, has_side_effects=True, vmem_limit_bytes=48 * 1024 * 1024
        ),
    )(packed, pair_values)


def on_device(n_ab, n_cd, pair_values, amplitudes, cd_first, cd_second, live_cols):
    slab = lax.axis_index("cd")
    orbit_block = amplitudes.shape[1]
    orbitals = amplitudes.shape[2]
    columns = cd_first.shape[0]
    local_first = cd_first - slab * orbit_block
    pair_block = amplitudes.shape[0]
    piece = pair_block * orbit_block * orbit_block
    padded = -(-piece // 1024) * 1024
    rows_first = jnp.transpose(amplitudes, (1, 0, 2)).reshape(orbit_block, pair_block, n_cd, orbit_block)
    chunks = jnp.transpose(rows_first, (2, 0, 1, 3)).reshape(n_cd, piece)
    chunks = jnp.pad(chunks, ((0, 0), (0, padded - piece)))
    landed, direct = exchange(chunks.reshape(n_cd, padded // 128, 128), amplitudes, cd_second, cd_first, n_cd)
    mirrored = landed.reshape(n_cd, padded)[:, :piece].reshape(n_cd, orbit_block, pair_block, orbit_block)
    pick_d = (lax.broadcasted_iota(jnp.int32, (orbitals, columns), 0) == cd_second[None, :]).astype(
        amplitudes.dtype
    )
    crossed_rows = lax.dot_general(
        mirrored,
        pick_d.reshape(n_cd, orbit_block, columns),
        (((0, 1), (0, 1)), ((), ())),
        preferred_element_type=jnp.float32,
    )
    pick_c = lax.broadcasted_iota(jnp.int32, (orbit_block, columns), 0) == local_first[None, :]
    both = direct + jnp.sum(jnp.where(pick_c[None], crossed_rows, 0.0), axis=1)
    live_count = live_cols[0]
    slots = jnp.arange(columns, dtype=jnp.int32)
    live = (slots < live_count).astype(jnp.float32)
    half = jnp.where(cd_first == cd_second, jnp.float32(0.5), jnp.float32(1.0))
    weight = half * live
    packed = (both * weight[None, :]).astype(jnp.bfloat16)
    return ladder(packed, pair_values, n_ab, n_cd)


def solution(mesh):
    placed = (P("ab", "cd"), P("ab", "cd", None), P("cd"), P("cd"), P("cd"))
    return jax.shard_map(
        functools.partial(on_device, mesh.shape["ab"], mesh.shape["cd"]),
        mesh=mesh, in_specs=placed, out_specs=P(None, ("ab", "cd")), check_vma=False,
    )
```

```python
import functools

import jax
import jax.numpy as jnp
from jax import lax
from jax.experimental import pallas as pl
from jax.experimental.pallas import tpu as pltpu
from jax.sharding import PartitionSpec as P

MESH = pl.DeviceIdType.MESH
X_CHIPS = 4


def exchange_kernel(
    n_cd, chunks_ref, amp_ref, second_ref, first_ref, out_ref, direct_ref, landed, send_sem, recv_sem, own_sem
):
    me_ab = lax.axis_index("ab")
    me_cd = lax.axis_index("cd")
    barrier = pltpu.get_barrier_semaphore()
    for k in range(1, n_cd):
        peer = lax.rem(me_cd + k, n_cd)
        pl.semaphore_signal(barrier, inc=1, device_id=(me_ab, peer), device_id_type=MESH)
    pl.semaphore_wait(barrier, n_cd - 1)
    own = pltpu.make_async_copy(chunks_ref.at[me_cd], landed.at[me_cd], own_sem.at[0])
    own.start()
    for k in range(1, n_cd):
        peer = lax.rem(me_cd + k, n_cd)

        @pl.when(peer < me_cd)
        def _():
            pltpu.make_async_remote_copy(
                src_ref=chunks_ref.at[peer],
                dst_ref=landed.at[me_cd],
                send_sem=send_sem.at[k],
                recv_sem=recv_sem.at[me_cd],
                device_id=(me_ab, peer),
                device_id_type=MESH,
            ).start()

    for k in range(1, n_cd):
        src = lax.rem(me_cd + k, n_cd)

        @pl.when(src < me_cd)
        def _():
            landed[src] = jnp.zeros(landed.shape[1:], landed.dtype)

    orbitals, columns = amp_ref.shape[2], second_ref.shape[1]
    pick_d = (lax.broadcasted_iota(jnp.int32, (orbitals, columns), 0) == second_ref[...]).astype(amp_ref.dtype)
    local = first_ref[...] - me_cd * amp_ref.shape[1]
    pick_c = lax.broadcasted_iota(jnp.int32, (amp_ref.shape[1], columns), 0) == local
    for ij in range(amp_ref.shape[0]):
        rows = jnp.dot(amp_ref[ij], pick_d, preferred_element_type=jnp.float32)
        direct_ref[ij:ij + 1, :] = jnp.sum(jnp.where(pick_c, rows, 0.0), axis=0, keepdims=True)

    own.wait()
    for k in range(1, n_cd):
        src = lax.rem(me_cd + n_cd - k, n_cd)

        @pl.when(src > me_cd)
        def _():
            pltpu.make_async_remote_copy(
                src_ref=chunks_ref.at[src],
                dst_ref=landed.at[src],
                send_sem=send_sem.at[k],
                recv_sem=recv_sem.at[src],
                device_id=(me_ab, src),
                device_id_type=MESH,
            ).wait_recv()

    out_ref[...] = landed[...]
    for k in range(1, n_cd):
        peer = lax.rem(me_cd + k, n_cd)

        @pl.when(peer < me_cd)
        def _():
            pltpu.make_async_remote_copy(
                src_ref=chunks_ref.at[me_cd],
                dst_ref=landed.at[me_cd],
                send_sem=send_sem.at[k],
                recv_sem=recv_sem.at[me_cd],
                device_id=(me_ab, me_cd),
                device_id_type=MESH,
            ).wait_send()


def exchange(chunks, amplitudes, second, first, n_cd):
    pair_block, columns = amplitudes.shape[0], second.shape[0]
    return pl.pallas_call(
        functools.partial(exchange_kernel, n_cd),
        out_shape=(
            jax.ShapeDtypeStruct(chunks.shape, chunks.dtype),
            jax.ShapeDtypeStruct((pair_block, columns), jnp.float32),
        ),
        in_specs=[pl.BlockSpec(memory_space=pltpu.VMEM)] * 4,
        out_specs=(pl.BlockSpec(memory_space=pltpu.VMEM), pl.BlockSpec(memory_space=pltpu.VMEM)),
        scratch_shapes=[
            pltpu.VMEM(chunks.shape, chunks.dtype),
            pltpu.SemaphoreType.DMA((n_cd,)),
            pltpu.SemaphoreType.DMA((n_cd,)),
            pltpu.SemaphoreType.DMA((1,)),
        ],
        compiler_params=pltpu.CompilerParams(collective_id=1, has_side_effects=True),
    )(chunks, amplitudes, second.reshape(1, columns), first.reshape(1, columns))


def ladder_kernel(
    n_ab, n_x, n_z, packed_ref, values_hbm, out_ref,
    slots, gathered, values_buf, first_out, first_in, second_out, second_in,
    values_sem, pk_send, pk_recv, first_send, first_recv, second_send, second_recv, own_sem,
):
    me_ab = lax.axis_index("ab")
    me_cd = lax.axis_index("cd")
    me_z = me_cd // n_x
    me_x = lax.rem(me_cd, n_x)
    rows = packed_ref.shape[0]
    block = values_buf.shape[1]

    z_order = [lax.rem(me_z + j, n_z) for j in list(range(1, n_z)) + [0]]
    order = []
    for z in z_order:
        for k in list(range(1, n_x)) + [0]:
            order.append(z * n_x + lax.rem(me_x + k, n_x))
    barrier = pltpu.get_barrier_semaphore()
    for k in range(1, n_ab):
        peer = lax.rem(me_ab + k, n_ab)
        pl.semaphore_signal(barrier, inc=1, device_id=(peer, me_cd), device_id_type=MESH)
    for k in range(1, n_x):
        peer = me_z * n_x + lax.rem(me_x + k, n_x)
        pl.semaphore_signal(barrier, inc=1, device_id=(me_ab, peer), device_id_type=MESH)
    for j in range(1, n_z):
        peer = lax.rem(me_z + j, n_z) * n_x + me_x
        pl.semaphore_signal(barrier, inc=1, device_id=(me_ab, peer), device_id_type=MESH)
    pl.semaphore_wait(barrier, (n_ab - 1) + (n_x - 1) + (n_z - 1))

    own = pltpu.make_async_copy(packed_ref, slots.at[me_ab], own_sem.at[0])
    own.start()
    for k in range(1, n_ab):
        peer = lax.rem(me_ab + k, n_ab)
        pltpu.make_async_remote_copy(
            src_ref=packed_ref,
            dst_ref=slots.at[me_ab],
            send_sem=pk_send.at[k],
            recv_sem=pk_recv.at[me_ab],
            device_id=(peer, me_cd),
            device_id_type=MESH,
        ).start()
    for step, owner in enumerate(order):
        pltpu.make_async_copy(
            values_hbm.at[pl.ds(pl.multiple_of(owner * block, block), block), :],
            values_buf.at[step],
            values_sem.at[step],
        ).start()
    own.wait()
    for k in range(1, n_ab):
        src = lax.rem(me_ab + n_ab - k, n_ab)
        pltpu.make_async_remote_copy(
            src_ref=packed_ref,
            dst_ref=slots.at[src],
            send_sem=pk_send.at[k],
            recv_sem=pk_recv.at[src],
            device_id=(src, me_cd),
            device_id_type=MESH,
        ).wait_recv()
    for k in range(n_ab):
        gathered[k * rows:(k + 1) * rows, :] = slots[k].astype(jnp.float32)
    lhs = gathered[...].astype(jnp.bfloat16)

    def one_block(step):
        pltpu.make_async_copy(
            values_hbm.at[pl.ds(0, block), :], values_buf.at[step], values_sem.at[step]
        ).wait()
        return lax.dot_general(
            lhs, values_buf[step], (((1,), (1,)), ((), ())), preferred_element_type=jnp.float32
        )

    def first_copy(j, k, peer):
        slot = j * (n_x - 1) + (k - 1)
        return pltpu.make_async_remote_copy(
            src_ref=first_out.at[slot],
            dst_ref=first_in.at[slot],
            send_sem=first_send.at[slot],
            recv_sem=first_recv.at[slot],
            device_id=(me_ab, peer),
            device_id_type=MESH,
        )

    def second_copy(j, peer):
        return pltpu.make_async_remote_copy(
            src_ref=second_out.at[j],
            dst_ref=second_in.at[j],
            send_sem=second_send.at[j],
            recv_sem=second_recv.at[j],
            device_id=(me_ab, peer),
            device_id_type=MESH,
        )

    own = []
    for j in range(n_z):
        for k in range(1, n_x):
            first_out[j * (n_x - 1) + (k - 1)] = one_block(j * n_x + (k - 1))
            first_copy(j, k, me_z * n_x + lax.rem(me_x + k, n_x)).start()
        own.append(one_block(j * n_x + (n_x - 1)))

    total = None
    for j in range(n_z):
        summed = own[j]
        for k in range(1, n_x):
            first_copy(j, k, me_z * n_x + lax.rem(me_x + n_x - k, n_x)).wait_recv()
            summed = summed + first_in[j * (n_x - 1) + (k - 1)]
        if j < n_z - 1:
            second_out[j] = summed
            second_copy(j, z_order[j] * n_x + me_x).start()
        else:
            total = summed
    for j in range(n_z - 1):
        second_copy(j, lax.rem(me_z + n_z - 1 - j, n_z) * n_x + me_x).wait_recv()
        total = total + second_in[j]
    out_ref[...] = total.astype(out_ref.dtype)

    for k in range(1, n_ab):
        pltpu.make_async_remote_copy(
            src_ref=packed_ref,
            dst_ref=slots.at[me_ab],
            send_sem=pk_send.at[k],
            recv_sem=pk_recv.at[me_ab],
            device_id=(me_ab, me_cd),
            device_id_type=MESH,
        ).wait_send()
    for j in range(n_z):
        for k in range(1, n_x):
            first_copy(j, k, me_cd).wait_send()
    for j in range(n_z - 1):
        second_copy(j, me_cd).wait_send()


def ladder(packed, pair_values, n_ab, n_cd):
    rows, columns = packed.shape
    ab_dev = pair_values.shape[0]
    block = ab_dev // n_cd
    n_x = X_CHIPS
    n_z = n_cd // n_x
    width = rows * n_ab
    return pl.pallas_call(
        functools.partial(ladder_kernel, n_ab, n_x, n_z),
        out_shape=jax.ShapeDtypeStruct((width, block), jnp.bfloat16),
        in_specs=[pl.BlockSpec(memory_space=pltpu.VMEM), pl.BlockSpec(memory_space=pl.ANY)],
        out_specs=pl.BlockSpec(memory_space=pltpu.VMEM),
        scratch_shapes=[
            pltpu.VMEM((n_ab, rows, columns), packed.dtype),
            pltpu.VMEM((width, columns), jnp.float32),
            pltpu.VMEM((n_cd, block, columns), pair_values.dtype),
            pltpu.VMEM((n_z * (n_x - 1), width, block), jnp.float32),
            pltpu.VMEM((n_z * (n_x - 1), width, block), jnp.float32),
            pltpu.VMEM((n_z - 1, width, block), jnp.float32),
            pltpu.VMEM((n_z - 1, width, block), jnp.float32),
            pltpu.SemaphoreType.DMA((n_cd,)),
            pltpu.SemaphoreType.DMA((n_ab,)),
            pltpu.SemaphoreType.DMA((n_ab,)),
            pltpu.SemaphoreType.DMA((n_z * (n_x - 1),)),
            pltpu.SemaphoreType.DMA((n_z * (n_x - 1),)),
            pltpu.SemaphoreType.DMA((n_z - 1,)),
            pltpu.SemaphoreType.DMA((n_z - 1,)),
            pltpu.SemaphoreType.DMA((1,)),
        ],
        compiler_params=pltpu.CompilerParams(
            collective_id=0, has_side_effects=True, vmem_limit_bytes=48 * 1024 * 1024
        ),
    )(packed, pair_values)


def on_device(n_ab, n_cd, pair_values, amplitudes, cd_first, cd_second, live_cols):
    slab = lax.axis_index("cd")
    orbit_block = amplitudes.shape[1]
    orbitals = amplitudes.shape[2]
    columns = cd_first.shape[0]
    local_first = cd_first - slab * orbit_block
    pair_block = amplitudes.shape[0]
    width = 64
    rows_first = jnp.transpose(amplitudes, (1, 0, 2)).reshape(orbit_block, pair_block, n_cd, orbit_block)
    rows_first = jnp.pad(rows_first, ((0, 0), (0, 0), (0, 0), (0, width - orbit_block)))
    chunks = jnp.transpose(rows_first, (2, 0, 1, 3)).reshape(n_cd, orbit_block * pair_block * width // 128, 128)
    landed, direct = exchange(chunks, amplitudes, cd_second, cd_first, n_cd)
    mirrored = landed.reshape(n_cd, orbit_block, pair_block, width)[..., :orbit_block]
    pick_d = (lax.broadcasted_iota(jnp.int32, (orbitals, columns), 0) == cd_second[None, :]).astype(
        amplitudes.dtype
    )
    crossed_rows = lax.dot_general(
        mirrored,
        pick_d.reshape(n_cd, orbit_block, columns),
        (((0, 1), (0, 1)), ((), ())),
        preferred_element_type=jnp.float32,
    )
    pick_c = lax.broadcasted_iota(jnp.int32, (orbit_block, columns), 0) == local_first[None, :]
    both = direct + jnp.sum(jnp.where(pick_c[None], crossed_rows, 0.0), axis=1)
    live_count = live_cols[0]
    slots = jnp.arange(columns, dtype=jnp.int32)
    live = (slots < live_count).astype(jnp.float32)
    half = jnp.where(cd_first == cd_second, jnp.float32(0.5), jnp.float32(1.0))
    weight = half * live
    packed = (both * weight[None, :]).astype(jnp.bfloat16)
    return ladder(packed, pair_values, n_ab, n_cd)


def solution(mesh):
    placed = (P("ab", "cd"), P("ab", "cd", None), P("cd"), P("cd"), P("cd"))
    return jax.shard_map(
        functools.partial(on_device, mesh.shape["ab"], mesh.shape["cd"]),
        mesh=mesh, in_specs=placed, out_specs=P(None, ("ab", "cd")), check_vma=False,
    )
```

```python
import functools

import jax
import jax.numpy as jnp
from jax import lax
from jax.experimental import pallas as pl
from jax.experimental.pallas import tpu as pltpu
from jax.sharding import PartitionSpec as P

MESH = pl.DeviceIdType.MESH
X_CHIPS = 4


def exchange_kernel(
    n_cd, chunks_ref, amp_ref, second_ref, first_ref, landed, direct_ref, send_sem, recv_sem, own_sem
):
    me_ab = lax.axis_index("ab")
    me_cd = lax.axis_index("cd")
    barrier = pltpu.get_barrier_semaphore()
    for k in range(1, n_cd):
        peer = lax.rem(me_cd + k, n_cd)
        pl.semaphore_signal(barrier, inc=1, device_id=(me_ab, peer), device_id_type=MESH)
    pl.semaphore_wait(barrier, n_cd - 1)
    own = pltpu.make_async_copy(chunks_ref.at[me_cd], landed.at[me_cd], own_sem.at[0])
    own.start()
    for k in range(1, n_cd):
        peer = lax.rem(me_cd + k, n_cd)

        @pl.when(peer < me_cd)
        def _():
            pltpu.make_async_remote_copy(
                src_ref=chunks_ref.at[peer],
                dst_ref=landed.at[me_cd],
                send_sem=send_sem.at[k],
                recv_sem=recv_sem.at[me_cd],
                device_id=(me_ab, peer),
                device_id_type=MESH,
            ).start()

    for k in range(1, n_cd):
        src = lax.rem(me_cd + k, n_cd)

        @pl.when(src < me_cd)
        def _():
            landed[src] = jnp.zeros(landed.shape[1:], landed.dtype)

    orbitals, columns = amp_ref.shape[2], second_ref.shape[1]
    pick_d = (lax.broadcasted_iota(jnp.int32, (orbitals, columns), 0) == second_ref[...]).astype(amp_ref.dtype)
    local = first_ref[...] - me_cd * amp_ref.shape[1]
    pick_c = lax.broadcasted_iota(jnp.int32, (amp_ref.shape[1], columns), 0) == local
    for ij in range(amp_ref.shape[0]):
        rows = jnp.dot(amp_ref[ij], pick_d, preferred_element_type=jnp.float32)
        direct_ref[ij:ij + 1, :] = jnp.sum(jnp.where(pick_c, rows, 0.0), axis=0, keepdims=True)

    own.wait()
    for k in range(1, n_cd):
        src = lax.rem(me_cd + n_cd - k, n_cd)

        @pl.when(src > me_cd)
        def _():
            pltpu.make_async_remote_copy(
                src_ref=chunks_ref.at[src],
                dst_ref=landed.at[src],
                send_sem=send_sem.at[k],
                recv_sem=recv_sem.at[src],
                device_id=(me_ab, src),
                device_id_type=MESH,
            ).wait_recv()

    for k in range(1, n_cd):
        peer = lax.rem(me_cd + k, n_cd)

        @pl.when(peer < me_cd)
        def _():
            pltpu.make_async_remote_copy(
                src_ref=chunks_ref.at[me_cd],
                dst_ref=landed.at[me_cd],
                send_sem=send_sem.at[k],
                recv_sem=recv_sem.at[me_cd],
                device_id=(me_ab, me_cd),
                device_id_type=MESH,
            ).wait_send()


def exchange(chunks, amplitudes, second, first, n_cd):
    pair_block, columns = amplitudes.shape[0], second.shape[0]
    return pl.pallas_call(
        functools.partial(exchange_kernel, n_cd),
        out_shape=(
            jax.ShapeDtypeStruct(chunks.shape, chunks.dtype),
            jax.ShapeDtypeStruct((pair_block, columns), jnp.float32),
        ),
        in_specs=[pl.BlockSpec(memory_space=pltpu.VMEM)] * 4,
        out_specs=(pl.BlockSpec(memory_space=pltpu.VMEM), pl.BlockSpec(memory_space=pltpu.VMEM)),
        scratch_shapes=[
            pltpu.SemaphoreType.DMA((n_cd,)),
            pltpu.SemaphoreType.DMA((n_cd,)),
            pltpu.SemaphoreType.DMA((1,)),
        ],
        compiler_params=pltpu.CompilerParams(collective_id=1, has_side_effects=True),
    )(chunks, amplitudes, second.reshape(1, columns), first.reshape(1, columns))


def ladder_kernel(
    n_ab, n_x, n_z, packed_ref, values_hbm, out_ref,
    slots, gathered, values_buf, first_out, first_in, second_out, second_in,
    values_sem, pk_send, pk_recv, first_send, first_recv, second_send, second_recv, own_sem,
):
    me_ab = lax.axis_index("ab")
    me_cd = lax.axis_index("cd")
    me_z = me_cd // n_x
    me_x = lax.rem(me_cd, n_x)
    rows = packed_ref.shape[0]
    block = values_buf.shape[1]

    z_order = [lax.rem(me_z + j, n_z) for j in list(range(1, n_z)) + [0]]
    order = []
    for z in z_order:
        for k in list(range(1, n_x)) + [0]:
            order.append(z * n_x + lax.rem(me_x + k, n_x))
    barrier = pltpu.get_barrier_semaphore()
    for k in range(1, n_ab):
        peer = lax.rem(me_ab + k, n_ab)
        pl.semaphore_signal(barrier, inc=1, device_id=(peer, me_cd), device_id_type=MESH)
    for k in range(1, n_x):
        peer = me_z * n_x + lax.rem(me_x + k, n_x)
        pl.semaphore_signal(barrier, inc=1, device_id=(me_ab, peer), device_id_type=MESH)
    for j in range(1, n_z):
        peer = lax.rem(me_z + j, n_z) * n_x + me_x
        pl.semaphore_signal(barrier, inc=1, device_id=(me_ab, peer), device_id_type=MESH)
    pl.semaphore_wait(barrier, (n_ab - 1) + (n_x - 1) + (n_z - 1))

    own = pltpu.make_async_copy(packed_ref, slots.at[me_ab], own_sem.at[0])
    own.start()
    for k in range(1, n_ab):
        peer = lax.rem(me_ab + k, n_ab)
        pltpu.make_async_remote_copy(
            src_ref=packed_ref,
            dst_ref=slots.at[me_ab],
            send_sem=pk_send.at[k],
            recv_sem=pk_recv.at[me_ab],
            device_id=(peer, me_cd),
            device_id_type=MESH,
        ).start()
    for step, owner in enumerate(order):
        pltpu.make_async_copy(
            values_hbm.at[pl.ds(pl.multiple_of(owner * block, block), block), :],
            values_buf.at[step],
            values_sem.at[step],
        ).start()
    own.wait()
    for k in range(1, n_ab):
        src = lax.rem(me_ab + n_ab - k, n_ab)
        pltpu.make_async_remote_copy(
            src_ref=packed_ref,
            dst_ref=slots.at[src],
            send_sem=pk_send.at[k],
            recv_sem=pk_recv.at[src],
            device_id=(src, me_cd),
            device_id_type=MESH,
        ).wait_recv()
    for k in range(n_ab):
        gathered[k * rows:(k + 1) * rows, :] = slots[k].astype(jnp.float32)
    lhs = gathered[...].astype(jnp.bfloat16)

    def one_block(step):
        pltpu.make_async_copy(
            values_hbm.at[pl.ds(0, block), :], values_buf.at[step], values_sem.at[step]
        ).wait()
        return lax.dot_general(
            lhs, values_buf[step], (((1,), (1,)), ((), ())), preferred_element_type=jnp.float32
        )

    def first_copy(j, k, peer):
        slot = j * (n_x - 1) + (k - 1)
        return pltpu.make_async_remote_copy(
            src_ref=first_out.at[slot],
            dst_ref=first_in.at[slot],
            send_sem=first_send.at[slot],
            recv_sem=first_recv.at[slot],
            device_id=(me_ab, peer),
            device_id_type=MESH,
        )

    def second_copy(j, peer):
        return pltpu.make_async_remote_copy(
            src_ref=second_out.at[j],
            dst_ref=second_in.at[j],
            send_sem=second_send.at[j],
            recv_sem=second_recv.at[j],
            device_id=(me_ab, peer),
            device_id_type=MESH,
        )

    own = []
    for j in range(n_z):
        for k in range(1, n_x):
            first_out[j * (n_x - 1) + (k - 1)] = one_block(j * n_x + (k - 1))
            first_copy(j, k, me_z * n_x + lax.rem(me_x + k, n_x)).start()
        own.append(one_block(j * n_x + (n_x - 1)))

    total = None
    for j in range(n_z):
        summed = own[j]
        for k in range(1, n_x):
            first_copy(j, k, me_z * n_x + lax.rem(me_x + n_x - k, n_x)).wait_recv()
            summed = summed + first_in[j * (n_x - 1) + (k - 1)]
        if j < n_z - 1:
            second_out[j] = summed
            second_copy(j, z_order[j] * n_x + me_x).start()
        else:
            total = summed
    for j in range(n_z - 1):
        second_copy(j, lax.rem(me_z + n_z - 1 - j, n_z) * n_x + me_x).wait_recv()
        total = total + second_in[j]
    out_ref[...] = total.astype(out_ref.dtype)

    for k in range(1, n_ab):
        pltpu.make_async_remote_copy(
            src_ref=packed_ref,
            dst_ref=slots.at[me_ab],
            send_sem=pk_send.at[k],
            recv_sem=pk_recv.at[me_ab],
            device_id=(me_ab, me_cd),
            device_id_type=MESH,
        ).wait_send()
    for j in range(n_z):
        for k in range(1, n_x):
            first_copy(j, k, me_cd).wait_send()
    for j in range(n_z - 1):
        second_copy(j, me_cd).wait_send()


def ladder(packed, pair_values, n_ab, n_cd):
    rows, columns = packed.shape
    ab_dev = pair_values.shape[0]
    block = ab_dev // n_cd
    n_x = X_CHIPS
    n_z = n_cd // n_x
    width = rows * n_ab
    return pl.pallas_call(
        functools.partial(ladder_kernel, n_ab, n_x, n_z),
        out_shape=jax.ShapeDtypeStruct((width, block), jnp.bfloat16),
        in_specs=[pl.BlockSpec(memory_space=pltpu.VMEM), pl.BlockSpec(memory_space=pl.ANY)],
        out_specs=pl.BlockSpec(memory_space=pltpu.VMEM),
        scratch_shapes=[
            pltpu.VMEM((n_ab, rows, columns), packed.dtype),
            pltpu.VMEM((width, columns), jnp.float32),
            pltpu.VMEM((n_cd, block, columns), pair_values.dtype),
            pltpu.VMEM((n_z * (n_x - 1), width, block), jnp.float32),
            pltpu.VMEM((n_z * (n_x - 1), width, block), jnp.float32),
            pltpu.VMEM((n_z - 1, width, block), jnp.float32),
            pltpu.VMEM((n_z - 1, width, block), jnp.float32),
            pltpu.SemaphoreType.DMA((n_cd,)),
            pltpu.SemaphoreType.DMA((n_ab,)),
            pltpu.SemaphoreType.DMA((n_ab,)),
            pltpu.SemaphoreType.DMA((n_z * (n_x - 1),)),
            pltpu.SemaphoreType.DMA((n_z * (n_x - 1),)),
            pltpu.SemaphoreType.DMA((n_z - 1,)),
            pltpu.SemaphoreType.DMA((n_z - 1,)),
            pltpu.SemaphoreType.DMA((1,)),
        ],
        compiler_params=pltpu.CompilerParams(
            collective_id=0, has_side_effects=True, vmem_limit_bytes=48 * 1024 * 1024
        ),
    )(packed, pair_values)


def on_device(n_ab, n_cd, pair_values, amplitudes, cd_first, cd_second, live_cols):
    slab = lax.axis_index("cd")
    orbit_block = amplitudes.shape[1]
    orbitals = amplitudes.shape[2]
    columns = cd_first.shape[0]
    local_first = cd_first - slab * orbit_block
    pair_block = amplitudes.shape[0]
    piece = pair_block * orbit_block * orbit_block
    padded = -(-piece // 1024) * 1024
    rows_first = jnp.transpose(amplitudes, (1, 0, 2)).reshape(orbit_block, pair_block, n_cd, orbit_block)
    chunks = jnp.transpose(rows_first, (2, 0, 1, 3)).reshape(n_cd, piece)
    chunks = jnp.pad(chunks, ((0, 0), (0, padded - piece)))
    landed, direct = exchange(chunks.reshape(n_cd, padded // 128, 128), amplitudes, cd_second, cd_first, n_cd)
    mirrored = landed.reshape(n_cd, padded)[:, :piece].reshape(n_cd, orbit_block, pair_block, orbit_block)
    pick_d = (lax.broadcasted_iota(jnp.int32, (orbitals, columns), 0) == cd_second[None, :]).astype(
        amplitudes.dtype
    )
    crossed_rows = lax.dot_general(
        mirrored,
        pick_d.reshape(n_cd, orbit_block, columns),
        (((0, 1), (0, 1)), ((), ())),
        preferred_element_type=jnp.float32,
    )
    pick_c = lax.broadcasted_iota(jnp.int32, (orbit_block, columns), 0) == local_first[None, :]
    both = direct + jnp.sum(jnp.where(pick_c[None], crossed_rows, 0.0), axis=1)
    live_count = live_cols[0]
    slots = jnp.arange(columns, dtype=jnp.int32)
    live = (slots < live_count).astype(jnp.float32)
    half = jnp.where(cd_first == cd_second, jnp.float32(0.5), jnp.float32(1.0))
    weight = half * live
    packed = (both * weight[None, :]).astype(jnp.bfloat16)
    return ladder(packed, pair_values, n_ab, n_cd)


def solution(mesh):
    placed = (P("ab", "cd"), P("ab", "cd", None), P("cd"), P("cd"), P("cd"))
    return jax.shard_map(
        functools.partial(on_device, mesh.shape["ab"], mesh.shape["cd"]),
        mesh=mesh, in_specs=placed, out_specs=P(None, ("ab", "cd")), check_vma=False,
    )
```

```python
import functools

import jax
import jax.numpy as jnp
from jax import lax
from jax.experimental import pallas as pl
from jax.experimental.pallas import tpu as pltpu
from jax.sharding import PartitionSpec as P

MESH = pl.DeviceIdType.MESH
X_CHIPS = 4


def exchange_kernel(
    n_cd, chunks_ref, amp_ref, second_ref, first_ref, landed, direct_ref, send_sem, recv_sem, own_sem
):
    me_ab = lax.axis_index("ab")
    me_cd = lax.axis_index("cd")
    barrier = pltpu.get_barrier_semaphore()
    for k in range(1, n_cd):
        peer = lax.rem(me_cd + k, n_cd)
        pl.semaphore_signal(barrier, inc=1, device_id=(me_ab, peer), device_id_type=MESH)
    pl.semaphore_wait(barrier, n_cd - 1)
    own = pltpu.make_async_copy(chunks_ref.at[me_cd], landed.at[me_cd], own_sem.at[0])
    own.start()
    for k in range(1, n_cd):
        peer = lax.rem(me_cd + k, n_cd)

        @pl.when(peer < me_cd)
        def _():
            pltpu.make_async_remote_copy(
                src_ref=chunks_ref.at[peer],
                dst_ref=landed.at[me_cd],
                send_sem=send_sem.at[k],
                recv_sem=recv_sem.at[me_cd],
                device_id=(me_ab, peer),
                device_id_type=MESH,
            ).start()

    for k in range(1, n_cd):
        src = lax.rem(me_cd + k, n_cd)

        @pl.when(src < me_cd)
        def _():
            landed[src] = jnp.zeros(landed.shape[1:], landed.dtype)

    orbitals, columns = amp_ref.shape[2], second_ref.shape[1]
    pick_d = (lax.broadcasted_iota(jnp.int32, (orbitals, columns), 0) == second_ref[...]).astype(amp_ref.dtype)
    local = first_ref[...] - me_cd * amp_ref.shape[1]
    pick_c = lax.broadcasted_iota(jnp.int32, (amp_ref.shape[1], columns), 0) == local
    for ij in range(amp_ref.shape[0]):
        rows = jnp.dot(amp_ref[ij], pick_d, preferred_element_type=jnp.float32)
        direct_ref[ij:ij + 1, :] = jnp.sum(jnp.where(pick_c, rows, 0.0), axis=0, keepdims=True)

    own.wait()
    for k in range(1, n_cd):
        src = lax.rem(me_cd + n_cd - k, n_cd)

        @pl.when(src > me_cd)
        def _():
            pltpu.make_async_remote_copy(
                src_ref=chunks_ref.at[src],
                dst_ref=landed.at[src],
                send_sem=send_sem.at[k],
                recv_sem=recv_sem.at[src],
                device_id=(me_ab, src),
                device_id_type=MESH,
            ).wait_recv()

    for k in range(1, n_cd):
        peer = lax.rem(me_cd + k, n_cd)

        @pl.when(peer < me_cd)
        def _():
            pltpu.make_async_remote_copy(
                src_ref=chunks_ref.at[me_cd],
                dst_ref=landed.at[me_cd],
                send_sem=send_sem.at[k],
                recv_sem=recv_sem.at[me_cd],
                device_id=(me_ab, me_cd),
                device_id_type=MESH,
            ).wait_send()


def exchange(chunks, amplitudes, second, first, n_cd):
    pair_block, columns = amplitudes.shape[0], second.shape[0]
    return pl.pallas_call(
        functools.partial(exchange_kernel, n_cd),
        out_shape=(
            jax.ShapeDtypeStruct(chunks.shape, chunks.dtype),
            jax.ShapeDtypeStruct((pair_block, columns), jnp.float32),
        ),
        in_specs=[pl.BlockSpec(memory_space=pltpu.VMEM)] * 4,
        out_specs=(pl.BlockSpec(memory_space=pltpu.VMEM), pl.BlockSpec(memory_space=pltpu.VMEM)),
        scratch_shapes=[
            pltpu.SemaphoreType.DMA((n_cd,)),
            pltpu.SemaphoreType.DMA((n_cd,)),
            pltpu.SemaphoreType.DMA((1,)),
        ],
        compiler_params=pltpu.CompilerParams(collective_id=1, has_side_effects=True),
    )(chunks, amplitudes, second.reshape(1, columns), first.reshape(1, columns))


def ladder_kernel(
    n_ab, n_x, n_z, packed_ref, values_hbm, out_ref,
    slots, gathered, values_buf, first_out, first_in, second_out, second_in,
    values_sem, pk_send, pk_recv, first_send, first_recv, second_send, second_recv, own_sem,
):
    me_ab = lax.axis_index("ab")
    me_cd = lax.axis_index("cd")
    me_z = me_cd // n_x
    me_x = lax.rem(me_cd, n_x)
    rows = packed_ref.shape[0]
    block = values_buf.shape[1]

    z_order = [lax.rem(me_z + j, n_z) for j in list(range(1, n_z)) + [0]]
    order = []
    for z in z_order:
        for k in list(range(1, n_x)) + [0]:
            order.append(z * n_x + lax.rem(me_x + k, n_x))
    barrier = pltpu.get_barrier_semaphore()
    for k in range(1, n_ab):
        peer = lax.rem(me_ab + k, n_ab)
        pl.semaphore_signal(barrier, inc=1, device_id=(peer, me_cd), device_id_type=MESH)
    for k in range(1, n_x):
        peer = me_z * n_x + lax.rem(me_x + k, n_x)
        pl.semaphore_signal(barrier, inc=1, device_id=(me_ab, peer), device_id_type=MESH)
    for j in range(1, n_z):
        peer = lax.rem(me_z + j, n_z) * n_x + me_x
        pl.semaphore_signal(barrier, inc=1, device_id=(me_ab, peer), device_id_type=MESH)
    pl.semaphore_wait(barrier, (n_ab - 1) + (n_x - 1) + (n_z - 1))

    own = pltpu.make_async_copy(packed_ref, slots.at[me_ab], own_sem.at[0])
    own.start()
    for k in range(1, n_ab):
        peer = lax.rem(me_ab + k, n_ab)
        pltpu.make_async_remote_copy(
            src_ref=packed_ref,
            dst_ref=slots.at[me_ab],
            send_sem=pk_send.at[k],
            recv_sem=pk_recv.at[me_ab],
            device_id=(peer, me_cd),
            device_id_type=MESH,
        ).start()
    for step, owner in enumerate(order):
        pltpu.make_async_copy(
            values_hbm.at[pl.ds(pl.multiple_of(owner * block, block), block), :],
            values_buf.at[step],
            values_sem.at[step],
        ).start()
    own.wait()
    for k in range(1, n_ab):
        src = lax.rem(me_ab + n_ab - k, n_ab)
        pltpu.make_async_remote_copy(
            src_ref=packed_ref,
            dst_ref=slots.at[src],
            send_sem=pk_send.at[k],
            recv_sem=pk_recv.at[src],
            device_id=(src, me_cd),
            device_id_type=MESH,
        ).wait_recv()
    for k in range(n_ab):
        gathered[k * rows:(k + 1) * rows, :] = slots[k]
    lhs = gathered[...]

    def one_block(step):
        pltpu.make_async_copy(
            values_hbm.at[pl.ds(0, block), :], values_buf.at[step], values_sem.at[step]
        ).wait()
        return lax.dot_general(
            lhs, values_buf[step], (((1,), (1,)), ((), ())), preferred_element_type=jnp.float32
        )

    def first_copy(j, k, peer):
        slot = j * (n_x - 1) + (k - 1)
        return pltpu.make_async_remote_copy(
            src_ref=first_out.at[slot],
            dst_ref=first_in.at[slot],
            send_sem=first_send.at[slot],
            recv_sem=first_recv.at[slot],
            device_id=(me_ab, peer),
            device_id_type=MESH,
        )

    def second_copy(j, peer):
        return pltpu.make_async_remote_copy(
            src_ref=second_out.at[j],
            dst_ref=second_in.at[j],
            send_sem=second_send.at[j],
            recv_sem=second_recv.at[j],
            device_id=(me_ab, peer),
            device_id_type=MESH,
        )

    own = []
    for j in range(n_z):
        for k in range(1, n_x):
            first_out[j * (n_x - 1) + (k - 1)] = one_block(j * n_x + (k - 1))
            first_copy(j, k, me_z * n_x + lax.rem(me_x + k, n_x)).start()
        own.append(one_block(j * n_x + (n_x - 1)))

    total = None
    for j in range(n_z):
        summed = own[j]
        for k in range(1, n_x):
            first_copy(j, k, me_z * n_x + lax.rem(me_x + n_x - k, n_x)).wait_recv()
            summed = summed + first_in[j * (n_x - 1) + (k - 1)]
        if j < n_z - 1:
            second_out[j] = summed
            second_copy(j, z_order[j] * n_x + me_x).start()
        else:
            total = summed
    for j in range(n_z - 1):
        second_copy(j, lax.rem(me_z + n_z - 1 - j, n_z) * n_x + me_x).wait_recv()
        total = total + second_in[j]
    out_ref[...] = total.astype(out_ref.dtype)

    for k in range(1, n_ab):
        pltpu.make_async_remote_copy(
            src_ref=packed_ref,
            dst_ref=slots.at[me_ab],
            send_sem=pk_send.at[k],
            recv_sem=pk_recv.at[me_ab],
            device_id=(me_ab, me_cd),
            device_id_type=MESH,
        ).wait_send()
    for j in range(n_z):
        for k in range(1, n_x):
            first_copy(j, k, me_cd).wait_send()
    for j in range(n_z - 1):
        second_copy(j, me_cd).wait_send()


def ladder(packed, pair_values, n_ab, n_cd):
    rows, columns = packed.shape
    ab_dev = pair_values.shape[0]
    block = ab_dev // n_cd
    n_x = X_CHIPS
    n_z = n_cd // n_x
    width = rows * n_ab
    return pl.pallas_call(
        functools.partial(ladder_kernel, n_ab, n_x, n_z),
        out_shape=jax.ShapeDtypeStruct((width, block), jnp.bfloat16),
        in_specs=[pl.BlockSpec(memory_space=pltpu.VMEM), pl.BlockSpec(memory_space=pl.ANY)],
        out_specs=pl.BlockSpec(memory_space=pltpu.VMEM),
        scratch_shapes=[
            pltpu.VMEM((n_ab, rows, columns), packed.dtype),
            pltpu.VMEM((width, columns), packed.dtype),
            pltpu.VMEM((n_cd, block, columns), pair_values.dtype),
            pltpu.VMEM((n_z * (n_x - 1), width, block), jnp.float32),
            pltpu.VMEM((n_z * (n_x - 1), width, block), jnp.float32),
            pltpu.VMEM((n_z - 1, width, block), jnp.float32),
            pltpu.VMEM((n_z - 1, width, block), jnp.float32),
            pltpu.SemaphoreType.DMA((n_cd,)),
            pltpu.SemaphoreType.DMA((n_ab,)),
            pltpu.SemaphoreType.DMA((n_ab,)),
            pltpu.SemaphoreType.DMA((n_z * (n_x - 1),)),
            pltpu.SemaphoreType.DMA((n_z * (n_x - 1),)),
            pltpu.SemaphoreType.DMA((n_z - 1,)),
            pltpu.SemaphoreType.DMA((n_z - 1,)),
            pltpu.SemaphoreType.DMA((1,)),
        ],
        compiler_params=pltpu.CompilerParams(
            collective_id=0, has_side_effects=True, vmem_limit_bytes=48 * 1024 * 1024
        ),
    )(packed, pair_values)


def on_device(n_ab, n_cd, pair_values, amplitudes, cd_first, cd_second, live_cols):
    slab = lax.axis_index("cd")
    orbit_block = amplitudes.shape[1]
    orbitals = amplitudes.shape[2]
    columns = cd_first.shape[0]
    local_first = cd_first - slab * orbit_block
    pair_block = amplitudes.shape[0]
    piece = pair_block * orbit_block * orbit_block
    padded = -(-piece // 1024) * 1024
    rows_first = jnp.transpose(amplitudes, (1, 0, 2)).reshape(orbit_block, pair_block, n_cd, orbit_block)
    chunks = jnp.transpose(rows_first, (2, 0, 1, 3)).reshape(n_cd, piece)
    chunks = jnp.pad(chunks, ((0, 0), (0, padded - piece)))
    landed, direct = exchange(chunks.reshape(n_cd, padded // 128, 128), amplitudes, cd_second, cd_first, n_cd)
    mirrored = landed.reshape(n_cd, padded)[:, :piece].reshape(n_cd, orbit_block, pair_block, orbit_block)
    pick_d = (lax.broadcasted_iota(jnp.int32, (orbitals, columns), 0) == cd_second[None, :]).astype(
        amplitudes.dtype
    )
    crossed_rows = lax.dot_general(
        mirrored,
        pick_d.reshape(n_cd, orbit_block, columns),
        (((0, 1), (0, 1)), ((), ())),
        preferred_element_type=jnp.float32,
    )
    pick_c = lax.broadcasted_iota(jnp.int32, (orbit_block, columns), 0) == local_first[None, :]
    both = direct + jnp.sum(jnp.where(pick_c[None], crossed_rows, 0.0), axis=1)
    live_count = live_cols[0]
    slots = jnp.arange(columns, dtype=jnp.int32)
    live = (slots < live_count).astype(jnp.float32)
    half = jnp.where(cd_first == cd_second, jnp.float32(0.5), jnp.float32(1.0))
    weight = half * live
    packed = (both * weight[None, :]).astype(jnp.bfloat16)
    return ladder(packed, pair_values, n_ab, n_cd)


def solution(mesh):
    placed = (P("ab", "cd"), P("ab", "cd", None), P("cd"), P("cd"), P("cd"))
    return jax.shard_map(
        functools.partial(on_device, mesh.shape["ab"], mesh.shape["cd"]),
        mesh=mesh, in_specs=placed, out_specs=P(None, ("ab", "cd")), check_vma=False,
    )
```

```python
import functools

import jax
import jax.numpy as jnp
from jax import lax
from jax.experimental import pallas as pl
from jax.experimental.pallas import tpu as pltpu
from jax.sharding import PartitionSpec as P

MESH = pl.DeviceIdType.MESH
X_CHIPS = 4


def exchange_kernel(
    n_cd, chunks_ref, amp_ref, second_ref, first_ref, landed, direct_ref, send_sem, recv_sem, own_sem
):
    me_ab = lax.axis_index("ab")
    me_cd = lax.axis_index("cd")
    barrier = pltpu.get_barrier_semaphore()
    for k in range(1, n_cd):
        peer = lax.rem(me_cd + k, n_cd)
        pl.semaphore_signal(barrier, inc=1, device_id=(me_ab, peer), device_id_type=MESH)
    pl.semaphore_wait(barrier, n_cd - 1)
    own = pltpu.make_async_copy(chunks_ref.at[me_cd], landed.at[me_cd], own_sem.at[0])
    own.start()
    for k in range(1, n_cd):
        peer = lax.rem(me_cd + n_cd - k, n_cd)

        @pl.when(peer < me_cd)
        def _():
            pltpu.make_async_remote_copy(
                src_ref=chunks_ref.at[peer],
                dst_ref=landed.at[me_cd],
                send_sem=send_sem.at[k],
                recv_sem=recv_sem.at[me_cd],
                device_id=(me_ab, peer),
                device_id_type=MESH,
            ).start()

    for k in range(1, n_cd):
        src = lax.rem(me_cd + k, n_cd)

        @pl.when(src < me_cd)
        def _():
            landed[src] = jnp.zeros(landed.shape[1:], landed.dtype)

    orbitals, columns = amp_ref.shape[2], second_ref.shape[1]
    pick_d = (lax.broadcasted_iota(jnp.int32, (orbitals, columns), 0) == second_ref[...]).astype(amp_ref.dtype)
    local = first_ref[...] - me_cd * amp_ref.shape[1]
    pick_c = lax.broadcasted_iota(jnp.int32, (amp_ref.shape[1], columns), 0) == local
    for ij in range(amp_ref.shape[0]):
        rows = jnp.dot(amp_ref[ij], pick_d, preferred_element_type=jnp.float32)
        direct_ref[ij:ij + 1, :] = jnp.sum(jnp.where(pick_c, rows, 0.0), axis=0, keepdims=True)

    own.wait()
    for k in range(1, n_cd):
        src = lax.rem(me_cd + n_cd - k, n_cd)

        @pl.when(src > me_cd)
        def _():
            pltpu.make_async_remote_copy(
                src_ref=chunks_ref.at[src],
                dst_ref=landed.at[src],
                send_sem=send_sem.at[k],
                recv_sem=recv_sem.at[src],
                device_id=(me_ab, src),
                device_id_type=MESH,
            ).wait_recv()

    for k in range(1, n_cd):
        peer = lax.rem(me_cd + n_cd - k, n_cd)

        @pl.when(peer < me_cd)
        def _():
            pltpu.make_async_remote_copy(
                src_ref=chunks_ref.at[me_cd],
                dst_ref=landed.at[me_cd],
                send_sem=send_sem.at[k],
                recv_sem=recv_sem.at[me_cd],
                device_id=(me_ab, me_cd),
                device_id_type=MESH,
            ).wait_send()


def exchange(chunks, amplitudes, second, first, n_cd):
    pair_block, columns = amplitudes.shape[0], second.shape[0]
    return pl.pallas_call(
        functools.partial(exchange_kernel, n_cd),
        out_shape=(
            jax.ShapeDtypeStruct(chunks.shape, chunks.dtype),
            jax.ShapeDtypeStruct((pair_block, columns), jnp.float32),
        ),
        in_specs=[pl.BlockSpec(memory_space=pltpu.VMEM)] * 4,
        out_specs=(pl.BlockSpec(memory_space=pltpu.VMEM), pl.BlockSpec(memory_space=pltpu.VMEM)),
        scratch_shapes=[
            pltpu.SemaphoreType.DMA((n_cd,)),
            pltpu.SemaphoreType.DMA((n_cd,)),
            pltpu.SemaphoreType.DMA((1,)),
        ],
        compiler_params=pltpu.CompilerParams(collective_id=1, has_side_effects=True),
    )(chunks, amplitudes, second.reshape(1, columns), first.reshape(1, columns))


def ladder_kernel(
    n_ab, n_x, n_z, packed_ref, values_hbm, out_ref,
    slots, gathered, values_buf, first_out, first_in, second_out, second_in,
    values_sem, pk_send, pk_recv, first_send, first_recv, second_send, second_recv, own_sem,
):
    me_ab = lax.axis_index("ab")
    me_cd = lax.axis_index("cd")
    me_z = me_cd // n_x
    me_x = lax.rem(me_cd, n_x)
    rows = packed_ref.shape[0]
    block = values_buf.shape[1]

    z_order = [lax.rem(me_z + j, n_z) for j in list(range(1, n_z)) + [0]]
    order = []
    for z in z_order:
        for k in list(range(1, n_x)) + [0]:
            order.append(z * n_x + lax.rem(me_x + k, n_x))
    barrier = pltpu.get_barrier_semaphore()
    for k in range(1, n_ab):
        peer = lax.rem(me_ab + k, n_ab)
        pl.semaphore_signal(barrier, inc=1, device_id=(peer, me_cd), device_id_type=MESH)
    for k in range(1, n_x):
        peer = me_z * n_x + lax.rem(me_x + k, n_x)
        pl.semaphore_signal(barrier, inc=1, device_id=(me_ab, peer), device_id_type=MESH)
    for j in range(1, n_z):
        peer = lax.rem(me_z + j, n_z) * n_x + me_x
        pl.semaphore_signal(barrier, inc=1, device_id=(me_ab, peer), device_id_type=MESH)
    pl.semaphore_wait(barrier, (n_ab - 1) + (n_x - 1) + (n_z - 1))

    own = pltpu.make_async_copy(packed_ref, slots.at[me_ab], own_sem.at[0])
    own.start()
    for k in range(1, n_ab):
        peer = lax.rem(me_ab + k, n_ab)
        pltpu.make_async_remote_copy(
            src_ref=packed_ref,
            dst_ref=slots.at[me_ab],
            send_sem=pk_send.at[k],
            recv_sem=pk_recv.at[me_ab],
            device_id=(peer, me_cd),
            device_id_type=MESH,
        ).start()
    for step, owner in enumerate(order):
        pltpu.make_async_copy(
            values_hbm.at[pl.ds(pl.multiple_of(owner * block, block), block), :],
            values_buf.at[step],
            values_sem.at[step],
        ).start()
    own.wait()
    for k in range(1, n_ab):
        src = lax.rem(me_ab + n_ab - k, n_ab)
        pltpu.make_async_remote_copy(
            src_ref=packed_ref,
            dst_ref=slots.at[src],
            send_sem=pk_send.at[k],
            recv_sem=pk_recv.at[src],
            device_id=(src, me_cd),
            device_id_type=MESH,
        ).wait_recv()
    for k in range(n_ab):
        gathered[k * rows:(k + 1) * rows, :] = slots[k].astype(jnp.float32)
    lhs = gathered[...].astype(jnp.bfloat16)

    def one_block(step):
        pltpu.make_async_copy(
            values_hbm.at[pl.ds(0, block), :], values_buf.at[step], values_sem.at[step]
        ).wait()
        return lax.dot_general(
            lhs, values_buf[step], (((1,), (1,)), ((), ())), preferred_element_type=jnp.float32
        )

    def first_copy(j, k, peer):
        slot = j * (n_x - 1) + (k - 1)
        return pltpu.make_async_remote_copy(
            src_ref=first_out.at[slot],
            dst_ref=first_in.at[slot],
            send_sem=first_send.at[slot],
            recv_sem=first_recv.at[slot],
            device_id=(me_ab, peer),
            device_id_type=MESH,
        )

    def second_copy(j, peer):
        return pltpu.make_async_remote_copy(
            src_ref=second_out.at[j],
            dst_ref=second_in.at[j],
            send_sem=second_send.at[j],
            recv_sem=second_recv.at[j],
            device_id=(me_ab, peer),
            device_id_type=MESH,
        )

    own = []
    for j in range(n_z):
        for k in range(1, n_x):
            first_out[j * (n_x - 1) + (k - 1)] = one_block(j * n_x + (k - 1))
            first_copy(j, k, me_z * n_x + lax.rem(me_x + k, n_x)).start()
        own.append(one_block(j * n_x + (n_x - 1)))

    total = None
    for j in range(n_z):
        summed = own[j]
        for k in range(1, n_x):
            first_copy(j, k, me_z * n_x + lax.rem(me_x + n_x - k, n_x)).wait_recv()
            summed = summed + first_in[j * (n_x - 1) + (k - 1)]
        if j < n_z - 1:
            second_out[j] = summed
            second_copy(j, z_order[j] * n_x + me_x).start()
        else:
            total = summed
    for j in range(n_z - 1):
        second_copy(j, lax.rem(me_z + n_z - 1 - j, n_z) * n_x + me_x).wait_recv()
        total = total + second_in[j]
    out_ref[...] = total.astype(out_ref.dtype)

    for k in range(1, n_ab):
        pltpu.make_async_remote_copy(
            src_ref=packed_ref,
            dst_ref=slots.at[me_ab],
            send_sem=pk_send.at[k],
            recv_sem=pk_recv.at[me_ab],
            device_id=(me_ab, me_cd),
            device_id_type=MESH,
        ).wait_send()
    for j in range(n_z):
        for k in range(1, n_x):
            first_copy(j, k, me_cd).wait_send()
    for j in range(n_z - 1):
        second_copy(j, me_cd).wait_send()


def ladder(packed, pair_values, n_ab, n_cd):
    rows, columns = packed.shape
    ab_dev = pair_values.shape[0]
    block = ab_dev // n_cd
    n_x = X_CHIPS
    n_z = n_cd // n_x
    width = rows * n_ab
    return pl.pallas_call(
        functools.partial(ladder_kernel, n_ab, n_x, n_z),
        out_shape=jax.ShapeDtypeStruct((width, block), jnp.bfloat16),
        in_specs=[pl.BlockSpec(memory_space=pltpu.VMEM), pl.BlockSpec(memory_space=pl.ANY)],
        out_specs=pl.BlockSpec(memory_space=pltpu.VMEM),
        scratch_shapes=[
            pltpu.VMEM((n_ab, rows, columns), packed.dtype),
            pltpu.VMEM((width, columns), jnp.float32),
            pltpu.VMEM((n_cd, block, columns), pair_values.dtype),
            pltpu.VMEM((n_z * (n_x - 1), width, block), jnp.float32),
            pltpu.VMEM((n_z * (n_x - 1), width, block), jnp.float32),
            pltpu.VMEM((n_z - 1, width, block), jnp.float32),
            pltpu.VMEM((n_z - 1, width, block), jnp.float32),
            pltpu.SemaphoreType.DMA((n_cd,)),
            pltpu.SemaphoreType.DMA((n_ab,)),
            pltpu.SemaphoreType.DMA((n_ab,)),
            pltpu.SemaphoreType.DMA((n_z * (n_x - 1),)),
            pltpu.SemaphoreType.DMA((n_z * (n_x - 1),)),
            pltpu.SemaphoreType.DMA((n_z - 1,)),
            pltpu.SemaphoreType.DMA((n_z - 1,)),
            pltpu.SemaphoreType.DMA((1,)),
        ],
        compiler_params=pltpu.CompilerParams(
            collective_id=0, has_side_effects=True, vmem_limit_bytes=48 * 1024 * 1024
        ),
    )(packed, pair_values)


def on_device(n_ab, n_cd, pair_values, amplitudes, cd_first, cd_second, live_cols):
    slab = lax.axis_index("cd")
    orbit_block = amplitudes.shape[1]
    orbitals = amplitudes.shape[2]
    columns = cd_first.shape[0]
    local_first = cd_first - slab * orbit_block
    pair_block = amplitudes.shape[0]
    piece = pair_block * orbit_block * orbit_block
    padded = -(-piece // 1024) * 1024
    rows_first = jnp.transpose(amplitudes, (1, 0, 2)).reshape(orbit_block, pair_block, n_cd, orbit_block)
    chunks = jnp.transpose(rows_first, (2, 0, 1, 3)).reshape(n_cd, piece)
    chunks = jnp.pad(chunks, ((0, 0), (0, padded - piece)))
    landed, direct = exchange(chunks.reshape(n_cd, padded // 128, 128), amplitudes, cd_second, cd_first, n_cd)
    mirrored = landed.reshape(n_cd, padded)[:, :piece].reshape(n_cd, orbit_block, pair_block, orbit_block)
    pick_d = (lax.broadcasted_iota(jnp.int32, (orbitals, columns), 0) == cd_second[None, :]).astype(
        amplitudes.dtype
    )
    crossed_rows = lax.dot_general(
        mirrored,
        pick_d.reshape(n_cd, orbit_block, columns),
        (((0, 1), (0, 1)), ((), ())),
        preferred_element_type=jnp.float32,
    )
    pick_c = lax.broadcasted_iota(jnp.int32, (orbit_block, columns), 0) == local_first[None, :]
    both = direct + jnp.sum(jnp.where(pick_c[None], crossed_rows, 0.0), axis=1)
    live_count = live_cols[0]
    slots = jnp.arange(columns, dtype=jnp.int32)
    live = (slots < live_count).astype(jnp.float32)
    half = jnp.where(cd_first == cd_second, jnp.float32(0.5), jnp.float32(1.0))
    weight = half * live
    packed = (both * weight[None, :]).astype(jnp.bfloat16)
    return ladder(packed, pair_values, n_ab, n_cd)


def solution(mesh):
    placed = (P("ab", "cd"), P("ab", "cd", None), P("cd"), P("cd"), P("cd"))
    return jax.shard_map(
        functools.partial(on_device, mesh.shape["ab"], mesh.shape["cd"]),
        mesh=mesh, in_specs=placed, out_specs=P(None, ("ab", "cd")), check_vma=False,
    )
```

```python
import functools

import jax
import jax.numpy as jnp
from jax import lax
from jax.experimental import pallas as pl
from jax.experimental.pallas import tpu as pltpu
from jax.sharding import PartitionSpec as P

MESH = pl.DeviceIdType.MESH
X_CHIPS = 4


def exchange_kernel(
    n_cd, chunks_ref, amp_ref, second_ref, first_ref, landed, direct_ref, send_sem, recv_sem, own_sem
):
    me_ab = lax.axis_index("ab")
    me_cd = lax.axis_index("cd")
    barrier = pltpu.get_barrier_semaphore()
    for k in range(1, n_cd):
        peer = lax.rem(me_cd + k, n_cd)
        pl.semaphore_signal(barrier, inc=1, device_id=(me_ab, peer), device_id_type=MESH)
    pl.semaphore_wait(barrier, n_cd - 1)
    own = pltpu.make_async_copy(chunks_ref.at[me_cd], landed.at[me_cd], own_sem.at[0])
    for k in range(1, n_cd):
        peer = lax.rem(me_cd + k, n_cd)

        @pl.when(peer < me_cd)
        def _():
            pltpu.make_async_remote_copy(
                src_ref=chunks_ref.at[peer],
                dst_ref=landed.at[me_cd],
                send_sem=send_sem.at[k],
                recv_sem=recv_sem.at[me_cd],
                device_id=(me_ab, peer),
                device_id_type=MESH,
            ).start()

    own.start()
    for k in range(1, n_cd):
        src = lax.rem(me_cd + k, n_cd)

        @pl.when(src < me_cd)
        def _():
            landed[src] = jnp.zeros(landed.shape[1:], landed.dtype)

    orbitals, columns = amp_ref.shape[2], second_ref.shape[1]
    pick_d = (lax.broadcasted_iota(jnp.int32, (orbitals, columns), 0) == second_ref[...]).astype(amp_ref.dtype)
    local = first_ref[...] - me_cd * amp_ref.shape[1]
    pick_c = lax.broadcasted_iota(jnp.int32, (amp_ref.shape[1], columns), 0) == local
    for ij in range(amp_ref.shape[0]):
        rows = jnp.dot(amp_ref[ij], pick_d, preferred_element_type=jnp.float32)
        direct_ref[ij:ij + 1, :] = jnp.sum(jnp.where(pick_c, rows, 0.0), axis=0, keepdims=True)

    own.wait()
    for k in range(1, n_cd):
        src = lax.rem(me_cd + n_cd - k, n_cd)

        @pl.when(src > me_cd)
        def _():
            pltpu.make_async_remote_copy(
                src_ref=chunks_ref.at[src],
                dst_ref=landed.at[src],
                send_sem=send_sem.at[k],
                recv_sem=recv_sem.at[src],
                device_id=(me_ab, src),
                device_id_type=MESH,
            ).wait_recv()

    for k in range(1, n_cd):
        peer = lax.rem(me_cd + k, n_cd)

        @pl.when(peer < me_cd)
        def _():
            pltpu.make_async_remote_copy(
                src_ref=chunks_ref.at[me_cd],
                dst_ref=landed.at[me_cd],
                send_sem=send_sem.at[k],
                recv_sem=recv_sem.at[me_cd],
                device_id=(me_ab, me_cd),
                device_id_type=MESH,
            ).wait_send()


def exchange(chunks, amplitudes, second, first, n_cd):
    pair_block, columns = amplitudes.shape[0], second.shape[0]
    return pl.pallas_call(
        functools.partial(exchange_kernel, n_cd),
        out_shape=(
            jax.ShapeDtypeStruct(chunks.shape, chunks.dtype),
            jax.ShapeDtypeStruct((pair_block, columns), jnp.float32),
        ),
        in_specs=[pl.BlockSpec(memory_space=pltpu.VMEM)] * 4,
        out_specs=(pl.BlockSpec(memory_space=pltpu.VMEM), pl.BlockSpec(memory_space=pltpu.VMEM)),
        scratch_shapes=[
            pltpu.SemaphoreType.DMA((n_cd,)),
            pltpu.SemaphoreType.DMA((n_cd,)),
            pltpu.SemaphoreType.DMA((1,)),
        ],
        compiler_params=pltpu.CompilerParams(collective_id=1, has_side_effects=True),
    )(chunks, amplitudes, second.reshape(1, columns), first.reshape(1, columns))


def ladder_kernel(
    n_ab, n_x, n_z, packed_ref, values_hbm, out_ref,
    slots, gathered, values_buf, first_out, first_in, second_out, second_in,
    values_sem, pk_send, pk_recv, first_send, first_recv, second_send, second_recv, own_sem,
):
    me_ab = lax.axis_index("ab")
    me_cd = lax.axis_index("cd")
    me_z = me_cd // n_x
    me_x = lax.rem(me_cd, n_x)
    rows = packed_ref.shape[0]
    block = values_buf.shape[1]

    z_order = [lax.rem(me_z + j, n_z) for j in list(range(1, n_z)) + [0]]
    order = []
    for z in z_order:
        for k in list(range(1, n_x)) + [0]:
            order.append(z * n_x + lax.rem(me_x + k, n_x))
    barrier = pltpu.get_barrier_semaphore()
    for k in range(1, n_ab):
        peer = lax.rem(me_ab + k, n_ab)
        pl.semaphore_signal(barrier, inc=1, device_id=(peer, me_cd), device_id_type=MESH)
    for k in range(1, n_x):
        peer = me_z * n_x + lax.rem(me_x + k, n_x)
        pl.semaphore_signal(barrier, inc=1, device_id=(me_ab, peer), device_id_type=MESH)
    for j in range(1, n_z):
        peer = lax.rem(me_z + j, n_z) * n_x + me_x
        pl.semaphore_signal(barrier, inc=1, device_id=(me_ab, peer), device_id_type=MESH)
    pl.semaphore_wait(barrier, (n_ab - 1) + (n_x - 1) + (n_z - 1))

    own = pltpu.make_async_copy(packed_ref, slots.at[me_ab], own_sem.at[0])
    own.start()
    for k in range(1, n_ab):
        peer = lax.rem(me_ab + k, n_ab)
        pltpu.make_async_remote_copy(
            src_ref=packed_ref,
            dst_ref=slots.at[me_ab],
            send_sem=pk_send.at[k],
            recv_sem=pk_recv.at[me_ab],
            device_id=(peer, me_cd),
            device_id_type=MESH,
        ).start()
    for step, owner in enumerate(order):
        pltpu.make_async_copy(
            values_hbm.at[pl.ds(pl.multiple_of(owner * block, block), block), :],
            values_buf.at[step],
            values_sem.at[step],
        ).start()
    own.wait()
    for k in range(1, n_ab):
        src = lax.rem(me_ab + n_ab - k, n_ab)
        pltpu.make_async_remote_copy(
            src_ref=packed_ref,
            dst_ref=slots.at[src],
            send_sem=pk_send.at[k],
            recv_sem=pk_recv.at[src],
            device_id=(src, me_cd),
            device_id_type=MESH,
        ).wait_recv()
    for k in range(n_ab):
        gathered[k * rows:(k + 1) * rows, :] = slots[k].astype(jnp.float32)
    lhs = gathered[...].astype(jnp.bfloat16)

    def one_block(step):
        pltpu.make_async_copy(
            values_hbm.at[pl.ds(0, block), :], values_buf.at[step], values_sem.at[step]
        ).wait()
        return lax.dot_general(
            lhs, values_buf[step], (((1,), (1,)), ((), ())), preferred_element_type=jnp.float32
        )

    def first_copy(j, k, peer):
        slot = j * (n_x - 1) + (k - 1)
        return pltpu.make_async_remote_copy(
            src_ref=first_out.at[slot],
            dst_ref=first_in.at[slot],
            send_sem=first_send.at[slot],
            recv_sem=first_recv.at[slot],
            device_id=(me_ab, peer),
            device_id_type=MESH,
        )

    def second_copy(j, peer):
        return pltpu.make_async_remote_copy(
            src_ref=second_out.at[j],
            dst_ref=second_in.at[j],
            send_sem=second_send.at[j],
            recv_sem=second_recv.at[j],
            device_id=(me_ab, peer),
            device_id_type=MESH,
        )

    own = []
    for j in range(n_z):
        for k in range(1, n_x):
            first_out[j * (n_x - 1) + (k - 1)] = one_block(j * n_x + (k - 1))
            first_copy(j, k, me_z * n_x + lax.rem(me_x + k, n_x)).start()
        own.append(one_block(j * n_x + (n_x - 1)))

    total = None
    for j in range(n_z):
        summed = own[j]
        for k in range(1, n_x):
            first_copy(j, k, me_z * n_x + lax.rem(me_x + n_x - k, n_x)).wait_recv()
            summed = summed + first_in[j * (n_x - 1) + (k - 1)]
        if j < n_z - 1:
            second_out[j] = summed
            second_copy(j, z_order[j] * n_x + me_x).start()
        else:
            total = summed
    for j in range(n_z - 1):
        second_copy(j, lax.rem(me_z + n_z - 1 - j, n_z) * n_x + me_x).wait_recv()
        total = total + second_in[j]
    out_ref[...] = total.astype(out_ref.dtype)

    for k in range(1, n_ab):
        pltpu.make_async_remote_copy(
            src_ref=packed_ref,
            dst_ref=slots.at[me_ab],
            send_sem=pk_send.at[k],
            recv_sem=pk_recv.at[me_ab],
            device_id=(me_ab, me_cd),
            device_id_type=MESH,
        ).wait_send()
    for j in range(n_z):
        for k in range(1, n_x):
            first_copy(j, k, me_cd).wait_send()
    for j in range(n_z - 1):
        second_copy(j, me_cd).wait_send()


def ladder(packed, pair_values, n_ab, n_cd):
    rows, columns = packed.shape
    ab_dev = pair_values.shape[0]
    block = ab_dev // n_cd
    n_x = X_CHIPS
    n_z = n_cd // n_x
    width = rows * n_ab
    return pl.pallas_call(
        functools.partial(ladder_kernel, n_ab, n_x, n_z),
        out_shape=jax.ShapeDtypeStruct((width, block), jnp.bfloat16),
        in_specs=[pl.BlockSpec(memory_space=pltpu.VMEM), pl.BlockSpec(memory_space=pl.ANY)],
        out_specs=pl.BlockSpec(memory_space=pltpu.VMEM),
        scratch_shapes=[
            pltpu.VMEM((n_ab, rows, columns), packed.dtype),
            pltpu.VMEM((width, columns), jnp.float32),
            pltpu.VMEM((n_cd, block, columns), pair_values.dtype),
            pltpu.VMEM((n_z * (n_x - 1), width, block), jnp.float32),
            pltpu.VMEM((n_z * (n_x - 1), width, block), jnp.float32),
            pltpu.VMEM((n_z - 1, width, block), jnp.float32),
            pltpu.VMEM((n_z - 1, width, block), jnp.float32),
            pltpu.SemaphoreType.DMA((n_cd,)),
            pltpu.SemaphoreType.DMA((n_ab,)),
            pltpu.SemaphoreType.DMA((n_ab,)),
            pltpu.SemaphoreType.DMA((n_z * (n_x - 1),)),
            pltpu.SemaphoreType.DMA((n_z * (n_x - 1),)),
            pltpu.SemaphoreType.DMA((n_z - 1,)),
            pltpu.SemaphoreType.DMA((n_z - 1,)),
            pltpu.SemaphoreType.DMA((1,)),
        ],
        compiler_params=pltpu.CompilerParams(
            collective_id=0, has_side_effects=True, vmem_limit_bytes=48 * 1024 * 1024
        ),
    )(packed, pair_values)


def on_device(n_ab, n_cd, pair_values, amplitudes, cd_first, cd_second, live_cols):
    slab = lax.axis_index("cd")
    orbit_block = amplitudes.shape[1]
    orbitals = amplitudes.shape[2]
    columns = cd_first.shape[0]
    local_first = cd_first - slab * orbit_block
    pair_block = amplitudes.shape[0]
    piece = pair_block * orbit_block * orbit_block
    padded = -(-piece // 1024) * 1024
    rows_first = jnp.transpose(amplitudes, (1, 0, 2)).reshape(orbit_block, pair_block, n_cd, orbit_block)
    chunks = jnp.transpose(rows_first, (2, 0, 1, 3)).reshape(n_cd, piece)
    chunks = jnp.pad(chunks, ((0, 0), (0, padded - piece)))
    landed, direct = exchange(chunks.reshape(n_cd, padded // 128, 128), amplitudes, cd_second, cd_first, n_cd)
    mirrored = landed.reshape(n_cd, padded)[:, :piece].reshape(n_cd, orbit_block, pair_block, orbit_block)
    pick_d = (lax.broadcasted_iota(jnp.int32, (orbitals, columns), 0) == cd_second[None, :]).astype(
        amplitudes.dtype
    )
    crossed_rows = lax.dot_general(
        mirrored,
        pick_d.reshape(n_cd, orbit_block, columns),
        (((0, 1), (0, 1)), ((), ())),
        preferred_element_type=jnp.float32,
    )
    pick_c = lax.broadcasted_iota(jnp.int32, (orbit_block, columns), 0) == local_first[None, :]
    both = direct + jnp.sum(jnp.where(pick_c[None], crossed_rows, 0.0), axis=1)
    live_count = live_cols[0]
    slots = jnp.arange(columns, dtype=jnp.int32)
    live = (slots < live_count).astype(jnp.float32)
    half = jnp.where(cd_first == cd_second, jnp.float32(0.5), jnp.float32(1.0))
    weight = half * live
    packed = (both * weight[None, :]).astype(jnp.bfloat16)
    return ladder(packed, pair_values, n_ab, n_cd)


def solution(mesh):
    placed = (P("ab", "cd"), P("ab", "cd", None), P("cd"), P("cd"), P("cd"))
    return jax.shard_map(
        functools.partial(on_device, mesh.shape["ab"], mesh.shape["cd"]),
        mesh=mesh, in_specs=placed, out_specs=P(None, ("ab", "cd")), check_vma=False,
    )
```

```python
import functools

import jax
import jax.numpy as jnp
from jax import lax
from jax.experimental import pallas as pl
from jax.experimental.pallas import tpu as pltpu
from jax.sharding import PartitionSpec as P

MESH = pl.DeviceIdType.MESH
X_CHIPS = 4


def exchange_kernel(
    n_cd, chunks_ref, amp_ref, second_ref, first_ref, landed, direct_ref, send_sem, recv_sem, own_sem
):
    me_ab = lax.axis_index("ab")
    me_cd = lax.axis_index("cd")
    barrier = pltpu.get_barrier_semaphore()
    for k in range(1, n_cd):
        peer = lax.rem(me_cd + k, n_cd)
        pl.semaphore_signal(barrier, inc=1, device_id=(me_ab, peer), device_id_type=MESH)
    pl.semaphore_wait(barrier, n_cd - 1)
    own = pltpu.make_async_copy(chunks_ref.at[me_cd], landed.at[me_cd], own_sem.at[0])
    own.start()
    for k in range(1, n_cd):
        peer = lax.rem(me_cd + k, n_cd)

        @pl.when(peer < me_cd)
        def _():
            pltpu.make_async_remote_copy(
                src_ref=chunks_ref.at[peer],
                dst_ref=landed.at[me_cd],
                send_sem=send_sem.at[k],
                recv_sem=recv_sem.at[me_cd],
                device_id=(me_ab, peer),
                device_id_type=MESH,
            ).start()

    for k in range(1, n_cd):
        src = lax.rem(me_cd + k, n_cd)

        @pl.when(src < me_cd)
        def _():
            landed[src] = jnp.zeros(landed.shape[1:], landed.dtype)

    orbitals, columns = amp_ref.shape[2], second_ref.shape[1]
    pick_d = (lax.broadcasted_iota(jnp.int32, (orbitals, columns), 0) == second_ref[...]).astype(amp_ref.dtype)
    local = first_ref[...] - me_cd * amp_ref.shape[1]
    pick_c = lax.broadcasted_iota(jnp.int32, (amp_ref.shape[1], columns), 0) == local
    for ij in range(amp_ref.shape[0]):
        rows = jnp.dot(amp_ref[ij], pick_d, preferred_element_type=jnp.float32)
        direct_ref[ij:ij + 1, :] = jnp.sum(jnp.where(pick_c, rows, 0.0), axis=0, keepdims=True)

    own.wait()
    for k in range(1, n_cd):
        src = lax.rem(me_cd + n_cd - k, n_cd)

        @pl.when(src > me_cd)
        def _():
            pltpu.make_async_remote_copy(
                src_ref=chunks_ref.at[src],
                dst_ref=landed.at[src],
                send_sem=send_sem.at[k],
                recv_sem=recv_sem.at[src],
                device_id=(me_ab, src),
                device_id_type=MESH,
            ).wait_recv()

    for k in range(1, n_cd):
        peer = lax.rem(me_cd + k, n_cd)

        @pl.when(peer < me_cd)
        def _():
            pltpu.make_async_remote_copy(
                src_ref=chunks_ref.at[me_cd],
                dst_ref=landed.at[me_cd],
                send_sem=send_sem.at[k],
                recv_sem=recv_sem.at[me_cd],
                device_id=(me_ab, me_cd),
                device_id_type=MESH,
            ).wait_send()


def exchange(chunks, amplitudes, second, first, n_cd):
    pair_block, columns = amplitudes.shape[0], second.shape[0]
    return pl.pallas_call(
        functools.partial(exchange_kernel, n_cd),
        out_shape=(
            jax.ShapeDtypeStruct(chunks.shape, chunks.dtype),
            jax.ShapeDtypeStruct((pair_block, columns), jnp.float32),
        ),
        in_specs=[pl.BlockSpec(memory_space=pltpu.VMEM)] * 4,
        out_specs=(pl.BlockSpec(memory_space=pltpu.VMEM), pl.BlockSpec(memory_space=pltpu.VMEM)),
        scratch_shapes=[
            pltpu.SemaphoreType.DMA((n_cd,)),
            pltpu.SemaphoreType.DMA((n_cd,)),
            pltpu.SemaphoreType.DMA((1,)),
        ],
        compiler_params=pltpu.CompilerParams(collective_id=1, has_side_effects=True),
    )(chunks, amplitudes, second.reshape(1, columns), first.reshape(1, columns))


def ladder_kernel(
    n_ab, n_x, n_z, packed_ref, values_hbm, out_ref,
    slots, gathered, values_buf, first_out, first_in, second_out, second_in,
    values_sem, pk_send, pk_recv, first_send, first_recv, second_send, second_recv, own_sem,
):
    me_ab = lax.axis_index("ab")
    me_cd = lax.axis_index("cd")
    me_z = me_cd // n_x
    me_x = lax.rem(me_cd, n_x)
    rows = packed_ref.shape[0]
    block = values_buf.shape[1]

    z_order = [lax.rem(me_z + j, n_z) for j in list(range(1, n_z)) + [0]]
    order = []
    for z in z_order:
        for k in list(range(1, n_x)) + [0]:
            order.append(z * n_x + lax.rem(me_x + k, n_x))
    barrier = pltpu.get_barrier_semaphore()
    for k in range(1, n_ab):
        peer = lax.rem(me_ab + k, n_ab)
        pl.semaphore_signal(barrier, inc=1, device_id=(peer, me_cd), device_id_type=MESH)
    for k in range(1, n_x):
        peer = me_z * n_x + lax.rem(me_x + k, n_x)
        pl.semaphore_signal(barrier, inc=1, device_id=(me_ab, peer), device_id_type=MESH)
    for j in range(1, n_z):
        peer = lax.rem(me_z + j, n_z) * n_x + me_x
        pl.semaphore_signal(barrier, inc=1, device_id=(me_ab, peer), device_id_type=MESH)
    pl.semaphore_wait(barrier, (n_ab - 1) + (n_x - 1) + (n_z - 1))

    own = pltpu.make_async_copy(packed_ref, slots.at[me_ab], own_sem.at[0])
    for k in range(1, n_ab):
        peer = lax.rem(me_ab + k, n_ab)
        pltpu.make_async_remote_copy(
            src_ref=packed_ref,
            dst_ref=slots.at[me_ab],
            send_sem=pk_send.at[k],
            recv_sem=pk_recv.at[me_ab],
            device_id=(peer, me_cd),
            device_id_type=MESH,
        ).start()
    own.start()
    for step, owner in enumerate(order):
        pltpu.make_async_copy(
            values_hbm.at[pl.ds(pl.multiple_of(owner * block, block), block), :],
            values_buf.at[step],
            values_sem.at[step],
        ).start()
    own.wait()
    for k in range(1, n_ab):
        src = lax.rem(me_ab + n_ab - k, n_ab)
        pltpu.make_async_remote_copy(
            src_ref=packed_ref,
            dst_ref=slots.at[src],
            send_sem=pk_send.at[k],
            recv_sem=pk_recv.at[src],
            device_id=(src, me_cd),
            device_id_type=MESH,
        ).wait_recv()
    for k in range(n_ab):
        gathered[k * rows:(k + 1) * rows, :] = slots[k].astype(jnp.float32)
    lhs = gathered[...].astype(jnp.bfloat16)

    def one_block(step):
        pltpu.make_async_copy(
            values_hbm.at[pl.ds(0, block), :], values_buf.at[step], values_sem.at[step]
        ).wait()
        return lax.dot_general(
            lhs, values_buf[step], (((1,), (1,)), ((), ())), preferred_element_type=jnp.float32
        )

    def first_copy(j, k, peer):
        slot = j * (n_x - 1) + (k - 1)
        return pltpu.make_async_remote_copy(
            src_ref=first_out.at[slot],
            dst_ref=first_in.at[slot],
            send_sem=first_send.at[slot],
            recv_sem=first_recv.at[slot],
            device_id=(me_ab, peer),
            device_id_type=MESH,
        )

    def second_copy(j, peer):
        return pltpu.make_async_remote_copy(
            src_ref=second_out.at[j],
            dst_ref=second_in.at[j],
            send_sem=second_send.at[j],
            recv_sem=second_recv.at[j],
            device_id=(me_ab, peer),
            device_id_type=MESH,
        )

    own = []
    for j in range(n_z):
        for k in range(1, n_x):
            first_out[j * (n_x - 1) + (k - 1)] = one_block(j * n_x + (k - 1))
            first_copy(j, k, me_z * n_x + lax.rem(me_x + k, n_x)).start()
        own.append(one_block(j * n_x + (n_x - 1)))

    total = None
    for j in range(n_z):
        summed = own[j]
        for k in range(1, n_x):
            first_copy(j, k, me_z * n_x + lax.rem(me_x + n_x - k, n_x)).wait_recv()
            summed = summed + first_in[j * (n_x - 1) + (k - 1)]
        if j < n_z - 1:
            second_out[j] = summed
            second_copy(j, z_order[j] * n_x + me_x).start()
        else:
            total = summed
    for j in range(n_z - 1):
        second_copy(j, lax.rem(me_z + n_z - 1 - j, n_z) * n_x + me_x).wait_recv()
        total = total + second_in[j]
    out_ref[...] = total.astype(out_ref.dtype)

    for k in range(1, n_ab):
        pltpu.make_async_remote_copy(
            src_ref=packed_ref,
            dst_ref=slots.at[me_ab],
            send_sem=pk_send.at[k],
            recv_sem=pk_recv.at[me_ab],
            device_id=(me_ab, me_cd),
            device_id_type=MESH,
        ).wait_send()
    for j in range(n_z):
        for k in range(1, n_x):
            first_copy(j, k, me_cd).wait_send()
    for j in range(n_z - 1):
        second_copy(j, me_cd).wait_send()


def ladder(packed, pair_values, n_ab, n_cd):
    rows, columns = packed.shape
    ab_dev = pair_values.shape[0]
    block = ab_dev // n_cd
    n_x = X_CHIPS
    n_z = n_cd // n_x
    width = rows * n_ab
    return pl.pallas_call(
        functools.partial(ladder_kernel, n_ab, n_x, n_z),
        out_shape=jax.ShapeDtypeStruct((width, block), jnp.bfloat16),
        in_specs=[pl.BlockSpec(memory_space=pltpu.VMEM), pl.BlockSpec(memory_space=pl.ANY)],
        out_specs=pl.BlockSpec(memory_space=pltpu.VMEM),
        scratch_shapes=[
            pltpu.VMEM((n_ab, rows, columns), packed.dtype),
            pltpu.VMEM((width, columns), jnp.float32),
            pltpu.VMEM((n_cd, block, columns), pair_values.dtype),
            pltpu.VMEM((n_z * (n_x - 1), width, block), jnp.float32),
            pltpu.VMEM((n_z * (n_x - 1), width, block), jnp.float32),
            pltpu.VMEM((n_z - 1, width, block), jnp.float32),
            pltpu.VMEM((n_z - 1, width, block), jnp.float32),
            pltpu.SemaphoreType.DMA((n_cd,)),
            pltpu.SemaphoreType.DMA((n_ab,)),
            pltpu.SemaphoreType.DMA((n_ab,)),
            pltpu.SemaphoreType.DMA((n_z * (n_x - 1),)),
            pltpu.SemaphoreType.DMA((n_z * (n_x - 1),)),
            pltpu.SemaphoreType.DMA((n_z - 1,)),
            pltpu.SemaphoreType.DMA((n_z - 1,)),
            pltpu.SemaphoreType.DMA((1,)),
        ],
        compiler_params=pltpu.CompilerParams(
            collective_id=0, has_side_effects=True, vmem_limit_bytes=48 * 1024 * 1024
        ),
    )(packed, pair_values)


def on_device(n_ab, n_cd, pair_values, amplitudes, cd_first, cd_second, live_cols):
    slab = lax.axis_index("cd")
    orbit_block = amplitudes.shape[1]
    orbitals = amplitudes.shape[2]
    columns = cd_first.shape[0]
    local_first = cd_first - slab * orbit_block
    pair_block = amplitudes.shape[0]
    piece = pair_block * orbit_block * orbit_block
    padded = -(-piece // 1024) * 1024
    rows_first = jnp.transpose(amplitudes, (1, 0, 2)).reshape(orbit_block, pair_block, n_cd, orbit_block)
    chunks = jnp.transpose(rows_first, (2, 0, 1, 3)).reshape(n_cd, piece)
    chunks = jnp.pad(chunks, ((0, 0), (0, padded - piece)))
    landed, direct = exchange(chunks.reshape(n_cd, padded // 128, 128), amplitudes, cd_second, cd_first, n_cd)
    mirrored = landed.reshape(n_cd, padded)[:, :piece].reshape(n_cd, orbit_block, pair_block, orbit_block)
    pick_d = (lax.broadcasted_iota(jnp.int32, (orbitals, columns), 0) == cd_second[None, :]).astype(
        amplitudes.dtype
    )
    crossed_rows = lax.dot_general(
        mirrored,
        pick_d.reshape(n_cd, orbit_block, columns),
        (((0, 1), (0, 1)), ((), ())),
        preferred_element_type=jnp.float32,
    )
    pick_c = lax.broadcasted_iota(jnp.int32, (orbit_block, columns), 0) == local_first[None, :]
    both = direct + jnp.sum(jnp.where(pick_c[None], crossed_rows, 0.0), axis=1)
    live_count = live_cols[0]
    slots = jnp.arange(columns, dtype=jnp.int32)
    live = (slots < live_count).astype(jnp.float32)
    half = jnp.where(cd_first == cd_second, jnp.float32(0.5), jnp.float32(1.0))
    weight = half * live
    packed = (both * weight[None, :]).astype(jnp.bfloat16)
    return ladder(packed, pair_values, n_ab, n_cd)


def solution(mesh):
    placed = (P("ab", "cd"), P("ab", "cd", None), P("cd"), P("cd"), P("cd"))
    return jax.shard_map(
        functools.partial(on_device, mesh.shape["ab"], mesh.shape["cd"]),
        mesh=mesh, in_specs=placed, out_specs=P(None, ("ab", "cd")), check_vma=False,
    )
```
